512 devices in a mesh: feat: 8 (over y), row: 64 (over x, z, core).
Axes of the slice: x: 4, y: 8, z: 8, core: 2. Of those that a mesh axis runs over, the one named last changes fastest.
Arguments:
- bin_values: int32 [131072, 1024], P('row', 'feat'), may hold values from 0 to 127
- leaf_ids: int32 [131072], P('row'), may hold values from 0 to 3
- treated: int32 [131072], P('row'), may hold values 0 or 1
- gradient: bfloat16 [131072], P('row'), may hold values from -6 to 6
- hessian: bfloat16 [131072], P('row'), may hold values from 0.099609375 to 2
Outputs:
- split_gain: float32 [4, 1024, 128], P(None, ('feat', 'row'))
- best_gain: float32 [4], replicated
The draws below stay inside these ranges and needn't reach their ends.
All inputs are finite; a program needn't handle non-finite values. No bound on the sum of `treated` on one device may be relied on, other than what follows from the above.
Results may differ from the reference program's by a relative error of at most 0.0003.
Values sent between devices are 32-bit elements; how exact they have to be, the bound alone decides.
A program may use at most 64 MiB of HBM per device.

```python
import math
import jax
import jax.numpy as jnp
import numpy as np
from jax import lax

BINS = 128
LEAVES = 4
F = 1024
ROWS = 131072


def plant(result, rng, smallest, largest):
    longest = result.shape.index(max(result.shape))
    spots = []
    for shift in (0, 1):
        where = [jax.random.randint(jax.random.fold_in(rng, axis), (), 0, length) for axis, length in enumerate(result.shape)]
        where[longest] = (where[longest] + shift) % result.shape[longest]
        spots.append(tuple(where))
    return result.at[spots[0]].set(smallest).at[spots[1]].set(largest)


def level_of(rng, shape, pieces, smallest, largest):
    level, own = 1.0, jax.random.fold_in(rng, 6)
    for position, shards_of in pieces:
        steps = jnp.exp(jax.random.uniform(jax.random.fold_in(own, position), (shards_of,), jnp.float32, smallest / len(pieces), largest / len(pieces)))
        level = level * jnp.repeat(steps, shape[position] // shards_of).reshape([-1 if axis == position else 1 for axis in range(len(shape))])
    return level


def rank_bounds(number_of, slope):
    weights = [(1 << 20) // math.isqrt(rank ** slope) + 1 for rank in range(1, number_of + 1)]
    scale = 1 + sum(weights) // (1 << 30)
    return np.cumsum(np.array([max(1, weight // scale) for weight in weights]))


def skewed_ids(rng, shape, count, slope):
    table = rank_bounds(count, slope)
    ticket = jax.random.randint(jax.random.fold_in(rng, 1), shape, 0, int(table[count - 1]))
    rank = jnp.searchsorted(jnp.asarray(table, jnp.int32), ticket, side="right")
    return jax.random.permutation(jax.random.fold_in(rng, 2), count)[rank].astype(jnp.int32)


def scatter_about(rng, shape, deviation, most, pieces=(), held_as=jnp.bfloat16):
    array = deviation * jax.random.normal(rng, shape, jnp.float32)
    if pieces:
        array = array * level_of(rng, shape, pieces, -0.22, 0.18)
    return jnp.clip(array, -most, most).astype(held_as)


def setup_inputs(seed: int = 0) -> dict:
    arg_keys = jax.random.split(jax.random.key(seed), 6)
    return {
        "bin_values": plant(jax.random.randint(arg_keys[0], (ROWS, F), 0, BINS), jax.random.fold_in(arg_keys[0], 1), 0, BINS - 1).astype(jnp.int32),
        "leaf_ids": plant(skewed_ids(arg_keys[1], (ROWS,), LEAVES, 2), jax.random.fold_in(arg_keys[1], 3), 0, LEAVES - 1).astype(jnp.int32),
        "treated": plant((jax.random.randint(arg_keys[2], (ROWS,), 0, 2) < 1).astype(jnp.int32), jax.random.fold_in(arg_keys[2], 1), 0, 1),
        "gradient": scatter_about(arg_keys[3], (ROWS,), 1.0, 6.0, ((0, 64),)),
        "hessian": jnp.clip(jnp.exp(math.log(2.0) - 2.9996462 * jax.random.uniform(arg_keys[4], (ROWS,), jnp.float32) ** level_of(arg_keys[4], (ROWS,), ((0, 64),), -0.2, 0.2)), 0.099609375, 2.0).astype(jnp.bfloat16),
    }


def node_score(totals):
    grad_t = totals[0]
    hess_t = totals[1]
    grad_c = totals[2]
    hess_c = totals[3]
    value_t = grad_t / (hess_t + 1.0)
    value_c = grad_c / (hess_c + 1.0)
    spread = value_t - value_c
    return grad_t * value_t + grad_c * value_c + (hess_t + hess_c) * spread * spread


def reference(bin_values, leaf_ids, treated, gradient, hessian):
    chosen = treated.astype(jnp.float32)
    others = 1.0 - chosen
    grad_full = gradient.astype(jnp.float32)
    hess_full = hessian.astype(jnp.float32)
    columns = jnp.stack([grad_full * chosen, hess_full * chosen, grad_full * others, hess_full * others], axis=1)
    block_width = math.gcd(F, 64)
    blocks = jnp.moveaxis(bin_values.reshape(ROWS, F // block_width, block_width), 1, 0)
    offsets = jnp.arange(block_width, dtype=jnp.int32)[None, :] * (LEAVES * BINS) + leaf_ids[:, None] * BINS
    payload = jnp.broadcast_to(columns[:, None, :], (ROWS, block_width, 4)).reshape(ROWS * block_width, 4)

    def block_hist(feat_block):
        segment_ids = (offsets + feat_block).reshape(-1).astype(jnp.int32)
        return jax.ops.segment_sum(payload, segment_ids, num_segments=block_width * LEAVES * BINS)

    histogram = lax.map(block_hist, blocks).reshape(F, LEAVES, BINS, 4)
    histogram = jnp.transpose(histogram, (3, 1, 0, 2))
    bin_range = jnp.arange(BINS, dtype=jnp.int32)
    ladder = (bin_range[:, None] <= bin_range[None, :]).astype(jnp.float32)
    left_sums = jnp.einsum("slfb,bk->slfk", histogram, ladder, precision=lax.Precision.HIGHEST)
    parent_sums = left_sums[:, :, :, BINS - 1:]
    right_sums = parent_sums - left_sums
    split_gain = node_score(left_sums) + node_score(right_sums) - node_score(parent_sums)
    best_gain = jnp.max(split_gain, axis=(1, 2))
    return split_gain, best_gain
```

```python
import jax
import jax.numpy as jnp
from jax import lax
from jax.experimental import pallas as pl
from jax.experimental.pallas import tpu as pltpu
from jax.sharding import PartitionSpec as P

MESH = pl.DeviceIdType.MESH
BF = jnp.bfloat16
NT = (((1,), (1,)), ((), ()))
ROWS = 2048
FEATS = 128
CHUNKS = ROWS // 128
GROUP = 4
NX, NZ, NY = 4, 8, 8


def prepare(bins_ref, leaf_ref, arm_ref, grad_ref, hess_ref, stat_scr, high_scr, low_scr):
    stat = lax.broadcasted_iota(jnp.int32, (16, 128), 0)
    kind, leaf_of = stat // 4, stat % 4
    for c in range(CHUNKS):
        cols = slice(c * 128, (c + 1) * 128)
        grad = grad_ref[c : c + 1, :].astype(jnp.float32)
        hess = hess_ref[c : c + 1, :].astype(jnp.float32)
        keep = (leaf_ref[c : c + 1, :] == leaf_of) & ((arm_ref[c : c + 1, :] == 1) == (kind < 2))
        value = jnp.where(kind % 2 == 0, grad, hess)
        stat_scr[:, cols] = jnp.where(keep, value, 0.0).astype(BF)
    row = lax.broadcasted_iota(jnp.int32, (FEATS, FEATS), 0)
    col = lax.broadcasted_iota(jnp.int32, (FEATS, FEATS), 1)
    eye = (row == col).astype(jnp.float32).astype(BF)
    for c in range(ROWS // 256):
        cols = slice(c * 256, (c + 1) * 256)
        block = bins_ref[cols, :].astype(jnp.float32).astype(BF)
        flipped = lax.dot_general(eye, block, NT, preferred_element_type=jnp.float32)
        high = (flipped >= 64.0).astype(jnp.float32)
        high_scr[:, :, cols] = high.reshape(16, 8, 256)
        low_scr[:, :, cols] = (flipped - high * 64.0).reshape(16, 8, 256)


def hist_kernel(bins_ref, leaf_ref, arm_ref, grad_ref, hess_ref, out_ref, stat_scr, high_scr, low_scr, w_scr, l_scr, a_scr):
    prepare(bins_ref, leaf_ref, arm_ref, grad_ref, hess_ref, stat_scr, high_scr, low_scr)
    sub = lax.broadcasted_iota(jnp.int32, (16, 128), 0)
    lows = [(sub + 16 * k).astype(jnp.float32).astype(BF) for k in range(4)]
    zero = jnp.zeros((16, 128), BF)
    one = jnp.ones((16, 128), BF)
    lane = lax.broadcasted_iota(jnp.int32, (64, 128), 1)
    half = lax.broadcasted_iota(jnp.int32, (32, 128), 1) < 64

    def generate(i, u, slot):
        for j in range(GROUP):
            f = u * GROUP + j
            for c in range(CHUNKS):
                cols = slice(c * 128, (c + 1) * 128)
                high = jnp.broadcast_to(high_scr[i, f : f + 1, cols], (16, 128)).astype(BF)
                low = jnp.broadcast_to(low_scr[i, f : f + 1, cols], (16, 128)).astype(BF)
                stat = stat_scr[:, cols]
                lower = high == zero
                w_scr[slot, 32 * j : 32 * j + 16, cols] = jnp.where(lower, stat, zero)
                w_scr[slot, 32 * j + 16 : 32 * j + 32, cols] = jnp.where(lower, zero, stat)
                for k in range(4):
                    at = 64 * j + 16 * k
                    l_scr[slot, at : at + 16, cols] = jnp.where(low == lows[k], one, zero)

    def multiply(slot):
        a_scr[slot] = lax.dot_general(l_scr[slot], w_scr[slot], NT, preferred_element_type=jnp.float32)

    def extract(g, slot):
        own = a_scr[slot, 0:64, :]
        for j in range(1, GROUP):
            own = jnp.where(lane // 32 == j, a_scr[slot, 64 * j : 64 * (j + 1), :], own)
        top, bottom = own[0:32], own[32:64]
        out_ref[0, g] = jnp.where(half, top, pltpu.roll(bottom, 64, 1))
        out_ref[1, g] = jnp.where(half, pltpu.roll(top, 64, 1), bottom)

    def step(i, carry):
        for u in range(2):
            generate(i, u, u)
            multiply(u)
            extract(2 * i + u, u)
        return carry

    lax.fori_loop(0, FEATS // 8, step, 0)


def finish(block, gain_ref):
    turned = block.T
    lane = lax.broadcasted_iota(jnp.int32, (16, 128), 1)
    best = None
    for j in range(2):
        pieces = [turned[64 * mid + 32 * j + 16 * top : 64 * mid + 32 * j + 16 * top + 16] for top in (0, 1) for mid in (0, 1)]
        left = jnp.concatenate(pieces, axis=1)
        for shift in (1, 2, 4, 8, 16, 32, 64):
            left = left + jnp.where(lane >= shift, pltpu.roll(left, shift, 1), 0.0)
        parent = jnp.broadcast_to(left[:, 127:128], (16, 128))
        gain = score(left) + score(parent - left) - score(parent)
        for leaf in range(4):
            gain_ref[leaf, j : j + 1, :] = gain[leaf : leaf + 1, :]
        best = gain if best is None else jnp.maximum(best, gain)
    top = jnp.max(best, axis=1, keepdims=True)
    return jnp.broadcast_to(jnp.concatenate([top, top], axis=0), (8, 128))


def score(totals):
    grad_t, hess_t, grad_c, hess_c = (totals[4 * k : 4 * k + 4] for k in range(4))
    value_t = grad_t / (hess_t + 1.0)
    value_c = grad_c / (hess_c + 1.0)
    spread = value_t - value_c
    return grad_t * value_t + grad_c * value_c + (hess_t + hess_c) * spread * spread


def exchange_kernel(
    hist_ref, gain_ref, best_ref, core_in, core_sum, x_in, x_sum, z_in, top_out, top_in,
    core_send, core_recv, x_send, x_recv, z_send, z_recv, top_send, top_recv,
):
    feat = lax.axis_index("feat")
    row = lax.axis_index("row")
    core = lax.rem(row, 2)
    z = lax.rem(row // 2, NZ)
    x = row // (2 * NZ)

    def at(x_, z_, core_):
        return (feat, (x_ * NZ + z_) * 2 + core_)

    other = at(x, z, 1 - core)
    x_peer = [at(lax.rem(x + d, NX), z, core) for d in range(NX)]
    x_other = [at(lax.rem(x + d, NX), z, 1 - core) for d in range(NX)]
    z_peer = [at(x, lax.rem(z + d, NZ), core) for d in range(NZ)]
    y_peer = [(lax.rem(feat + d, NY), row) for d in range(NY)]

    barrier = pltpu.get_barrier_semaphore()
    greeted = x_other + x_peer[1:] + z_peer[1:] + y_peer[1:]
    for peer in greeted:
        pl.semaphore_signal(barrier, inc=1, device_id=peer, device_id_type=MESH)
    pl.semaphore_wait(barrier, len(greeted))

    def copy(src, dst, send, recv, peer):
        return pltpu.make_async_remote_copy(
            src_ref=src, dst_ref=dst, send_sem=send, recv_sem=recv, device_id=peer, device_id_type=MESH
        )

    order = [1, 2, 3, 0]
    sent = []
    first = []
    for d in order:
        chips = pl.ds(lax.rem(x + d, NX) * NZ, NZ)
        c = copy(hist_ref.at[1 - core, chips], core_in.at[chips], core_send.at[d], core_recv.at[d], other)
        c.start()
        first.append(c)
    second = []
    for d, c in zip(order, first):
        chips = pl.ds(lax.rem(x + d, NX) * NZ, NZ)
        c.wait_recv()
        core_sum[chips] = hist_ref[core, chips] + core_in[chips]
        if d:
            s = copy(core_sum.at[chips], x_in.at[d - 1], x_send.at[d - 1], x_recv.at[d - 1], x_peer[d])
            s.start()
            second.append(s)
    total = core_sum[pl.ds(x * NZ, NZ)]
    for s in second:
        s.wait_recv()
    x_sum[...] = total + x_in[0] + x_in[1] + x_in[2]
    third = []
    for d in range(1, NZ):
        s = copy(x_sum.at[lax.rem(z + d, NZ)], z_in.at[d - 1], z_send.at[d - 1], z_recv.at[d - 1], z_peer[d])
        s.start()
        third.append(s)
    block = x_sum[z]
    for d, s in enumerate(third):
        s.wait_recv()
        block = block + z_in[d]

    top = finish(block, gain_ref)
    for stage, peers in enumerate((x_other + x_peer[1:], z_peer[1:], y_peer[1:])):
        top_out[stage] = top
        round_ = []
        for k, peer in enumerate(peers):
            s = copy(top_out.at[stage], top_in.at[stage, k], top_send.at[stage, k], top_recv.at[stage, k], peer)
            s.start()
            round_.append(s)
        for k, s in enumerate(round_):
            s.wait_recv()
            top = jnp.maximum(top, top_in[stage, k])
        sent += round_
    for leaf in range(4):
        best_ref[leaf] = jnp.max(top[leaf : leaf + 1, :])
    for s in first + second + third + sent:
        s.wait_send()


def body(bin_values, leaf_ids, treated, gradient, hessian):
    vmem = pl.BlockSpec(memory_space=pltpu.VMEM)
    f32 = jnp.float32
    shape = (CHUNKS, 128)
    hist = pl.pallas_call(
        hist_kernel,
        out_shape=jax.ShapeDtypeStruct((2, 32, 32, 128), f32),
        in_specs=[vmem] * 5,
        out_specs=vmem,
        scratch_shapes=[
            pltpu.VMEM((16, ROWS), BF),
            pltpu.VMEM((16, 8, ROWS), f32),
            pltpu.VMEM((16, 8, ROWS), f32),
            pltpu.VMEM((2, 128, ROWS), BF),
            pltpu.VMEM((2, 256, ROWS), BF),
            pltpu.VMEM((2, 256, 128), f32),
        ],
        compiler_params=pltpu.CompilerParams(vmem_limit_bytes=40 << 20),
    )(bin_values, leaf_ids.reshape(shape), treated.reshape(shape), gradient.reshape(shape), hessian.reshape(shape))
    dma = pltpu.SemaphoreType.DMA
    return pl.pallas_call(
        exchange_kernel,
        out_shape=(jax.ShapeDtypeStruct((4, 2, 128), f32), jax.ShapeDtypeStruct((4,), f32)),
        in_specs=[vmem],
        out_specs=(vmem, pl.BlockSpec(memory_space=pltpu.SMEM)),
        scratch_shapes=[
            pltpu.VMEM((32, 32, 128), f32),
            pltpu.VMEM((32, 32, 128), f32),
            pltpu.VMEM((NX - 1, NZ, 32, 128), f32),
            pltpu.VMEM((NZ, 32, 128), f32),
            pltpu.VMEM((NZ - 1, 32, 128), f32),
            pltpu.VMEM((3, 8, 128), f32),
            pltpu.VMEM((3, 7, 8, 128), f32),
            dma((4,)), dma((4,)), dma((3,)), dma((3,)), dma((7,)), dma((7,)), dma((3, 7)), dma((3, 7)),
        ],
        compiler_params=pltpu.CompilerParams(
            collective_id=0, has_side_effects=True, vmem_limit_bytes=20 << 20
        ),
    )(hist)


def solution(mesh):
    in_specs = (P("row", "feat"), P("row"), P("row"), P("row"), P("row"))
    out_specs = (P(None, ("feat", "row"), None), P())
    return jax.shard_map(body, mesh=mesh, in_specs=in_specs, out_specs=out_specs, check_vma=False)
```

```python
import jax
import jax.numpy as jnp
from jax import lax
from jax.experimental import pallas as pl
from jax.experimental.pallas import tpu as pltpu
from jax.sharding import PartitionSpec as P

MESH = pl.DeviceIdType.MESH
BF = jnp.bfloat16
NT = (((1,), (1,)), ((), ()))
ROWS = 2048
FEATS = 128
CHUNKS = ROWS // 128
GROUP = 4
NX, NZ, NY = 4, 8, 8
FAR = ((4, 3), (5, 2), (6, 1), (7, 0))


def prepare(bins_ref, leaf_ref, arm_ref, grad_ref, hess_ref, stat_scr, high_scr, low_scr):
    stat = lax.broadcasted_iota(jnp.int32, (16, 128), 0)
    kind, leaf_of = stat // 4, stat % 4
    for c in range(CHUNKS):
        cols = slice(c * 128, (c + 1) * 128)
        grad = grad_ref[c : c + 1, :].astype(jnp.float32)
        hess = hess_ref[c : c + 1, :].astype(jnp.float32)
        keep = (leaf_ref[c : c + 1, :] == leaf_of) & ((arm_ref[c : c + 1, :] == 1) == (kind < 2))
        value = jnp.where(kind % 2 == 0, grad, hess)
        stat_scr[:, cols] = jnp.where(keep, value, 0.0).astype(BF)
    row = lax.broadcasted_iota(jnp.int32, (2 * FEATS, FEATS), 0)
    col = lax.broadcasted_iota(jnp.int32, (2 * FEATS, FEATS), 1)
    pick = ((row // 8 * 4 + row % 8 == col) & (row % 8 < 4)).astype(jnp.float32).astype(BF)
    for c in range(ROWS // 256):
        cols = slice(c * 256, (c + 1) * 256)
        block = bins_ref[cols, :].astype(jnp.float32).astype(BF)
        flipped = lax.dot_general(pick, block, NT, preferred_element_type=jnp.float32)
        high = (flipped >= 64.0).astype(jnp.float32)
        high_scr[:, :, cols] = high.reshape(32, 8, 256)
        low_scr[:, :, cols] = (flipped - high * 64.0).reshape(32, 8, 256)


def make_histogram(hist, stat_scr, high_scr, low_scr, w_scr, l_scr, a_scr):
    sub = lax.broadcasted_iota(jnp.int32, (16, 128), 0)
    lows = [(sub + 16 * k).astype(jnp.float32).astype(BF) for k in range(4)]
    zero = jnp.zeros((16, 128), BF)
    one = jnp.ones((16, 128), BF)
    lane = lax.broadcasted_iota(jnp.int32, (64, 128), 1)
    half = lax.broadcasted_iota(jnp.int32, (32, 128), 1) < 64

    def generate(chip, slot):
        for j in range(GROUP):
            for c in range(CHUNKS):
                cols = slice(c * 128, (c + 1) * 128)
                high = jnp.broadcast_to(high_scr[chip, j : j + 1, cols], (16, 128)).astype(BF)
                low = jnp.broadcast_to(low_scr[chip, j : j + 1, cols], (16, 128)).astype(BF)
                stat = stat_scr[:, cols]
                lower = high == zero
                w_scr[slot, 32 * j : 32 * j + 16, cols] = jnp.where(lower, stat, zero)
                w_scr[slot, 32 * j + 16 : 32 * j + 32, cols] = jnp.where(lower, zero, stat)
                for k in range(4):
                    at = 64 * j + 16 * k
                    l_scr[slot, at : at + 16, cols] = jnp.where(low == lows[k], one, zero)

    def multiply(slot):
        a_scr[slot] = lax.dot_general(l_scr[slot], w_scr[slot], NT, preferred_element_type=jnp.float32)

    def extract(chunk, u, i, slot):
        own = a_scr[slot, 0:64, :]
        for j in range(1, GROUP):
            own = jnp.where(lane // 32 == j, a_scr[slot, 64 * j : 64 * (j + 1), :], own)
        top, bottom = own[0:32], own[32:64]
        hist[0, chunk, u, i] = jnp.where(half, top, pltpu.roll(bottom, 64, 1))
        hist[1, chunk, u, i] = jnp.where(half, pltpu.roll(top, 64, 1), bottom)

    def one_chunk(chunk, far):
        def step(i, carry):
            for u in range(2):
                generate(i * NZ + far[u], u)
                multiply(u)
                extract(chunk, u, i, u)
            return carry

        lax.fori_loop(0, NX, step, 0)

    return one_chunk


def finish(block, gain_ref):
    turned = block.T
    lane = lax.broadcasted_iota(jnp.int32, (16, 128), 1)
    best = None
    for j in range(2):
        pieces = [turned[64 * mid + 32 * j + 16 * top : 64 * mid + 32 * j + 16 * top + 16] for top in (0, 1) for mid in (0, 1)]
        left = jnp.concatenate(pieces, axis=1)
        for shift in (1, 2, 4, 8, 16, 32, 64):
            left = left + jnp.where(lane >= shift, pltpu.roll(left, shift, 1), 0.0)
        parent = jnp.broadcast_to(left[:, 127:128], (16, 128))
        gain = score(left) + score(parent - left) - score(parent)
        for leaf in range(4):
            gain_ref[leaf, j : j + 1, :] = gain[leaf : leaf + 1, :]
        best = gain if best is None else jnp.maximum(best, gain)
    top = jnp.max(best, axis=1, keepdims=True)
    return jnp.broadcast_to(jnp.concatenate([top, top], axis=0), (8, 128))


def score(totals):
    grad_t, hess_t, grad_c, hess_c = (totals[4 * k : 4 * k + 4] for k in range(4))
    value_t = grad_t / (hess_t + 1.0)
    value_c = grad_c / (hess_c + 1.0)
    spread = value_t - value_c
    return grad_t * value_t + grad_c * value_c + (hess_t + hess_c) * spread * spread


def kernel(
    bins_hbm, leaf_hbm, arm_hbm, grad_hbm, hess_hbm, gain_ref, best_ref,
    bins_ref, leaf_ref, arm_ref, grad_ref, hess_ref, stat_scr, high_scr, low_scr, w_scr, l_scr, a_scr,
    hist, core_in, core_sum, x_in, x_sum, z_in, top_out, top_in,
    load_sem, core_send, core_recv, x_send, x_recv, z_send, z_recv, top_send, top_recv,
):
    feat = lax.axis_index("feat")
    row = lax.axis_index("row")
    core = lax.rem(row, 2)
    z = lax.rem(row // 2, NZ)
    x = row // (2 * NZ)

    def at(x_, z_, core_):
        return (feat, (x_ * NZ + z_) * 2 + core_)

    other = at(x, z, 1 - core)
    x_peer = [at(lax.rem(x + d, NX), z, core) for d in range(NX)]
    z_peer = [at(x, lax.rem(z + d, NZ), core) for d in range(NZ)]
    y_peer = [(lax.rem(feat + d, NY), row) for d in range(NY)]

    loads = [
        pltpu.make_async_copy(src, dst, load_sem.at[k])
        for k, (src, dst) in enumerate(
            zip(
                (leaf_hbm, arm_hbm, grad_hbm, hess_hbm, bins_hbm),
                (leaf_ref, arm_ref, grad_ref, hess_ref, bins_ref),
            )
        )
    ]
    for load in loads:
        load.start()
    barrier = pltpu.get_barrier_semaphore()
    greeted = [other] + x_peer[1:] + z_peer[1:] + y_peer[1:]
    for peer in greeted:
        pl.semaphore_signal(barrier, inc=1, device_id=peer, device_id_type=MESH)
    for load in loads:
        load.wait()

    prepare(bins_ref, leaf_ref, arm_ref, grad_ref, hess_ref, stat_scr, high_scr, low_scr)
    one_chunk = make_histogram(hist, stat_scr, high_scr, low_scr, w_scr, l_scr, a_scr)

    def copy(src, dst, send, recv, peer):
        return pltpu.make_async_remote_copy(
            src_ref=src, dst_ref=dst, send_sem=send, recv_sem=recv, device_id=peer, device_id_type=MESH
        )

    core_copies, x_copies, z_copies, top_copies = [], {}, {}, []

    def start_core(c):
        s = copy(hist.at[1 - core, c], core_in.at[c], core_send.at[c], core_recv.at[c], other)
        s.start()
        core_copies.append(s)

    def start_x(c):
        core_copies[c].wait_recv()
        core_sum[c] = hist[core, c] + core_in[c]
        for d in (2, 1, 3):
            s = copy(
                core_sum.at[c, :, lax.rem(x + d, NX)], x_in.at[c, d - 1], x_send.at[c, d - 1], x_recv.at[c, d - 1], x_peer[d]
            )
            s.start()
            x_copies[c, d] = s

    def start_z(c):
        for d in (1, 3, 2):
            x_copies[c, d].wait_recv()
        x_sum[c] = core_sum[c, :, x] + x_in[c, 0] + x_in[c, 1] + x_in[c, 2]
        for u, d in enumerate(FAR[c]):
            if d:
                s = copy(x_sum.at[c, u], z_in.at[d - 1], z_send.at[d - 1], z_recv.at[d - 1], z_peer[d])
                s.start()
                z_copies[d] = s

    for c in range(4):
        one_chunk(c, [lax.rem(z + d, NZ) for d in FAR[c]])
        if c == 0:
            pl.semaphore_wait(barrier, len(greeted))
        start_core(c)
        if c >= 1:
            start_x(c - 1)
        if c >= 2:
            start_z(c - 2)
    start_x(3)
    start_z(2)
    start_z(3)
    block = x_sum[3, 1]
    for d in (1, 7, 2, 6, 3, 5, 4):
        z_copies[d].wait_recv()
        block = block + z_in[d - 1]

    top = finish(block, gain_ref)
    for stage, peers in enumerate(([other], x_peer[1:], z_peer[1:], y_peer[1:])):
        top_out[stage] = top
        round_ = []
        for k, peer in enumerate(peers):
            s = copy(top_out.at[stage], top_in.at[stage, k], top_send.at[stage, k], top_recv.at[stage, k], peer)
            s.start()
            round_.append(s)
        for k, s in enumerate(round_):
            s.wait_recv()
            top = jnp.maximum(top, top_in[stage, k])
        top_copies += round_
    for leaf in range(4):
        best_ref[leaf] = jnp.max(top[leaf : leaf + 1, :])
    for s in core_copies + list(x_copies.values()) + list(z_copies.values()) + top_copies:
        s.wait_send()


def body(bin_values, leaf_ids, treated, gradient, hessian):
    vmem = pl.BlockSpec(memory_space=pltpu.VMEM)
    f32 = jnp.float32
    shape = (CHUNKS, 128)
    dma = pltpu.SemaphoreType.DMA
    return pl.pallas_call(
        kernel,
        out_shape=(jax.ShapeDtypeStruct((4, 2, 128), f32), jax.ShapeDtypeStruct((4,), f32)),
        in_specs=[pl.BlockSpec(memory_space=pltpu.HBM)] * 5,
        out_specs=(vmem, pl.BlockSpec(memory_space=pltpu.SMEM)),
        scratch_shapes=[
            pltpu.VMEM((ROWS, FEATS), jnp.int32),
            pltpu.VMEM(shape, jnp.int32),
            pltpu.VMEM(shape, jnp.int32),
            pltpu.VMEM(shape, BF),
            pltpu.VMEM(shape, BF),
            pltpu.VMEM((16, ROWS), BF),
            pltpu.VMEM((32, 8, ROWS), f32),
            pltpu.VMEM((32, 8, ROWS), f32),
            pltpu.VMEM((2, 128, ROWS), BF),
            pltpu.VMEM((2, 256, ROWS), BF),
            pltpu.VMEM((2, 256, 128), f32),
            pltpu.VMEM((2, 4, 2, NX, 32, 128), f32),
            pltpu.VMEM((4, 2, NX, 32, 128), f32),
            pltpu.VMEM((4, 2, NX, 32, 128), f32),
            pltpu.VMEM((4, NX - 1, 2, 32, 128), f32),
            pltpu.VMEM((4, 2, 32, 128), f32),
            pltpu.VMEM((NZ - 1, 32, 128), f32),
            pltpu.VMEM((4, 8, 128), f32),
            pltpu.VMEM((4, 7, 8, 128), f32),
            dma((5,)), dma((4,)), dma((4,)), dma((4, 3)), dma((4, 3)), dma((7,)), dma((7,)), dma((4, 7)), dma((4, 7)),
        ],
        compiler_params=pltpu.CompilerParams(collective_id=0, has_side_effects=True, vmem_limit_bytes=24 << 20),
    )(bin_values, leaf_ids.reshape(shape), treated.reshape(shape), gradient.reshape(shape), hessian.reshape(shape))


def solution(mesh):
    in_specs = (P("row", "feat"), P("row"), P("row"), P("row"), P("row"))
    out_specs = (P(None, ("feat", "row"), None), P())
    return jax.shard_map(body, mesh=mesh, in_specs=in_specs, out_specs=out_specs, check_vma=False)
```

```python
import jax
import jax.numpy as jnp
from jax import lax
from jax.experimental import pallas as pl
from jax.experimental.pallas import tpu as pltpu
from jax.sharding import PartitionSpec as P

MESH = pl.DeviceIdType.MESH
BF = jnp.bfloat16
F32 = jnp.float32
ROWS = 2048
FEATS = 128
TILE = 256
TILES = ROWS // TILE
PAIRS = 8
NX, NZ, NY = 4, 8, 8


def load_stats(leaf_ref, arm_ref, grad_ref, hess_ref, stat_scr):
    stat = lax.broadcasted_iota(jnp.int32, (16, 128), 0)
    kind, leaf_of = stat // 4, stat % 4
    for c in range(ROWS // 128):
        grad = grad_ref[c : c + 1, :].astype(F32)
        hess = hess_ref[c : c + 1, :].astype(F32)
        keep = (leaf_ref[c : c + 1, :] == leaf_of) & ((arm_ref[c : c + 1, :] == 1) == (kind < 2))
        value = jnp.where(kind % 2 == 0, grad, hess)
        stat_scr[:, c * 128 : (c + 1) * 128] = jnp.where(keep, value, 0.0).astype(BF)


def lane_orders(z):
    feat = lax.broadcasted_iota(jnp.int32, (TILE, 128), 0)
    lane = lax.broadcasted_iota(jnp.int32, (TILE, 128), 1)
    owner = lane // 8
    core, u, x = owner // 8, owner // 4 % 2, owner % 4
    orders = []
    for c in range(4):
        far = lax.rem(z + jnp.where(u == 0, 4 + c, 3 - c), NZ)
        orders.append((feat == ((x * NZ + far) * 2 + core) * 2 + lane % 2).astype(F32).astype(BF))
    return [jnp.concatenate(orders[:2], axis=1), jnp.concatenate(orders[2:], axis=1)]


def spread_bins(accs, orders, bins_ref, bins_scr):
    def drain(r):
        rows = slice(r * TILE, (r + 1) * TILE)
        for p in range(2):
            spread = pltpu.matmul_pop(accs[2 * (r % 2) + p]).astype(BF)
            bins_scr[2 * p, rows, :] = spread[:, :128]
            bins_scr[2 * p + 1, rows, :] = spread[:, 128:]

    for p in range(2):
        pltpu.matmul_push_rhs(orders[p], staging_register=0, mxu_index=p)
    for r in range(TILES):
        block = bins_ref[r * TILE : (r + 1) * TILE, :].astype(F32).astype(BF)
        block = jnp.concatenate([block, block], axis=1)
        for p in range(2):
            pltpu.matmul_acc_lhs(accs[2 * (r % 2) + p], block, load_staged_rhs=0 if r == 0 else None)
        if r:
            drain(r - 1)
    drain(TILES - 1)


def half_chunk(accs, c, w, stat_scr, bins_scr, turn_scr):
    shape = (16, 16, 128)
    one, zero = jnp.ones(shape, BF), jnp.zeros(shape, BF)
    group = lax.broadcasted_iota(jnp.int32, (16, 128), 1) % 8 // 2
    first = 2 * PAIRS * w
    wanted = [(group * 32 + (first + q)).astype(F32).astype(BF)[None] for q in range(2 * PAIRS)]
    for k in range(TILES):
        rows = slice(k * TILE, (k + 1) * TILE)
        bins = bins_scr[c, rows, :].reshape(shape)
        stat = stat_scr[:, rows]
        for q in range(PAIRS):
            hot = [jnp.where(bins == wanted[2 * q + e], one, zero).reshape(TILE, 128) for e in range(2)]
            reg = (k * (PAIRS // 2) + q // 2) % 2
            pltpu.matmul_push_rhs(jnp.concatenate(hot, axis=1), staging_register=reg, mxu_index=q % 2)
            pltpu.matmul_acc_lhs(accs[q], stat, load_staged_rhs=reg)
    for q in range(PAIRS):
        sums = pltpu.matmul_pop(accs[q])
        for e in range(2):
            turn_scr[pl.ds(first + 2 * q + e, 16, stride=32), :] = sums[:, e * 128 : (e + 1) * 128]


def turn_chunk(c, turn_scr, hist):
    for t in range(4):
        turned = turn_scr[t * 128 : (t + 1) * 128, :].T
        hist[c, :, :, :, :, t * 128 : (t + 1) * 128] = turned.reshape(2, 2, NX, 8, 128)


def score(totals):
    grad_t, hess_t, grad_c, hess_c = (totals[8 * k : 8 * k + 8] for k in range(4))
    value_t = grad_t / (hess_t + 1.0)
    value_c = grad_c / (hess_c + 1.0)
    spread = value_t - value_c
    return grad_t * value_t + grad_c * value_c + (hess_t + hess_c) * spread * spread


def finish(block, gain_ref):
    x = jnp.concatenate([block[:, 128 * k : 128 * (k + 1)] for k in range(4)], axis=0)
    low = lax.broadcasted_iota(jnp.int32, (32, 128), 1) % 32
    sub = lax.broadcasted_iota(jnp.int32, (32, 128), 0) % 8
    for shift in (1, 2, 4, 8, 16):
        x = x + jnp.where(low >= shift, pltpu.roll(x, shift, 1), 0.0)
    total = jnp.where(low == 31, x, 0.0)
    for shift in (1, 2, 4, 8, 16):
        total = total + jnp.where(low <= 31 - shift, pltpu.roll(total, 128 - shift, 1), 0.0)
    upto = total + jnp.where(sub >= 2, pltpu.roll(total, 2, 0), 0.0)
    upto = upto + jnp.where(sub >= 4, pltpu.roll(upto, 4, 0), 0.0)
    left = x + jnp.where(sub >= 2, pltpu.roll(upto, 2, 0), 0.0)
    parent = jnp.where(sub >= 6, upto, 0.0)
    parent = parent + jnp.where((sub >= 4) & (sub < 6), pltpu.roll(parent, 30, 0), 0.0)
    parent = parent + jnp.where(sub < 4, pltpu.roll(parent, 28, 0), 0.0)
    gain = score(left) + score(parent - left) - score(parent)
    lane_block = lax.broadcasted_iota(jnp.int32, (8, 128), 1) // 32
    row_block = lax.broadcasted_iota(jnp.int32, (8, 128), 0) // 2
    out = gain
    for d in range(1, 4):
        moved = pltpu.roll(pltpu.roll(gain, 32 * d, 1), 8 - 2 * d, 0)
        out = jnp.where((lane_block + 4 - row_block) % 4 == d, moved, out)
    gain_ref[...] = out
    return jnp.max(gain, axis=0, keepdims=True)


def kernel(
    bins_hbm, leaf_hbm, arm_hbm, grad_hbm, hess_hbm, gain_ref, best_ref,
    bins_ref, leaf_ref, arm_ref, grad_ref, hess_ref, stat_scr, bins_scr, turn_scr,
    hist, core_in, core_sum, x_in, x_sum, z_in, last_x, last_z, top_out, top_in,
    load_sem, core_send, core_recv, x_send, x_recv, z_send, z_recv,
    last_x_send, last_x_recv, last_z_send, last_z_recv, top_send, top_recv,
):
    feat = lax.axis_index("feat")
    row = lax.axis_index("row")
    core = lax.rem(row, 2)
    z = lax.rem(row // 2, NZ)
    x = row // (2 * NZ)

    def at(dx, dz, core_):
        return (feat, (lax.rem(x + dx, NX) * NZ + lax.rem(z + dz, NZ)) * 2 + core_)

    other = at(0, 0, 1 - core)
    x_peer = [at(d, 0, core) for d in range(NX)]
    y_peer = [(lax.rem(feat + d, NY), row) for d in range(NY)]

    loads = [
        pltpu.make_async_copy(src, dst, load_sem.at[k])
        for k, (src, dst) in enumerate(
            zip(
                (leaf_hbm, arm_hbm, grad_hbm, hess_hbm, bins_hbm),
                (leaf_ref, arm_ref, grad_ref, hess_ref, bins_ref),
            )
        )
    ]
    for load in loads:
        load.start()
    barrier = pltpu.get_barrier_semaphore()
    greeted = [other] + x_peer[1:] + [at(0, d, core) for d in range(1, NZ)] + y_peer[1:]
    greeted += [at(d, e, core) for d in range(1, NX) for e in (1, NZ - 1)]
    for peer in greeted:
        pl.semaphore_signal(barrier, inc=1, device_id=peer, device_id_type=MESH)

    for load in loads[:4]:
        load.wait()
    load_stats(leaf_ref, arm_ref, grad_ref, hess_ref, stat_scr)
    orders = lane_orders(z)
    loads[4].wait()
    pl.run_scoped(
        lambda *accs: spread_bins(accs, orders, bins_ref, bins_scr),
        *[pltpu.ACC(q % 2)((TILE, TILE), F32) for q in range(4)],
    )

    def copy(src, dst, send, recv, peer):
        return pltpu.make_async_remote_copy(
            src_ref=src, dst_ref=dst, send_sem=send, recv_sem=recv, device_id=peer, device_id_type=MESH
        )

    def core_copy(c):
        return copy(hist.at[c, 1 - core], core_in.at[c], core_send.at[c], core_recv.at[c], other)

    def x_copy(c, d):
        return copy(
            core_sum.at[c, :, lax.rem(x + d, NX)], x_in.at[c, d - 1], x_send.at[c, d - 1], x_recv.at[c, d - 1], x_peer[d]
        )

    def z_copy(c, u):
        d = 3 - c if u else 4 + c
        return copy(x_sum.at[c, u], z_in.at[d - 1], z_send.at[d - 1], z_recv.at[d - 1], at(0, d, core))

    def last_x_copy(d):
        return copy(
            core_sum.at[3, 1, lax.rem(x + d, NX)], last_x.at[d - 1], last_x_send.at[d - 1], last_x_recv.at[d - 1], x_peer[d]
        )

    def last_z_copy(d):
        return copy(
            core_sum.at[3, 0, lax.rem(x + d, NX)], last_z.at[d], last_z_send.at[d], last_z_recv.at[d], at(d, NZ - 1, core)
        )

    def add_core(c):
        core_copy(c).wait_recv()
        core_sum[c] = hist[c, core] + core_in[c]

    def start_x(c):
        add_core(c)
        for d in (2, 1, 3):
            x_copy(c, d).start()

    def start_z(c):
        for d in (1, 3, 2):
            x_copy(c, d).wait_recv()
        x_sum[c] = core_sum[c, :, x] + x_in[c, 0] + x_in[c, 1] + x_in[c, 2]
        for u in range(2):
            z_copy(c, u).start()

    def all_halves(*accs):
        def step(h, carry):
            c, w = h // 2, h % 2
            half_chunk(accs, c, w, stat_scr, bins_scr, turn_scr)

            @pl.when(h == 1)
            def _():
                pl.semaphore_wait(barrier, len(greeted))

            @pl.when(w == 1)
            def _():
                turn_chunk(c, turn_scr, hist)
                core_copy(c).start()

            @pl.when((w == 0) & (c >= 1))
            def _():
                start_x(c - 1)

            @pl.when((w == 0) & (c >= 2))
            def _():
                start_z(c - 2)

            return carry

        lax.fori_loop(0, 8, step, 0)

    pl.run_scoped(all_halves, *[pltpu.ACC(q % 2)((16, TILE), F32) for q in range(PAIRS)])

    add_core(3)
    for d in (2, 1, 3, 0):
        last_z_copy(d).start()
        if d:
            last_x_copy(d).start()
    start_z(2)
    block = core_sum[3, 1, x]
    for c in range(2):
        for u in range(2):
            z_copy(c, u).wait_recv()
            block = block + z_in[2 - c if u else 3 + c]
    for d in range(NX):
        last_z_copy(d).wait_recv()
        block = block + last_z[d]
        if d:
            last_x_copy(d).wait_recv()
            block = block + last_x[d - 1]
    for u in range(2):
        z_copy(2, u).wait_recv()
        block = block + z_in[0 if u else 5]

    top = finish(block, gain_ref)
    rounds = ([other], x_peer[1:], [at(0, d, core) for d in range(1, NZ)], y_peer[1:])
    top_copies = []
    for stage, peers in enumerate(rounds):
        top_out[stage] = top
        sent = []
        for k, peer in enumerate(peers):
            s = copy(top_out.at[stage], top_in.at[stage, k], top_send.at[stage, k], top_recv.at[stage, k], peer)
            s.start()
            sent.append(s)
        for k, s in enumerate(sent):
            s.wait_recv()
            top = jnp.maximum(top, top_in[stage, k])
        top_copies += sent
    for leaf in range(4):
        best_ref[leaf] = jnp.max(top[:, 32 * leaf : 32 * (leaf + 1)])
    for c in range(4):
        core_copy(c).wait_send()
    for c in range(3):
        for d in range(1, NX):
            x_copy(c, d).wait_send()
        for u in range(2):
            z_copy(c, u).wait_send()
    for d in range(NX):
        last_z_copy(d).wait_send()
        if d:
            last_x_copy(d).wait_send()
    for s in top_copies:
        s.wait_send()


def body(bin_values, leaf_ids, treated, gradient, hessian):
    shape = (ROWS // 128, 128)
    dma = pltpu.SemaphoreType.DMA
    block = (8, 512)
    gain, best = pl.pallas_call(
        kernel,
        out_shape=(jax.ShapeDtypeStruct((8, 128), F32), jax.ShapeDtypeStruct((4,), F32)),
        in_specs=[pl.BlockSpec(memory_space=pltpu.HBM)] * 5,
        out_specs=(pl.BlockSpec(memory_space=pltpu.VMEM), pl.BlockSpec(memory_space=pltpu.SMEM)),
        scratch_shapes=[
            pltpu.VMEM((ROWS, FEATS), jnp.int32),
            pltpu.VMEM(shape, jnp.int32),
            pltpu.VMEM(shape, jnp.int32),
            pltpu.VMEM(shape, BF),
            pltpu.VMEM(shape, BF),
            pltpu.VMEM((16, ROWS), BF),
            pltpu.VMEM((4, ROWS, 128), BF),
            pltpu.VMEM((512, 128), F32),
            pltpu.VMEM((4, 2, 2, NX) + block, F32),
            pltpu.VMEM((4, 2, NX) + block, F32),
            pltpu.VMEM((4, 2, NX) + block, F32),
            pltpu.VMEM((3, NX - 1, 2) + block, F32),
            pltpu.VMEM((3, 2) + block, F32),
            pltpu.VMEM((6,) + block, F32),
            pltpu.VMEM((NX - 1,) + block, F32),
            pltpu.VMEM((NX,) + block, F32),
            pltpu.VMEM((4, 1, 128), F32),
            pltpu.VMEM((4, 7, 1, 128), F32),
            dma((5,)), dma((4,)), dma((4,)), dma((3, 3)), dma((3, 3)), dma((6,)), dma((6,)),
            dma((3,)), dma((3,)), dma((4,)), dma((4,)), dma((4, 7)), dma((4, 7)),
        ],
        compiler_params=pltpu.CompilerParams(collective_id=0, has_side_effects=True, vmem_limit_bytes=56 << 20),
    )(bin_values, leaf_ids.reshape(shape), treated.reshape(shape), gradient.reshape(shape), hessian.reshape(shape))
    return gain.reshape(4, 2, 128), best


def solution(mesh):
    in_specs = (P("row", "feat"), P("row"), P("row"), P("row"), P("row"))
    out_specs = (P(None, ("feat", "row"), None), P())
    return jax.shard_map(body, mesh=mesh, in_specs=in_specs, out_specs=out_specs, check_vma=False)
```

```python
import jax
import jax.numpy as jnp
from jax import lax
from jax.experimental import pallas as pl
from jax.experimental.pallas import tpu as pltpu
from jax.sharding import PartitionSpec as P

MESH = pl.DeviceIdType.MESH
BF = jnp.bfloat16
F32 = jnp.float32
ROWS = 2048
FEATS = 128
TILE = 256
TILES = ROWS // TILE
PAIRS = 8
NX, NZ, NY = 4, 8, 8


def load_stats(leaf_ref, arm_ref, grad_ref, hess_ref, stat_scr):
    stat = lax.broadcasted_iota(jnp.int32, (16, 128), 0)
    kind, leaf_of = stat // 4, stat % 4
    for c in range(ROWS // 128):
        grad = grad_ref[c : c + 1, :].astype(F32)
        hess = hess_ref[c : c + 1, :].astype(F32)
        keep = (leaf_ref[c : c + 1, :] == leaf_of) & ((arm_ref[c : c + 1, :] == 1) == (kind < 2))
        value = jnp.where(kind % 2 == 0, grad, hess)
        stat_scr[:, c * 128 : (c + 1) * 128] = jnp.where(keep, value, 0.0).astype(BF)


def lane_orders(z):
    feat = lax.broadcasted_iota(jnp.int32, (TILE, 128), 0)
    lane = lax.broadcasted_iota(jnp.int32, (TILE, 128), 1)
    owner = lane // 8
    core, u, x = owner // 8, owner // 4 % 2, owner % 4
    orders = []
    for c in range(4):
        far = lax.rem(z + jnp.where(u == 0, 4 + c, 3 - c), NZ)
        orders.append((feat == ((x * NZ + far) * 2 + core) * 2 + lane % 2).astype(F32).astype(BF))
    return [jnp.concatenate(orders[:2], axis=1), jnp.concatenate(orders[2:], axis=1)]


def spread_bins(accs, orders, bins_ref, bins_scr):
    def drain(r):
        rows = slice(r * TILE, (r + 1) * TILE)
        for p in range(2):
            spread = pltpu.matmul_pop(accs[2 * (r % 2) + p]).astype(BF)
            bins_scr[2 * p, rows, :] = spread[:, :128]
            bins_scr[2 * p + 1, rows, :] = spread[:, 128:]

    for p in range(2):
        pltpu.matmul_push_rhs(orders[p], staging_register=0, mxu_index=p)
    for r in range(TILES):
        block = bins_ref[r * TILE : (r + 1) * TILE, :].astype(F32).astype(BF)
        block = jnp.concatenate([block, block], axis=1)
        for p in range(2):
            pltpu.matmul_acc_lhs(accs[2 * (r % 2) + p], block, load_staged_rhs=0 if r == 0 else None)
        if r:
            drain(r - 1)
    drain(TILES - 1)


def half_chunk(accs, c, w, stat_scr, bins_scr, turn_scr):
    shape = (16, 16, 128)
    one, zero = jnp.ones(shape, BF), jnp.zeros(shape, BF)
    group = lax.broadcasted_iota(jnp.int32, (16, 128), 1) % 8 // 2
    first = 2 * PAIRS * w
    wanted = [(group * 32 + (first + q)).astype(F32).astype(BF)[None] for q in range(2 * PAIRS)]
    for k in range(TILES):
        rows = slice(k * TILE, (k + 1) * TILE)
        bins = bins_scr[c, rows, :].reshape(shape)
        stat = stat_scr[:, rows]
        for q in range(PAIRS):
            hot = [jnp.where(bins == wanted[2 * q + e], one, zero).reshape(TILE, 128) for e in range(2)]
            reg = (k * (PAIRS // 2) + q // 2) % 2
            pltpu.matmul_push_rhs(jnp.concatenate(hot, axis=1), staging_register=reg, mxu_index=q % 2)
            pltpu.matmul_acc_lhs(accs[q], stat, load_staged_rhs=reg)
    for q in range(PAIRS):
        sums = pltpu.matmul_pop(accs[q])
        for e in range(2):
            turn_scr[pl.ds(first + 2 * q + e, 16, stride=32), :] = sums[:, e * 128 : (e + 1) * 128]


def turn_chunk(c, turn_scr, hist):
    for t in range(4):
        turned = turn_scr[t * 128 : (t + 1) * 128, :].T
        hist[c, :, :, :, :, t * 128 : (t + 1) * 128] = turned.reshape(2, 2, NX, 8, 128)


def score(totals):
    grad_t, hess_t, grad_c, hess_c = (totals[8 * k : 8 * k + 8] for k in range(4))
    value_t = grad_t / (hess_t + 1.0)
    value_c = grad_c / (hess_c + 1.0)
    spread = value_t - value_c
    return grad_t * value_t + grad_c * value_c + (hess_t + hess_c) * spread * spread


def finish(block):
    x = jnp.concatenate([block[:, 128 * k : 128 * (k + 1)] for k in range(4)], axis=0)
    low = lax.broadcasted_iota(jnp.int32, (32, 128), 1) % 32
    sub = lax.broadcasted_iota(jnp.int32, (32, 128), 0) % 8
    for shift in (1, 2, 4, 8, 16):
        x = x + jnp.where(low >= shift, pltpu.roll(x, shift, 1), 0.0)
    total = jnp.where(low == 31, x, 0.0)
    for shift in (1, 2, 4, 8, 16):
        total = total + jnp.where(low <= 31 - shift, pltpu.roll(total, 128 - shift, 1), 0.0)
    upto = total + jnp.where(sub >= 2, pltpu.roll(total, 2, 0), 0.0)
    upto = upto + jnp.where(sub >= 4, pltpu.roll(upto, 4, 0), 0.0)
    left = x + jnp.where(sub >= 2, pltpu.roll(upto, 2, 0), 0.0)
    parent = jnp.where(sub >= 6, upto, 0.0)
    parent = parent + jnp.where((sub >= 4) & (sub < 6), pltpu.roll(parent, 30, 0), 0.0)
    parent = parent + jnp.where(sub < 4, pltpu.roll(parent, 28, 0), 0.0)
    gain = score(left) + score(parent - left) - score(parent)
    return gain


def store_gain(gain, gain_ref):
    lane_block = lax.broadcasted_iota(jnp.int32, (8, 128), 1) // 32
    row_block = lax.broadcasted_iota(jnp.int32, (8, 128), 0) // 2
    out = gain
    for d in range(1, 4):
        moved = pltpu.roll(pltpu.roll(gain, 32 * d, 1), 8 - 2 * d, 0)
        out = jnp.where((lane_block + 4 - row_block) % 4 == d, moved, out)
    gain_ref[...] = out


def kernel(
    bins_hbm, leaf_hbm, arm_hbm, grad_hbm, hess_hbm, gain_ref, best_ref,
    bins_ref, leaf_ref, arm_ref, grad_ref, hess_ref, stat_scr, bins_scr, turn_scr,
    hist, core_in, core_sum, x_in, x_sum, z_in, last_x, last_z, top_out, top_in,
    load_sem, core_send, core_recv, x_send, x_recv, z_send, z_recv,
    last_x_send, last_x_recv, last_z_send, last_z_recv, top_send, top_recv,
):
    feat = lax.axis_index("feat")
    row = lax.axis_index("row")
    core = lax.rem(row, 2)
    z = lax.rem(row // 2, NZ)
    x = row // (2 * NZ)

    def at(dx, dz, core_):
        return (feat, (lax.rem(x + dx, NX) * NZ + lax.rem(z + dz, NZ)) * 2 + core_)

    other = at(0, 0, 1 - core)
    x_peer = [at(d, 0, core) for d in range(NX)]
    y_peer = [(lax.rem(feat + d, NY), row) for d in range(NY)]

    loads = [
        pltpu.make_async_copy(src, dst, load_sem.at[k])
        for k, (src, dst) in enumerate(
            zip(
                (leaf_hbm, arm_hbm, grad_hbm, hess_hbm, bins_hbm),
                (leaf_ref, arm_ref, grad_ref, hess_ref, bins_ref),
            )
        )
    ]
    for load in loads:
        load.start()
    barrier = pltpu.get_barrier_semaphore()
    greeted = [other] + x_peer[1:] + [at(0, d, core) for d in range(1, NZ)] + y_peer[1:]
    greeted += [at(d, e, core) for d in range(1, NX) for e in (1, NZ - 1)]
    for peer in greeted:
        pl.semaphore_signal(barrier, inc=1, device_id=peer, device_id_type=MESH)

    for load in loads[:4]:
        load.wait()
    load_stats(leaf_ref, arm_ref, grad_ref, hess_ref, stat_scr)
    orders = lane_orders(z)
    loads[4].wait()
    pl.run_scoped(
        lambda *accs: spread_bins(accs, orders, bins_ref, bins_scr),
        *[pltpu.ACC(q % 2)((TILE, TILE), F32) for q in range(4)],
    )

    def copy(src, dst, send, recv, peer):
        return pltpu.make_async_remote_copy(
            src_ref=src, dst_ref=dst, send_sem=send, recv_sem=recv, device_id=peer, device_id_type=MESH
        )

    def core_copy(c):
        return copy(hist.at[c, 1 - core], core_in.at[c], core_send.at[c], core_recv.at[c], other)

    def x_copy(c, d):
        return copy(
            core_sum.at[c, :, lax.rem(x + d, NX)], x_in.at[c, d - 1], x_send.at[c, d - 1], x_recv.at[c, d - 1], x_peer[d]
        )

    def z_copy(c, u):
        d = 3 - c if u else 4 + c
        return copy(x_sum.at[c, u], z_in.at[d - 1], z_send.at[d - 1], z_recv.at[d - 1], at(0, d, core))

    def last_x_copy(d):
        return copy(
            core_sum.at[3, 1, lax.rem(x + d, NX)], last_x.at[d - 1], last_x_send.at[d - 1], last_x_recv.at[d - 1], x_peer[d]
        )

    def last_z_copy(d):
        return copy(
            core_sum.at[3, 0, lax.rem(x + d, NX)], last_z.at[d], last_z_send.at[d], last_z_recv.at[d], at(d, NZ - 1, core)
        )

    def add_core(c):
        core_copy(c).wait_recv()
        core_sum[c] = hist[c, core] + core_in[c]

    def start_x(c):
        add_core(c)
        for d in (2, 1, 3):
            x_copy(c, d).start()

    def start_z(c):
        for d in (1, 3, 2):
            x_copy(c, d).wait_recv()
        x_sum[c] = core_sum[c, :, x] + x_in[c, 0] + x_in[c, 1] + x_in[c, 2]
        for u in range(2):
            z_copy(c, u).start()

    def all_halves(*accs):
        def step(h, carry):
            c, w = h // 2, h % 2
            half_chunk(accs, c, w, stat_scr, bins_scr, turn_scr)

            @pl.when(h == 1)
            def _():
                pl.semaphore_wait(barrier, len(greeted))

            @pl.when(w == 1)
            def _():
                turn_chunk(c, turn_scr, hist)
                core_copy(c).start()

            @pl.when((w == 0) & (c >= 1))
            def _():
                start_x(c - 1)

            @pl.when((w == 0) & (c >= 2))
            def _():
                start_z(c - 2)

            return carry

        lax.fori_loop(0, 8, step, 0)

    pl.run_scoped(all_halves, *[pltpu.ACC(q % 2)((16, TILE), F32) for q in range(PAIRS)])

    add_core(3)
    for d in (2, 1, 3, 0):
        last_z_copy(d).start()
        if d:
            last_x_copy(d).start()
    start_z(2)
    block = core_sum[3, 1, x]
    for c in range(2):
        for u in range(2):
            z_copy(c, u).wait_recv()
            block = block + z_in[2 - c if u else 3 + c]
    for d in range(NX):
        last_z_copy(d).wait_recv()
        block = block + last_z[d]
        if d:
            last_x_copy(d).wait_recv()
            block = block + last_x[d - 1]
    for u in range(2):
        z_copy(2, u).wait_recv()
        block = block + z_in[0 if u else 5]

    gain = finish(block)
    top = jnp.max(gain, axis=0, keepdims=True)

    def wait_sends():
        for c in range(4):
            core_copy(c).wait_send()
        for c in range(3):
            for d in range(1, NX):
                x_copy(c, d).wait_send()
            for u in range(2):
                z_copy(c, u).wait_send()
        for d in range(NX):
            last_z_copy(d).wait_send()
            if d:
                last_x_copy(d).wait_send()

    rounds = ([other], x_peer[1:], [at(0, d, core) for d in range(1, NZ)], y_peer[1:])
    top_copies = []
    for stage, peers in enumerate(rounds):
        top_out[stage] = top
        sent = []
        for k, peer in enumerate(peers):
            s = copy(top_out.at[stage], top_in.at[stage, k], top_send.at[stage, k], top_recv.at[stage, k], peer)
            s.start()
            sent.append(s)
        if stage == 0:
            store_gain(gain, gain_ref)
        if stage == 2:
            wait_sends()
        if stage:
            for s in top_copies:
                s.wait_send()
            top_copies = []
        for k, s in enumerate(sent):
            s.wait_recv()
            top = jnp.maximum(top, top_in[stage, k])
        top_copies += sent
    for leaf in range(4):
        best_ref[leaf] = jnp.max(top[:, 32 * leaf : 32 * (leaf + 1)])
    for s in top_copies:
        s.wait_send()


def body(bin_values, leaf_ids, treated, gradient, hessian):
    shape = (ROWS // 128, 128)
    dma = pltpu.SemaphoreType.DMA
    block = (8, 512)
    bin_values, leaf_ids, treated, gradient, hessian = (
        pltpu.with_memory_space_constraint(v, pltpu.HBM)
        for v in (bin_values, leaf_ids.reshape(shape), treated.reshape(shape), gradient.reshape(shape), hessian.reshape(shape))
    )
    gain, best = pl.pallas_call(
        kernel,
        out_shape=(jax.ShapeDtypeStruct((8, 128), F32), jax.ShapeDtypeStruct((4,), F32)),
        in_specs=[pl.BlockSpec(memory_space=pltpu.HBM)] * 5,
        out_specs=(pl.BlockSpec(memory_space=pltpu.VMEM), pl.BlockSpec(memory_space=pltpu.SMEM)),
        scratch_shapes=[
            pltpu.VMEM((ROWS, FEATS), jnp.int32),
            pltpu.VMEM(shape, jnp.int32),
            pltpu.VMEM(shape, jnp.int32),
            pltpu.VMEM(shape, BF),
            pltpu.VMEM(shape, BF),
            pltpu.VMEM((16, ROWS), BF),
            pltpu.VMEM((4, ROWS, 128), BF),
            pltpu.VMEM((512, 128), F32),
            pltpu.VMEM((4, 2, 2, NX) + block, F32),
            pltpu.VMEM((4, 2, NX) + block, F32),
            pltpu.VMEM((4, 2, NX) + block, F32),
            pltpu.VMEM((3, NX - 1, 2) + block, F32),
            pltpu.VMEM((3, 2) + block, F32),
            pltpu.VMEM((6,) + block, F32),
            pltpu.VMEM((NX - 1,) + block, F32),
            pltpu.VMEM((NX,) + block, F32),
            pltpu.VMEM((4, 1, 128), F32),
            pltpu.VMEM((4, 7, 1, 128), F32),
            dma((5,)), dma((4,)), dma((4,)), dma((3, 3)), dma((3, 3)), dma((6,)), dma((6,)),
            dma((3,)), dma((3,)), dma((4,)), dma((4,)), dma((4, 7)), dma((4, 7)),
        ],
        compiler_params=pltpu.CompilerParams(collective_id=0, has_side_effects=True, vmem_limit_bytes=24 << 20),
    )(bin_values, leaf_ids, treated, gradient, hessian)
    return gain.reshape(4, 2, 128), best


def solution(mesh):
    in_specs = (P("row", "feat"), P("row"), P("row"), P("row"), P("row"))
    out_specs = (P(None, ("feat", "row"), None), P())
    return jax.shard_map(body, mesh=mesh, in_specs=in_specs, out_specs=out_specs, check_vma=False)
```

```python
import jax
import jax.numpy as jnp
from jax import lax
from jax.experimental import pallas as pl
from jax.experimental.pallas import tpu as pltpu
from jax.sharding import PartitionSpec as P

MESH = pl.DeviceIdType.MESH
BF = jnp.bfloat16
F32 = jnp.float32
ROWS = 2048
FEATS = 128
TILE = 256
TILES = ROWS // TILE
PAIRS = 8
NX, NZ, NY = 4, 8, 8


def load_stats(leaf_ref, arm_ref, grad_ref, hess_ref, stat_scr):
    stat = lax.broadcasted_iota(jnp.int32, (16, 128), 0)
    kind, leaf_of = stat // 4, stat % 4
    for c in range(ROWS // 128):
        grad = grad_ref[c : c + 1, :].astype(F32)
        hess = hess_ref[c : c + 1, :].astype(F32)
        keep = (leaf_ref[c : c + 1, :] == leaf_of) & ((arm_ref[c : c + 1, :] == 1) == (kind < 2))
        value = jnp.where(kind % 2 == 0, grad, hess)
        stat_scr[:, c * 128 : (c + 1) * 128] = jnp.where(keep, value, 0.0).astype(BF)


def lane_orders(z):
    feat = lax.broadcasted_iota(jnp.int32, (TILE, 128), 0)
    lane = lax.broadcasted_iota(jnp.int32, (TILE, 128), 1)
    owner = lane // 8
    core, u, x = owner // 8, owner // 4 % 2, owner % 4
    orders = []
    for c in range(4):
        far = lax.rem(z + jnp.where(u == 0, 4 + c, 3 - c), NZ)
        orders.append((feat == ((x * NZ + far) * 2 + core) * 2 + lane % 2).astype(F32).astype(BF))
    return [jnp.concatenate(orders[:2], axis=1), jnp.concatenate(orders[2:], axis=1)]


def spread_bins(accs, orders, bins_ref, bins_scr):
    def drain(r):
        rows = slice(r * TILE, (r + 1) * TILE)
        for p in range(2):
            spread = pltpu.matmul_pop(accs[2 * (r % 2) + p]).astype(BF)
            bins_scr[2 * p, rows, :] = spread[:, :128]
            bins_scr[2 * p + 1, rows, :] = spread[:, 128:]

    for p in range(2):
        pltpu.matmul_push_rhs(orders[p], staging_register=0, mxu_index=p)
    for r in range(TILES):
        block = bins_ref[r * TILE : (r + 1) * TILE, :].astype(F32).astype(BF)
        block = jnp.concatenate([block, block], axis=1)
        for p in range(2):
            pltpu.matmul_acc_lhs(accs[2 * (r % 2) + p], block, load_staged_rhs=0 if r == 0 else None)
        if r:
            drain(r - 1)
    drain(TILES - 1)


def half_chunk(accs, c, w, stat_scr, bins_scr, turn_scr):
    shape = (16, 16, 128)
    one, zero = jnp.ones(shape, BF), jnp.zeros(shape, BF)
    group = lax.broadcasted_iota(jnp.int32, (16, 128), 1) % 8 // 2
    first = 2 * PAIRS * w
    past = [(group * 32 + (first + q + 1)).astype(F32).astype(BF)[None] for q in range(2 * PAIRS)]
    for k in range(TILES):
        rows = slice(k * TILE, (k + 1) * TILE)
        bins = bins_scr[c, rows, :].reshape(shape)
        stat = stat_scr[:, rows]
        for q in range(PAIRS):
            hot = [jnp.clip(past[2 * q + e] - bins, zero, one).reshape(TILE, 128) for e in range(2)]
            reg = (k * (PAIRS // 2) + q // 2) % 2
            pltpu.matmul_push_rhs(jnp.concatenate(hot, axis=1), staging_register=reg, mxu_index=q % 2)
            pltpu.matmul_acc_lhs(accs[q], stat, load_staged_rhs=reg)
    for q in range(PAIRS):
        sums = pltpu.matmul_pop(accs[q])
        for e in range(2):
            turn_scr[pl.ds(first + 2 * q + e, 16, stride=32), :] = sums[:, e * 128 : (e + 1) * 128]


def turn_chunk(c, turn_scr, hist):
    for t in range(4):
        turned = turn_scr[t * 128 : (t + 1) * 128, :].T
        hist[c, :, :, :, :, t * 128 : (t + 1) * 128] = turned.reshape(2, 2, NX, 8, 128)


def score(totals):
    grad_t, hess_t, grad_c, hess_c = (totals[8 * k : 8 * k + 8] for k in range(4))
    value_t = grad_t / (hess_t + 1.0)
    value_c = grad_c / (hess_c + 1.0)
    spread = value_t - value_c
    return grad_t * value_t + grad_c * value_c + (hess_t + hess_c) * spread * spread


def finish(block):
    left = jnp.concatenate([block[:, 128 * k : 128 * (k + 1)] for k in range(4)], axis=0)
    leaf = lax.broadcasted_iota(jnp.int32, (32, 128), 1) // 32
    sub = lax.broadcasted_iota(jnp.int32, (32, 128), 0) % 8
    last = jnp.where(sub >= 6, left, 0.0)
    last = last + jnp.where((sub >= 4) & (sub < 6), pltpu.roll(last, 30, 0), 0.0)
    last = last + jnp.where(sub < 4, pltpu.roll(last, 28, 0), 0.0)
    parent = jnp.broadcast_to(last[:, 127:128], (32, 128))
    for k in range(3):
        parent = jnp.where(leaf == k, jnp.broadcast_to(last[:, 32 * k + 31 : 32 * k + 32], (32, 128)), parent)
    gain = score(left) + score(parent - left) - score(parent)
    return gain


def store_gain(gain, gain_ref):
    lane_block = lax.broadcasted_iota(jnp.int32, (8, 128), 1) // 32
    row_block = lax.broadcasted_iota(jnp.int32, (8, 128), 0) // 2
    out = gain
    for d in range(1, 4):
        moved = pltpu.roll(pltpu.roll(gain, 32 * d, 1), 8 - 2 * d, 0)
        out = jnp.where((lane_block + 4 - row_block) % 4 == d, moved, out)
    gain_ref[...] = out


def kernel(
    bins_hbm, leaf_hbm, arm_hbm, grad_hbm, hess_hbm, gain_ref, best_ref,
    bins_ref, leaf_ref, arm_ref, grad_ref, hess_ref, stat_scr, bins_scr, turn_scr,
    hist, core_in, core_sum, x_in, x_sum, z_in, last_x, last_z, top_out, top_in,
    load_sem, core_send, core_recv, x_send, x_recv, z_send, z_recv,
    last_x_send, last_x_recv, last_z_send, last_z_recv, top_send, top_recv,
):
    feat = lax.axis_index("feat")
    row = lax.axis_index("row")
    core = lax.rem(row, 2)
    z = lax.rem(row // 2, NZ)
    x = row // (2 * NZ)

    def at(dx, dz, core_):
        return (feat, (lax.rem(x + dx, NX) * NZ + lax.rem(z + dz, NZ)) * 2 + core_)

    other = at(0, 0, 1 - core)
    x_peer = [at(d, 0, core) for d in range(NX)]
    y_peer = [(lax.rem(feat + d, NY), row) for d in range(NY)]

    loads = [
        pltpu.make_async_copy(src, dst, load_sem.at[k])
        for k, (src, dst) in enumerate(
            zip(
                (leaf_hbm, arm_hbm, grad_hbm, hess_hbm, bins_hbm),
                (leaf_ref, arm_ref, grad_ref, hess_ref, bins_ref),
            )
        )
    ]
    for load in loads:
        load.start()
    barrier = pltpu.get_barrier_semaphore()
    greeted = [other] + x_peer[1:] + [at(0, d, core) for d in range(1, NZ)] + y_peer[1:]
    greeted += [at(d, e, core) for d in range(1, NX) for e in (1, NZ - 1)]
    for peer in greeted:
        pl.semaphore_signal(barrier, inc=1, device_id=peer, device_id_type=MESH)

    for load in loads[:4]:
        load.wait()
    load_stats(leaf_ref, arm_ref, grad_ref, hess_ref, stat_scr)
    orders = lane_orders(z)
    loads[4].wait()
    pl.run_scoped(
        lambda *accs: spread_bins(accs, orders, bins_ref, bins_scr),
        *[pltpu.ACC(q % 2)((TILE, TILE), F32) for q in range(4)],
    )

    def copy(src, dst, send, recv, peer):
        return pltpu.make_async_remote_copy(
            src_ref=src, dst_ref=dst, send_sem=send, recv_sem=recv, device_id=peer, device_id_type=MESH
        )

    def core_copy(c):
        return copy(hist.at[c, 1 - core], core_in.at[c], core_send.at[c], core_recv.at[c], other)

    def x_copy(c, d):
        return copy(
            core_sum.at[c, :, lax.rem(x + d, NX)], x_in.at[c, d - 1], x_send.at[c, d - 1], x_recv.at[c, d - 1], x_peer[d]
        )

    def z_copy(c, u):
        d = 3 - c if u else 4 + c
        return copy(x_sum.at[c, u], z_in.at[d - 1], z_send.at[d - 1], z_recv.at[d - 1], at(0, d, core))

    def last_x_copy(d):
        return copy(
            core_sum.at[3, 1, lax.rem(x + d, NX)], last_x.at[d - 1], last_x_send.at[d - 1], last_x_recv.at[d - 1], x_peer[d]
        )

    def last_z_copy(d):
        return copy(
            core_sum.at[3, 0, lax.rem(x + d, NX)], last_z.at[d], last_z_send.at[d], last_z_recv.at[d], at(d, NZ - 1, core)
        )

    def add_core(c):
        core_copy(c).wait_recv()
        core_sum[c] = hist[c, core] + core_in[c]

    def start_x(c):
        add_core(c)
        for d in (2, 1, 3):
            x_copy(c, d).start()

    def start_z(c):
        for d in (1, 3, 2):
            x_copy(c, d).wait_recv()
        x_sum[c] = core_sum[c, :, x] + x_in[c, 0] + x_in[c, 1] + x_in[c, 2]
        for u in range(2):
            z_copy(c, u).start()

    def all_halves(*accs):
        def step(h, carry):
            c, w = h // 2, h % 2
            half_chunk(accs, c, w, stat_scr, bins_scr, turn_scr)

            @pl.when(h == 1)
            def _():
                pl.semaphore_wait(barrier, len(greeted))

            @pl.when(w == 1)
            def _():
                turn_chunk(c, turn_scr, hist)
                core_copy(c).start()

            @pl.when((w == 0) & (c >= 1))
            def _():
                start_x(c - 1)

            @pl.when((w == 0) & (c >= 2))
            def _():
                start_z(c - 2)

            return carry

        lax.fori_loop(0, 8, step, 0)

    pl.run_scoped(all_halves, *[pltpu.ACC(q % 2)((16, TILE), F32) for q in range(PAIRS)])

    add_core(3)
    for d in (2, 1, 3, 0):
        last_z_copy(d).start()
        if d:
            last_x_copy(d).start()
    start_z(2)
    block = core_sum[3, 1, x]
    for c in range(2):
        for u in range(2):
            z_copy(c, u).wait_recv()
            block = block + z_in[2 - c if u else 3 + c]
    for d in range(NX):
        last_z_copy(d).wait_recv()
        block = block + last_z[d]
        if d:
            last_x_copy(d).wait_recv()
            block = block + last_x[d - 1]
    for u in range(2):
        z_copy(2, u).wait_recv()
        block = block + z_in[0 if u else 5]

    gain = finish(block)
    top = jnp.max(gain, axis=0, keepdims=True)

    def wait_sends():
        for c in range(4):
            core_copy(c).wait_send()
        for c in range(3):
            for d in range(1, NX):
                x_copy(c, d).wait_send()
            for u in range(2):
                z_copy(c, u).wait_send()
        for d in range(NX):
            last_z_copy(d).wait_send()
            if d:
                last_x_copy(d).wait_send()

    rounds = ([other], x_peer[1:], [at(0, d, core) for d in range(1, NZ)], y_peer[1:])
    top_copies = []
    for stage, peers in enumerate(rounds):
        top_out[stage] = top
        sent = []
        for k, peer in enumerate(peers):
            s = copy(top_out.at[stage], top_in.at[stage, k], top_send.at[stage, k], top_recv.at[stage, k], peer)
            s.start()
            sent.append(s)
        if stage == 0:
            store_gain(gain, gain_ref)
        if stage == 2:
            wait_sends()
        if stage:
            for s in top_copies:
                s.wait_send()
            top_copies = []
        for k, s in enumerate(sent):
            s.wait_recv()
            top = jnp.maximum(top, top_in[stage, k])
        top_copies += sent
    for leaf in range(4):
        best_ref[leaf] = jnp.max(top[:, 32 * leaf : 32 * (leaf + 1)])
    for s in top_copies:
        s.wait_send()


def body(bin_values, leaf_ids, treated, gradient, hessian):
    shape = (ROWS // 128, 128)
    dma = pltpu.SemaphoreType.DMA
    block = (8, 512)
    bin_values, leaf_ids, treated, gradient, hessian = (
        pltpu.with_memory_space_constraint(v, pltpu.HBM)
        for v in (bin_values, leaf_ids.reshape(shape), treated.reshape(shape), gradient.reshape(shape), hessian.reshape(shape))
    )
    gain, best = pl.pallas_call(
        kernel,
        out_shape=(jax.ShapeDtypeStruct((8, 128), F32), jax.ShapeDtypeStruct((4,), F32)),
        in_specs=[pl.BlockSpec(memory_space=pltpu.HBM)] * 5,
        out_specs=(pl.BlockSpec(memory_space=pltpu.VMEM), pl.BlockSpec(memory_space=pltpu.SMEM)),
        scratch_shapes=[
            pltpu.VMEM((ROWS, FEATS), jnp.int32),
            pltpu.VMEM(shape, jnp.int32),
            pltpu.VMEM(shape, jnp.int32),
            pltpu.VMEM(shape, BF),
            pltpu.VMEM(shape, BF),
            pltpu.VMEM((16, ROWS), BF),
            pltpu.VMEM((4, ROWS, 128), BF),
            pltpu.VMEM((512, 128), F32),
            pltpu.VMEM((4, 2, 2, NX) + block, F32),
            pltpu.VMEM((4, 2, NX) + block, F32),
            pltpu.VMEM((4, 2, NX) + block, F32),
            pltpu.VMEM((3, NX - 1, 2) + block, F32),
            pltpu.VMEM((3, 2) + block, F32),
            pltpu.VMEM((6,) + block, F32),
            pltpu.VMEM((NX - 1,) + block, F32),
            pltpu.VMEM((NX,) + block, F32),
            pltpu.VMEM((4, 1, 128), F32),
            pltpu.VMEM((4, 7, 1, 128), F32),
            dma((5,)), dma((4,)), dma((4,)), dma((3, 3)), dma((3, 3)), dma((6,)), dma((6,)),
            dma((3,)), dma((3,)), dma((4,)), dma((4,)), dma((4, 7)), dma((4, 7)),
        ],
        compiler_params=pltpu.CompilerParams(collective_id=0, has_side_effects=True, vmem_limit_bytes=24 << 20),
    )(bin_values, leaf_ids, treated, gradient, hessian)
    return gain.reshape(4, 2, 128), best


def solution(mesh):
    in_specs = (P("row", "feat"), P("row"), P("row"), P("row"), P("row"))
    out_specs = (P(None, ("feat", "row"), None), P())
    return jax.shard_map(body, mesh=mesh, in_specs=in_specs, out_specs=out_specs, check_vma=False)
```

```python
import jax
import jax.numpy as jnp
from jax import lax
from jax.experimental import pallas as pl
from jax.experimental.pallas import tpu as pltpu
from jax.sharding import PartitionSpec as P

MESH = pl.DeviceIdType.MESH
BF = jnp.bfloat16
F32 = jnp.float32
ROWS = 2048
FEATS = 128
TILE = 256
TILES = ROWS // TILE
PAIRS = 8
NX, NZ, NY = 4, 8, 8


def load_stats(leaf_ref, arm_ref, grad_ref, hess_ref, stat_scr):
    stat = lax.broadcasted_iota(jnp.int32, (16, 128), 0)
    kind, leaf_of = stat // 4, stat % 4
    for c in range(ROWS // 128):
        grad = grad_ref[c : c + 1, :].astype(F32)
        hess = hess_ref[c : c + 1, :].astype(F32)
        keep = (leaf_ref[c : c + 1, :] == leaf_of) & ((arm_ref[c : c + 1, :] == 1) == (kind < 2))
        value = jnp.where(kind % 2 == 0, grad, hess)
        stat_scr[:, c * 128 : (c + 1) * 128] = jnp.where(keep, value, 0.0).astype(BF)


def lane_orders(z):
    feat = lax.broadcasted_iota(jnp.int32, (TILE, 128), 0)
    lane = lax.broadcasted_iota(jnp.int32, (TILE, 128), 1)
    owner = lane // 8
    core, u, x = owner // 8, owner // 4 % 2, owner % 4
    orders = []
    for c in range(4):
        far = lax.rem(z + jnp.where(u == 0, 4 + c, 3 - c), NZ)
        orders.append((feat == ((x * NZ + far) * 2 + core) * 2 + lane % 2).astype(F32).astype(BF))
    return [jnp.concatenate(orders[:2], axis=1), jnp.concatenate(orders[2:], axis=1)]


def spread_bins(accs, orders, loads, bins_ref, bins_scr):
    def drain(r):
        rows = slice(r * TILE, (r + 1) * TILE)
        for p in range(2):
            spread = pltpu.matmul_pop(accs[2 * (r % 2) + p]).astype(BF)
            bins_scr[2 * p, rows, :] = spread[:, :128]
            bins_scr[2 * p + 1, rows, :] = spread[:, 128:]

    for p in range(2):
        pltpu.matmul_push_rhs(orders[p], staging_register=0, mxu_index=p)
    for r in range(TILES):
        if r % 2 == 0:
            loads[r // 2].wait()
        block = bins_ref[r * TILE : (r + 1) * TILE, :].astype(F32).astype(BF)
        block = jnp.concatenate([block, block], axis=1)
        for p in range(2):
            pltpu.matmul_acc_lhs(accs[2 * (r % 2) + p], block, load_staged_rhs=0 if r == 0 else None)
        if r:
            drain(r - 1)
    drain(TILES - 1)


def half_chunk(accs, c, w, stat_scr, bins_scr, turn_scr):
    shape = (16, 16, 128)
    one, zero = jnp.ones(shape, BF), jnp.zeros(shape, BF)
    group = lax.broadcasted_iota(jnp.int32, (16, 128), 1) % 8 // 2
    first = 2 * PAIRS * w
    past = [(group * 32 + (first + q + 1)).astype(F32).astype(BF)[None] for q in range(2 * PAIRS)]
    for k in range(TILES):
        rows = slice(k * TILE, (k + 1) * TILE)
        bins = bins_scr[c, rows, :].reshape(shape)
        stat = stat_scr[:, rows]
        for q in range(PAIRS):
            hot = [jnp.clip(past[2 * q + e] - bins, zero, one).reshape(TILE, 128) for e in range(2)]
            reg = (k * (PAIRS // 2) + q // 2) % 2
            pltpu.matmul_push_rhs(jnp.concatenate(hot, axis=1), staging_register=reg, mxu_index=q % 2)
            pltpu.matmul_acc_lhs(accs[q], stat, load_staged_rhs=reg)
    for q in range(PAIRS):
        sums = pltpu.matmul_pop(accs[q])
        for e in range(2):
            turn_scr[pl.ds(first + 2 * q + e, 16, stride=32), :] = sums[:, e * 128 : (e + 1) * 128]


def turn_chunk(c, turn_scr, hist):
    for t in range(4):
        turned = turn_scr[t * 128 : (t + 1) * 128, :].T
        hist[c, :, :, :, :, t * 128 : (t + 1) * 128] = turned.reshape(2, 2, NX, 8, 128)


def score(totals):
    grad_t, hess_t, grad_c, hess_c = (totals[8 * k : 8 * k + 8] for k in range(4))
    value_t = grad_t / (hess_t + 1.0)
    value_c = grad_c / (hess_c + 1.0)
    spread = value_t - value_c
    return grad_t * value_t + grad_c * value_c + (hess_t + hess_c) * spread * spread


def finish(block):
    left = jnp.concatenate([block[:, 128 * k : 128 * (k + 1)] for k in range(4)], axis=0)
    leaf = lax.broadcasted_iota(jnp.int32, (32, 128), 1) // 32
    sub = lax.broadcasted_iota(jnp.int32, (32, 128), 0) % 8
    last = jnp.where(sub >= 6, left, 0.0)
    last = last + jnp.where((sub >= 4) & (sub < 6), pltpu.roll(last, 30, 0), 0.0)
    last = last + jnp.where(sub < 4, pltpu.roll(last, 28, 0), 0.0)
    parent = jnp.broadcast_to(last[:, 127:128], (32, 128))
    for k in range(3):
        parent = jnp.where(leaf == k, jnp.broadcast_to(last[:, 32 * k + 31 : 32 * k + 32], (32, 128)), parent)
    gain = score(left) + score(parent - left) - score(parent)
    return gain


def store_gain(gain, gain_ref):
    lane_block = lax.broadcasted_iota(jnp.int32, (8, 128), 1) // 32
    row_block = lax.broadcasted_iota(jnp.int32, (8, 128), 0) // 2
    out = gain
    for d in range(1, 4):
        moved = pltpu.roll(pltpu.roll(gain, 32 * d, 1), 8 - 2 * d, 0)
        out = jnp.where((lane_block + 4 - row_block) % 4 == d, moved, out)
    gain_ref[...] = out


def kernel(
    bins_hbm, leaf_hbm, arm_hbm, grad_hbm, hess_hbm, gain_ref, best_ref,
    bins_ref, leaf_ref, arm_ref, grad_ref, hess_ref, stat_scr, bins_scr, turn_scr,
    hist, core_in, core_sum, x_in, x_sum, z_in, last_x, last_z, top_out, top_in,
    load_sem, core_send, core_recv, x_send, x_recv, z_send, z_recv,
    last_x_send, last_x_recv, last_z_send, last_z_recv, top_send, top_recv,
):
    feat = lax.axis_index("feat")
    row = lax.axis_index("row")
    core = lax.rem(row, 2)
    z = lax.rem(row // 2, NZ)
    x = row // (2 * NZ)

    def at(dx, dz, core_):
        return (feat, (lax.rem(x + dx, NX) * NZ + lax.rem(z + dz, NZ)) * 2 + core_)

    other = at(0, 0, 1 - core)
    x_peer = [at(d, 0, core) for d in range(NX)]
    y_peer = [(lax.rem(feat + d, NY), row) for d in range(NY)]

    pairs = [(leaf_hbm, leaf_ref), (arm_hbm, arm_ref), (grad_hbm, grad_ref), (hess_hbm, hess_ref)]
    pairs += [(bins_hbm.at[pl.ds(k * 512, 512)], bins_ref.at[pl.ds(k * 512, 512)]) for k in range(4)]
    loads = [pltpu.make_async_copy(src, dst, load_sem.at[k]) for k, (src, dst) in enumerate(pairs)]
    for load in loads:
        load.start()
    barrier = pltpu.get_barrier_semaphore()
    greeted = [other] + x_peer[1:] + [at(0, d, core) for d in range(1, NZ)] + y_peer[1:]
    greeted += [at(d, e, core) for d in range(1, NX) for e in (1, NZ - 1)]
    for peer in greeted:
        pl.semaphore_signal(barrier, inc=1, device_id=peer, device_id_type=MESH)

    for load in loads[:4]:
        load.wait()
    load_stats(leaf_ref, arm_ref, grad_ref, hess_ref, stat_scr)
    orders = lane_orders(z)
    pl.run_scoped(
        lambda *accs: spread_bins(accs, orders, loads[4:], bins_ref, bins_scr),
        *[pltpu.ACC(q % 2)((TILE, TILE), F32) for q in range(4)],
    )

    def copy(src, dst, send, recv, peer):
        return pltpu.make_async_remote_copy(
            src_ref=src, dst_ref=dst, send_sem=send, recv_sem=recv, device_id=peer, device_id_type=MESH
        )

    def core_copy(c):
        return copy(hist.at[c, 1 - core], core_in.at[c], core_send.at[c], core_recv.at[c], other)

    def last_core_copy(u):
        k = 3 + u
        return copy(hist.at[3, 1 - core, u], core_in.at[3, u], core_send.at[k], core_recv.at[k], other)

    def x_copy(c, d):
        return copy(
            core_sum.at[c, :, lax.rem(x + d, NX)], x_in.at[c, d - 1], x_send.at[c, d - 1], x_recv.at[c, d - 1], x_peer[d]
        )

    def z_copy(c, u):
        d = 3 - c if u else 4 + c
        return copy(x_sum.at[c, u], z_in.at[d - 1], z_send.at[d - 1], z_recv.at[d - 1], at(0, d, core))

    def last_x_copy(d):
        return copy(
            core_sum.at[3, 1, lax.rem(x + d, NX)], last_x.at[d - 1], last_x_send.at[d - 1], last_x_recv.at[d - 1], x_peer[d]
        )

    def last_z_copy(d):
        return copy(
            core_sum.at[3, 0, lax.rem(x + d, NX)], last_z.at[d], last_z_send.at[d], last_z_recv.at[d], at(d, NZ - 1, core)
        )

    def add_core(c):
        core_copy(c).wait_recv()
        core_sum[c] = hist[c, core] + core_in[c]

    def start_x(c):
        add_core(c)
        for d in (2, 1, 3):
            x_copy(c, d).start()

    def start_z(c):
        for d in (1, 3, 2):
            x_copy(c, d).wait_recv()
        x_sum[c] = core_sum[c, :, x] + x_in[c, 0] + x_in[c, 1] + x_in[c, 2]
        for u in range(2):
            z_copy(c, u).start()

    def all_halves(*accs):
        def step(h, carry):
            c, w = h // 2, h % 2
            half_chunk(accs, c, w, stat_scr, bins_scr, turn_scr)

            @pl.when(h == 1)
            def _():
                pl.semaphore_wait(barrier, len(greeted))

            @pl.when(w == 1)
            def _():
                turn_chunk(c, turn_scr, hist)

            @pl.when((w == 1) & (c < 3))
            def _():
                core_copy(c).start()

            @pl.when((w == 1) & (c == 3))
            def _():
                for u in range(2):
                    last_core_copy(u).start()

            @pl.when((w == 0) & (c >= 1))
            def _():
                start_x(c - 1)

            @pl.when((w == 0) & (c >= 2))
            def _():
                start_z(c - 2)

            return carry

        lax.fori_loop(0, 8, step, 0)

    pl.run_scoped(all_halves, *[pltpu.ACC(q % 2)((16, TILE), F32) for q in range(PAIRS)])

    for u in range(2):
        last_core_copy(u).wait_recv()
        core_sum[3, u] = hist[3, core, u] + core_in[3, u]
        for d in (2, 1, 3, 0):
            if u == 0:
                last_z_copy(d).start()
            elif d:
                last_x_copy(d).start()
    start_z(2)
    block = core_sum[3, 1, x]
    for c in range(2):
        for u in range(2):
            z_copy(c, u).wait_recv()
            block = block + z_in[2 - c if u else 3 + c]
    for d in range(NX):
        last_z_copy(d).wait_recv()
        block = block + last_z[d]
        if d:
            last_x_copy(d).wait_recv()
            block = block + last_x[d - 1]
    for u in range(2):
        z_copy(2, u).wait_recv()
        block = block + z_in[0 if u else 5]

    gain = finish(block)
    top = jnp.max(gain, axis=0, keepdims=True)

    def wait_sends():
        for u in range(2):
            last_core_copy(u).wait_send()
        for c in range(3):
            core_copy(c).wait_send()
            for d in range(1, NX):
                x_copy(c, d).wait_send()
            for u in range(2):
                z_copy(c, u).wait_send()
        for d in range(NX):
            last_z_copy(d).wait_send()
            if d:
                last_x_copy(d).wait_send()

    near_last = (4, 3, 5, 2, 6, 1, 7)
    rounds = (
        [other],
        [x_peer[d] for d in (2, 1, 3)],
        [at(0, d, core) for d in near_last],
        [y_peer[d] for d in near_last],
    )
    top_copies = []
    for stage, peers in enumerate(rounds):
        top_out[stage] = top
        sent = []
        for k, peer in enumerate(peers):
            s = copy(top_out.at[stage], top_in.at[stage, k], top_send.at[stage, k], top_recv.at[stage, k], peer)
            s.start()
            sent.append(s)
        if stage == 0:
            store_gain(gain, gain_ref)
        if stage == 2:
            wait_sends()
        if stage:
            for s in top_copies:
                s.wait_send()
            top_copies = []
        for s in reversed(sent):
            s.wait_recv()
        for k in range(len(sent)):
            top = jnp.maximum(top, top_in[stage, k])
        top_copies += sent
    best_ref[...] = top
    for s in top_copies:
        s.wait_send()


def write_kernel(gain_ref, top_ref, gain_hbm, best_ref, sem):
    write = pltpu.make_async_copy(gain_ref, gain_hbm, sem)
    write.start()
    for leaf in range(4):
        best_ref[leaf] = jnp.max(top_ref[:, 32 * leaf : 32 * (leaf + 1)])
    write.wait()


def body(bin_values, leaf_ids, treated, gradient, hessian):
    shape = (ROWS // 128, 128)
    dma = pltpu.SemaphoreType.DMA
    block = (8, 512)
    bin_values, leaf_ids, treated, gradient, hessian = (
        pltpu.with_memory_space_constraint(v, pltpu.HBM)
        for v in (bin_values, leaf_ids.reshape(shape), treated.reshape(shape), gradient.reshape(shape), hessian.reshape(shape))
    )
    gain, top = pl.pallas_call(
        kernel,
        out_shape=(jax.ShapeDtypeStruct((8, 128), F32), jax.ShapeDtypeStruct((1, 128), F32)),
        in_specs=[pl.BlockSpec(memory_space=pltpu.HBM)] * 5,
        out_specs=(pl.BlockSpec(memory_space=pltpu.VMEM),) * 2,
        scratch_shapes=[
            pltpu.VMEM((ROWS, FEATS), jnp.int32),
            pltpu.VMEM(shape, jnp.int32),
            pltpu.VMEM(shape, jnp.int32),
            pltpu.VMEM(shape, BF),
            pltpu.VMEM(shape, BF),
            pltpu.VMEM((16, ROWS), BF),
            pltpu.VMEM((4, ROWS, 128), BF),
            pltpu.VMEM((512, 128), F32),
            pltpu.VMEM((4, 2, 2, NX) + block, F32),
            pltpu.VMEM((4, 2, NX) + block, F32),
            pltpu.VMEM((4, 2, NX) + block, F32),
            pltpu.VMEM((3, NX - 1, 2) + block, F32),
            pltpu.VMEM((3, 2) + block, F32),
            pltpu.VMEM((6,) + block, F32),
            pltpu.VMEM((NX - 1,) + block, F32),
            pltpu.VMEM((NX,) + block, F32),
            pltpu.VMEM((4, 1, 128), F32),
            pltpu.VMEM((4, 7, 1, 128), F32),
            dma((8,)), dma((5,)), dma((5,)), dma((3, 3)), dma((3, 3)), dma((6,)), dma((6,)),
            dma((3,)), dma((3,)), dma((4,)), dma((4,)), dma((4, 7)), dma((4, 7)),
        ],
        compiler_params=pltpu.CompilerParams(collective_id=0, has_side_effects=True, vmem_limit_bytes=24 << 20),
    )(bin_values, leaf_ids, treated, gradient, hessian)
    vmem = pl.BlockSpec(memory_space=pltpu.VMEM)
    gain, best = pl.pallas_call(
        write_kernel,
        out_shape=(jax.ShapeDtypeStruct((8, 128), F32), jax.ShapeDtypeStruct((4,), F32)),
        in_specs=[vmem, vmem],
        out_specs=(pl.BlockSpec(memory_space=pltpu.HBM), pl.BlockSpec(memory_space=pltpu.SMEM)),
        scratch_shapes=[dma(())],
        compiler_params=pltpu.CompilerParams(vmem_limit_bytes=1 << 20),
    )(gain, top)
    return gain.reshape(4, 2, 128), best


def solution(mesh):
    in_specs = (P("row", "feat"), P("row"), P("row"), P("row"), P("row"))
    out_specs = (P(None, ("feat", "row"), None), P())
    return jax.shard_map(body, mesh=mesh, in_specs=in_specs, out_specs=out_specs, check_vma=False)
```

```python
import jax
import jax.numpy as jnp
from jax import lax
from jax.experimental import pallas as pl
from jax.experimental.pallas import tpu as pltpu
from jax.sharding import PartitionSpec as P

MESH = pl.DeviceIdType.MESH
BF = jnp.bfloat16
F32 = jnp.float32
F8 = jnp.float8_e4m3fn
ROWS = 2048
FEATS = 128
TILE = 256
TILES = ROWS // TILE
PAIRS = 8
NX, NZ, NY = 4, 8, 8


def load_stats(leaf_ref, arm_ref, grad_ref, hess_ref, stat_scr):
    stat = lax.broadcasted_iota(jnp.int32, (16, 128), 0)
    kind, leaf_of = stat // 4, stat % 4
    for c in range(ROWS // 128):
        grad = grad_ref[c : c + 1, :].astype(F32)
        hess = hess_ref[c : c + 1, :].astype(F32)
        keep = (leaf_ref[c : c + 1, :] == leaf_of) & ((arm_ref[c : c + 1, :] == 1) == (kind < 2))
        value = jnp.where(kind % 2 == 0, grad, hess)
        stat_scr[:, c * 128 : (c + 1) * 128] = jnp.where(keep, value, 0.0).astype(BF)


def lane_orders(z):
    feat = lax.broadcasted_iota(jnp.int32, (TILE, 128), 0)
    lane = lax.broadcasted_iota(jnp.int32, (TILE, 128), 1)
    owner = lane // 8
    core, u, x = owner // 8, owner // 4 % 2, owner % 4
    orders = []
    for c in range(4):
        far = lax.rem(z + jnp.where(u == 0, 4 + c, 3 - c), NZ)
        orders.append((feat == ((x * NZ + far) * 2 + core) * 2 + lane % 2).astype(F32).astype(BF))
    return [jnp.concatenate(orders[:2], axis=1), jnp.concatenate(orders[2:], axis=1)]


def spread_bins(accs, orders, loads, bins_ref, bins_scr):
    def drain(r):
        rows = slice(r * TILE, (r + 1) * TILE)
        for p in range(2):
            spread = pltpu.matmul_pop(accs[2 * (r % 2) + p]).astype(jnp.int32).astype(jnp.int8)
            bins_scr[2 * p, rows, :] = spread[:, :128]
            bins_scr[2 * p + 1, rows, :] = spread[:, 128:]

    for p in range(2):
        pltpu.matmul_push_rhs(orders[p], staging_register=0, mxu_index=p)
    for r in range(TILES):
        if r % 2 == 0:
            loads[r // 2].wait()
        block = bins_ref[r * TILE : (r + 1) * TILE, :].astype(F32).astype(BF)
        block = jnp.concatenate([block, block], axis=1)
        for p in range(2):
            pltpu.matmul_acc_lhs(accs[2 * (r % 2) + p], block, load_staged_rhs=0 if r == 0 else None)
        if r:
            drain(r - 1)
    drain(TILES - 1)


def half_chunk(accs, c, w, stat_scr, bins_scr, turn_scr):
    shape = (TILE // 32, 32, 128)
    one, zero = jnp.ones(shape, F8), jnp.zeros(shape, F8)
    group = lax.broadcasted_iota(jnp.int32, (32, 128), 1) % 8 // 2
    first = 2 * PAIRS * w
    last = [(group * 32 + (first + q)).astype(jnp.int8)[None] for q in range(2 * PAIRS)]
    for k in range(TILES):
        rows = slice(k * TILE, (k + 1) * TILE)
        bins = bins_scr[c, rows, :].reshape(shape)
        stat = stat_scr[:, rows]
        for q in range(PAIRS):
            hot = [jnp.where(bins <= last[2 * q + e], one, zero).reshape(TILE, 128) for e in range(2)]
            reg = (k * (PAIRS // 2) + q // 2) % 2
            pltpu.matmul_push_rhs(jnp.concatenate(hot, axis=1), staging_register=reg, mxu_index=q % 2)
            pltpu.matmul_acc_lhs(accs[q], stat, load_staged_rhs=reg)
    for q in range(PAIRS):
        sums = pltpu.matmul_pop(accs[q])
        for e in range(2):
            turn_scr[pl.ds(first + 2 * q + e, 16, stride=32), :] = sums[:, e * 128 : (e + 1) * 128]


def turn_chunk(c, turn_scr, hist):
    for t in range(4):
        turned = turn_scr[t * 128 : (t + 1) * 128, :].T
        hist[c, :, :, :, :, t * 128 : (t + 1) * 128] = turned.reshape(2, 2, NX, 8, 128)


def score(totals):
    grad_t, hess_t, grad_c, hess_c = (totals[8 * k : 8 * k + 8] for k in range(4))
    value_t = grad_t / (hess_t + 1.0)
    value_c = grad_c / (hess_c + 1.0)
    spread = value_t - value_c
    return grad_t * value_t + grad_c * value_c + (hess_t + hess_c) * spread * spread


def finish(block):
    left = jnp.concatenate([block[:, 128 * k : 128 * (k + 1)] for k in range(4)], axis=0)
    leaf = lax.broadcasted_iota(jnp.int32, (32, 128), 1) // 32
    sub = lax.broadcasted_iota(jnp.int32, (32, 128), 0) % 8
    last = jnp.where(sub >= 6, left, 0.0)
    last = last + jnp.where((sub >= 4) & (sub < 6), pltpu.roll(last, 30, 0), 0.0)
    last = last + jnp.where(sub < 4, pltpu.roll(last, 28, 0), 0.0)
    parent = jnp.broadcast_to(last[:, 127:128], (32, 128))
    for k in range(3):
        parent = jnp.where(leaf == k, jnp.broadcast_to(last[:, 32 * k + 31 : 32 * k + 32], (32, 128)), parent)
    gain = score(left) + score(parent - left) - score(parent)
    return gain


def store_gain(gain, gain_ref):
    lane_block = lax.broadcasted_iota(jnp.int32, (8, 128), 1) // 32
    row_block = lax.broadcasted_iota(jnp.int32, (8, 128), 0) // 2
    out = gain
    for d in range(1, 4):
        moved = pltpu.roll(pltpu.roll(gain, 32 * d, 1), 8 - 2 * d, 0)
        out = jnp.where((lane_block + 4 - row_block) % 4 == d, moved, out)
    gain_ref[...] = out


def kernel(
    bins_hbm, leaf_hbm, arm_hbm, grad_hbm, hess_hbm, gain_ref, best_ref,
    bins_ref, leaf_ref, arm_ref, grad_ref, hess_ref, stat_scr, bins_scr, turn_scr,
    hist, core_in, core_sum, x_in, x_sum, z_in, last_x, last_z, top_out, top_in,
    load_sem, core_send, core_recv, x_send, x_recv, z_send, z_recv,
    last_x_send, last_x_recv, last_z_send, last_z_recv, top_send, top_recv,
):
    feat = lax.axis_index("feat")
    row = lax.axis_index("row")
    core = lax.rem(row, 2)
    z = lax.rem(row // 2, NZ)
    x = row // (2 * NZ)

    def at(dx, dz, core_):
        return (feat, (lax.rem(x + dx, NX) * NZ + lax.rem(z + dz, NZ)) * 2 + core_)

    other = at(0, 0, 1 - core)
    x_peer = [at(d, 0, core) for d in range(NX)]
    y_peer = [(lax.rem(feat + d, NY), row) for d in range(NY)]

    pairs = [(leaf_hbm, leaf_ref), (arm_hbm, arm_ref), (grad_hbm, grad_ref), (hess_hbm, hess_ref)]
    pairs += [(bins_hbm.at[pl.ds(k * 512, 512)], bins_ref.at[pl.ds(k * 512, 512)]) for k in range(4)]
    loads = [pltpu.make_async_copy(src, dst, load_sem.at[k]) for k, (src, dst) in enumerate(pairs)]
    for load in loads:
        load.start()
    barrier = pltpu.get_barrier_semaphore()
    greeted = [other] + x_peer[1:] + [at(0, d, core) for d in range(1, NZ)] + y_peer[1:]
    greeted += [at(d, e, core) for d in range(1, NX) for e in (1, NZ - 1)]
    for peer in greeted:
        pl.semaphore_signal(barrier, inc=1, device_id=peer, device_id_type=MESH)

    for load in loads[:4]:
        load.wait()
    load_stats(leaf_ref, arm_ref, grad_ref, hess_ref, stat_scr)
    orders = lane_orders(z)
    pl.run_scoped(
        lambda *accs: spread_bins(accs, orders, loads[4:], bins_ref, bins_scr),
        *[pltpu.ACC(q % 2)((TILE, TILE), F32) for q in range(4)],
    )

    def copy(src, dst, send, recv, peer):
        return pltpu.make_async_remote_copy(
            src_ref=src, dst_ref=dst, send_sem=send, recv_sem=recv, device_id=peer, device_id_type=MESH
        )

    def core_copy(c):
        return copy(hist.at[c, 1 - core], core_in.at[c], core_send.at[c], core_recv.at[c], other)

    def last_core_copy(u):
        k = 3 + u
        return copy(hist.at[3, 1 - core, u], core_in.at[3, u], core_send.at[k], core_recv.at[k], other)

    def x_copy(c, d):
        return copy(
            core_sum.at[c, :, lax.rem(x + d, NX)], x_in.at[c, d - 1], x_send.at[c, d - 1], x_recv.at[c, d - 1], x_peer[d]
        )

    def z_copy(c, u):
        d = 3 - c if u else 4 + c
        return copy(x_sum.at[c, u], z_in.at[d - 1], z_send.at[d - 1], z_recv.at[d - 1], at(0, d, core))

    def last_x_copy(d):
        return copy(
            core_sum.at[3, 1, lax.rem(x + d, NX)], last_x.at[d - 1], last_x_send.at[d - 1], last_x_recv.at[d - 1], x_peer[d]
        )

    def last_z_copy(d):
        return copy(
            core_sum.at[3, 0, lax.rem(x + d, NX)], last_z.at[d], last_z_send.at[d], last_z_recv.at[d], at(d, NZ - 1, core)
        )

    def add_core(c):
        core_copy(c).wait_recv()
        core_sum[c] = hist[c, core] + core_in[c]

    def start_x(c):
        add_core(c)
        for d in (2, 1, 3):
            x_copy(c, d).start()

    def start_z(c):
        for d in (1, 3, 2):
            x_copy(c, d).wait_recv()
        x_sum[c] = core_sum[c, :, x] + x_in[c, 0] + x_in[c, 1] + x_in[c, 2]
        for u in range(2):
            z_copy(c, u).start()

    def all_halves(*accs):
        def step(h, carry):
            c, w = h // 2, h % 2
            half_chunk(accs, c, w, stat_scr, bins_scr, turn_scr)

            @pl.when(h == 1)
            def _():
                pl.semaphore_wait(barrier, len(greeted))

            @pl.when(w == 1)
            def _():
                turn_chunk(c, turn_scr, hist)

            @pl.when((w == 1) & (c < 3))
            def _():
                core_copy(c).start()

            @pl.when((w == 1) & (c == 3))
            def _():
                for u in range(2):
                    last_core_copy(u).start()

            @pl.when((w == 0) & (c >= 1))
            def _():
                start_x(c - 1)

            @pl.when((w == 0) & (c >= 2))
            def _():
                start_z(c - 2)

            return carry

        lax.fori_loop(0, 8, step, 0)

    pl.run_scoped(all_halves, *[pltpu.ACC(q % 2)((16, TILE), F32) for q in range(PAIRS)])

    for u in range(2):
        last_core_copy(u).wait_recv()
        core_sum[3, u] = hist[3, core, u] + core_in[3, u]
        for d in (2, 1, 3, 0):
            if u == 0:
                last_z_copy(d).start()
            elif d:
                last_x_copy(d).start()
    start_z(2)
    block = core_sum[3, 1, x]
    for c in range(2):
        for u in range(2):
            z_copy(c, u).wait_recv()
            block = block + z_in[2 - c if u else 3 + c]
    for d in range(NX):
        last_z_copy(d).wait_recv()
        block = block + last_z[d]
        if d:
            last_x_copy(d).wait_recv()
            block = block + last_x[d - 1]
    for u in range(2):
        z_copy(2, u).wait_recv()
        block = block + z_in[0 if u else 5]

    gain = finish(block)
    top = jnp.max(gain, axis=0, keepdims=True)

    def wait_sends():
        for u in range(2):
            last_core_copy(u).wait_send()
        for c in range(3):
            core_copy(c).wait_send()
            for d in range(1, NX):
                x_copy(c, d).wait_send()
            for u in range(2):
                z_copy(c, u).wait_send()
        for d in range(NX):
            last_z_copy(d).wait_send()
            if d:
                last_x_copy(d).wait_send()

    near_last = (4, 3, 5, 2, 6, 1, 7)
    rounds = (
        [other],
        [x_peer[d] for d in (2, 1, 3)],
        [at(0, d, core) for d in near_last],
        [y_peer[d] for d in near_last],
    )
    top_copies = []
    for stage, peers in enumerate(rounds):
        top_out[stage] = top
        sent = []
        for k, peer in enumerate(peers):
            s = copy(top_out.at[stage], top_in.at[stage, k], top_send.at[stage, k], top_recv.at[stage, k], peer)
            s.start()
            sent.append(s)
        if stage == 0:
            store_gain(gain, gain_ref)
        if stage == 2:
            wait_sends()
        if stage:
            for s in top_copies:
                s.wait_send()
            top_copies = []
        for s in reversed(sent):
            s.wait_recv()
        for k in range(len(sent)):
            top = jnp.maximum(top, top_in[stage, k])
        top_copies += sent
    best_ref[...] = top
    for s in top_copies:
        s.wait_send()


def write_kernel(gain_ref, top_ref, gain_hbm, best_ref, sem):
    write = pltpu.make_async_copy(gain_ref, gain_hbm, sem)
    write.start()
    for leaf in range(4):
        best_ref[leaf] = jnp.max(top_ref[:, 32 * leaf : 32 * (leaf + 1)])
    write.wait()


def body(bin_values, leaf_ids, treated, gradient, hessian):
    shape = (ROWS // 128, 128)
    dma = pltpu.SemaphoreType.DMA
    block = (8, 512)
    bin_values, leaf_ids, treated, gradient, hessian = (
        pltpu.with_memory_space_constraint(v, pltpu.HBM)
        for v in (bin_values, leaf_ids.reshape(shape), treated.reshape(shape), gradient.reshape(shape), hessian.reshape(shape))
    )
    gain, top = pl.pallas_call(
        kernel,
        out_shape=(jax.ShapeDtypeStruct((8, 128), F32), jax.ShapeDtypeStruct((1, 128), F32)),
        in_specs=[pl.BlockSpec(memory_space=pltpu.HBM)] * 5,
        out_specs=(pl.BlockSpec(memory_space=pltpu.VMEM),) * 2,
        scratch_shapes=[
            pltpu.VMEM((ROWS, FEATS), jnp.int32),
            pltpu.VMEM(shape, jnp.int32),
            pltpu.VMEM(shape, jnp.int32),
            pltpu.VMEM(shape, BF),
            pltpu.VMEM(shape, BF),
            pltpu.VMEM((16, ROWS), BF),
            pltpu.VMEM((4, ROWS, 128), jnp.int8),
            pltpu.VMEM((512, 128), F32),
            pltpu.VMEM((4, 2, 2, NX) + block, F32),
            pltpu.VMEM((4, 2, NX) + block, F32),
            pltpu.VMEM((4, 2, NX) + block, F32),
            pltpu.VMEM((3, NX - 1, 2) + block, F32),
            pltpu.VMEM((3, 2) + block, F32),
            pltpu.VMEM((6,) + block, F32),
            pltpu.VMEM((NX - 1,) + block, F32),
            pltpu.VMEM((NX,) + block, F32),
            pltpu.VMEM((4, 1, 128), F32),
            pltpu.VMEM((4, 7, 1, 128), F32),
            dma((8,)), dma((5,)), dma((5,)), dma((3, 3)), dma((3, 3)), dma((6,)), dma((6,)),
            dma((3,)), dma((3,)), dma((4,)), dma((4,)), dma((4, 7)), dma((4, 7)),
        ],
        compiler_params=pltpu.CompilerParams(collective_id=0, has_side_effects=True, vmem_limit_bytes=24 << 20),
    )(bin_values, leaf_ids, treated, gradient, hessian)
    vmem = pl.BlockSpec(memory_space=pltpu.VMEM)
    gain, best = pl.pallas_call(
        write_kernel,
        out_shape=(jax.ShapeDtypeStruct((8, 128), F32), jax.ShapeDtypeStruct((4,), F32)),
        in_specs=[vmem, vmem],
        out_specs=(pl.BlockSpec(memory_space=pltpu.HBM), pl.BlockSpec(memory_space=pltpu.SMEM)),
        scratch_shapes=[dma(())],
        compiler_params=pltpu.CompilerParams(vmem_limit_bytes=1 << 20),
    )(gain, top)
    return gain.reshape(4, 2, 128), best


def solution(mesh):
    in_specs = (P("row", "feat"), P("row"), P("row"), P("row"), P("row"))
    out_specs = (P(None, ("feat", "row"), None), P())
    return jax.shard_map(body, mesh=mesh, in_specs=in_specs, out_specs=out_specs, check_vma=False)
```

```python
import jax
import jax.numpy as jnp
from jax import lax
from jax.experimental import pallas as pl
from jax.experimental.pallas import tpu as pltpu
from jax.sharding import PartitionSpec as P

MESH = pl.DeviceIdType.MESH
BF = jnp.bfloat16
F32 = jnp.float32
F8 = jnp.float8_e4m3fn
ROWS = 2048
FEATS = 128
TILE = 256
TILES = ROWS // TILE
PAIRS = 8
NX, NZ, NY = 4, 8, 8


def load_stats(leaf_ref, arm_ref, grad_ref, hess_ref, stat_scr):
    stat = lax.broadcasted_iota(jnp.int32, (16, 128), 0)
    kind, leaf_of = stat // 4, stat % 4
    for c in range(ROWS // 128):
        grad = grad_ref[c : c + 1, :].astype(F32)
        hess = hess_ref[c : c + 1, :].astype(F32)
        keep = (leaf_ref[c : c + 1, :] == leaf_of) & ((arm_ref[c : c + 1, :] == 1) == (kind < 2))
        value = jnp.where(kind % 2 == 0, grad, hess)
        stat_scr[:, c * 128 : (c + 1) * 128] = jnp.where(keep, value, 0.0).astype(BF)


def lane_orders(z):
    feat = lax.broadcasted_iota(jnp.int32, (TILE, 128), 0)
    lane = lax.broadcasted_iota(jnp.int32, (TILE, 128), 1)
    owner = lane // 8
    core, u, x = owner // 8, owner // 4 % 2, owner % 4
    orders = []
    for c in range(4):
        far = lax.rem(z + jnp.where(u == 0, 4 + c, 3 - c), NZ)
        orders.append((feat == ((x * NZ + far) * 2 + core) * 2 + lane % 2).astype(F32).astype(BF))
    return [jnp.concatenate(orders[:2], axis=1), jnp.concatenate(orders[2:], axis=1)]


def spread_bins(accs, orders, loads, bins_ref, bins_scr):
    def drain(r):
        rows = slice(r * TILE, (r + 1) * TILE)
        for p in range(2):
            spread = pltpu.matmul_pop(accs[2 * (r % 2) + p]).astype(jnp.int32).astype(jnp.int8)
            bins_scr[2 * p, rows, :] = spread[:, :128]
            bins_scr[2 * p + 1, rows, :] = spread[:, 128:]

    for p in range(2):
        pltpu.matmul_push_rhs(orders[p], staging_register=0, mxu_index=p)
    for r in range(TILES):
        if r % 2 == 0:
            loads[r // 2].wait()
        block = bins_ref[r * TILE : (r + 1) * TILE, :].astype(F32).astype(BF)
        block = jnp.concatenate([block, block], axis=1)
        for p in range(2):
            pltpu.matmul_acc_lhs(accs[2 * (r % 2) + p], block, load_staged_rhs=0 if r == 0 else None)
        if r:
            drain(r - 1)
    drain(TILES - 1)


def half_chunk(accs, c, w, stat_scr, bins_scr, turn_scr):
    shape = (TILE // 32, 32, 128)
    one, zero = jnp.ones(shape, F8), jnp.zeros(shape, F8)
    group = lax.broadcasted_iota(jnp.int32, (32, 128), 1) % 8 // 2
    first = 2 * PAIRS * w
    last = [(group * 32 + (first + q)).astype(jnp.int8)[None] for q in range(2 * PAIRS)]
    for k in range(TILES):
        rows = slice(k * TILE, (k + 1) * TILE)
        bins = bins_scr[c, rows, :].reshape(shape)
        stat = stat_scr[:, rows]
        for q in range(PAIRS):
            hot = [jnp.where(bins <= last[2 * q + e], one, zero).reshape(TILE, 128) for e in range(2)]
            reg = (k * (PAIRS // 2) + q // 2) % 2
            pltpu.matmul_push_rhs(jnp.concatenate(hot, axis=1), staging_register=reg, mxu_index=q % 2)
            pltpu.matmul_acc_lhs(accs[q], stat, load_staged_rhs=reg)
    for q in range(PAIRS):
        sums = pltpu.matmul_pop(accs[q])
        for e in range(2):
            turn_scr[pl.ds(first + 2 * q + e, 16, stride=32), :] = sums[:, e * 128 : (e + 1) * 128]


def turn_chunk(c, turn_scr, hist):
    for t in range(4):
        turned = turn_scr[t * 128 : (t + 1) * 128, :].T
        hist[c, :, :, :, :, t * 128 : (t + 1) * 128] = turned.reshape(2, 2, NX, 8, 128)


def score(totals):
    grad_t, hess_t, grad_c, hess_c = (totals[8 * k : 8 * k + 8] for k in range(4))
    value_t = grad_t / (hess_t + 1.0)
    value_c = grad_c / (hess_c + 1.0)
    spread = value_t - value_c
    return grad_t * value_t + grad_c * value_c + (hess_t + hess_c) * spread * spread


def finish(block):
    left = jnp.concatenate([block[:, 128 * k : 128 * (k + 1)] for k in range(4)], axis=0)
    leaf = lax.broadcasted_iota(jnp.int32, (32, 128), 1) // 32
    sub = lax.broadcasted_iota(jnp.int32, (32, 128), 0) % 8
    last = jnp.where(sub >= 6, left, 0.0)
    last = last + jnp.where((sub >= 4) & (sub < 6), pltpu.roll(last, 30, 0), 0.0)
    last = last + jnp.where(sub < 4, pltpu.roll(last, 28, 0), 0.0)
    parent = jnp.broadcast_to(last[:, 127:128], (32, 128))
    for k in range(3):
        parent = jnp.where(leaf == k, jnp.broadcast_to(last[:, 32 * k + 31 : 32 * k + 32], (32, 128)), parent)
    gain = score(left) + score(parent - left) - score(parent)
    return gain


def store_gain(gain, gain_ref):
    lane_block = lax.broadcasted_iota(jnp.int32, (8, 128), 1) // 32
    row_block = lax.broadcasted_iota(jnp.int32, (8, 128), 0) // 2
    out = gain
    for d in range(1, 4):
        moved = pltpu.roll(pltpu.roll(gain, 32 * d, 1), 8 - 2 * d, 0)
        out = jnp.where((lane_block + 4 - row_block) % 4 == d, moved, out)
    gain_ref[...] = out


def kernel(
    bins_hbm, leaf_hbm, arm_hbm, grad_hbm, hess_hbm, gain_ref, best_ref,
    bins_ref, leaf_ref, arm_ref, grad_ref, hess_ref, stat_scr, bins_scr, turn_scr,
    hist, core_in, core_sum, x_in, x_sum, z_in, last_x, last_z, top_out, top_in,
    load_sem, core_send, core_recv, x_send, x_recv, z_send, z_recv,
    last_x_send, last_x_recv, last_z_send, last_z_recv, top_send, top_recv,
):
    feat = lax.axis_index("feat")
    row = lax.axis_index("row")
    core = lax.rem(row, 2)
    z = lax.rem(row // 2, NZ)
    x = row // (2 * NZ)

    def at(dx, dz, core_):
        return (feat, (lax.rem(x + dx, NX) * NZ + lax.rem(z + dz, NZ)) * 2 + core_)

    other = at(0, 0, 1 - core)
    x_peer = [at(d, 0, core) for d in range(NX)]
    y_peer = [(lax.rem(feat + d, NY), row) for d in range(NY)]

    pairs = [(leaf_hbm, leaf_ref), (arm_hbm, arm_ref), (grad_hbm, grad_ref), (hess_hbm, hess_ref)]
    pairs += [(bins_hbm.at[pl.ds(k * 512, 512)], bins_ref.at[pl.ds(k * 512, 512)]) for k in range(4)]
    loads = [pltpu.make_async_copy(src, dst, load_sem.at[k]) for k, (src, dst) in enumerate(pairs)]
    for load in loads:
        load.start()
    barrier = pltpu.get_barrier_semaphore()
    greeted = [other] + x_peer[1:] + [at(0, d, core) for d in range(1, NZ)] + y_peer[1:]
    greeted += [at(d, e, core) for d in range(1, NX) for e in (1, NZ - 1)]
    for peer in greeted:
        pl.semaphore_signal(barrier, inc=1, device_id=peer, device_id_type=MESH)

    for load in loads[:4]:
        load.wait()
    load_stats(leaf_ref, arm_ref, grad_ref, hess_ref, stat_scr)
    orders = lane_orders(z)
    pl.run_scoped(
        lambda *accs: spread_bins(accs, orders, loads[4:], bins_ref, bins_scr),
        *[pltpu.ACC(q % 2)((TILE, TILE), F32) for q in range(4)],
    )

    def copy(src, dst, send, recv, peer):
        return pltpu.make_async_remote_copy(
            src_ref=src, dst_ref=dst, send_sem=send, recv_sem=recv, device_id=peer, device_id_type=MESH
        )

    def core_copy(c):
        return copy(hist.at[c, 1 - core], core_in.at[c], core_send.at[c], core_recv.at[c], other)

    def last_core_copy(u):
        k = 3 + u
        return copy(hist.at[3, 1 - core, u], core_in.at[3, u], core_send.at[k], core_recv.at[k], other)

    def x_copy(c, d):
        return copy(
            core_sum.at[c, :, lax.rem(x + d, NX)], x_in.at[c, d - 1], x_send.at[c, d - 1], x_recv.at[c, d - 1], x_peer[d]
        )

    def z_copy(c, u):
        d = 3 - c if u else 4 + c
        return copy(x_sum.at[c, u], z_in.at[d - 1], z_send.at[d - 1], z_recv.at[d - 1], at(0, d, core))

    def last_x_copy(d):
        return copy(
            core_sum.at[3, 1, lax.rem(x + d, NX)], last_x.at[d - 1], last_x_send.at[d - 1], last_x_recv.at[d - 1], x_peer[d]
        )

    def last_z_copy(d):
        return copy(
            core_sum.at[3, 0, lax.rem(x + d, NX)], last_z.at[d], last_z_send.at[d], last_z_recv.at[d], at(d, NZ - 1, core)
        )

    def add_core(c):
        core_copy(c).wait_recv()
        core_sum[c] = hist[c, core] + core_in[c]

    def start_x(c):
        add_core(c)
        for d in (2, 1, 3):
            x_copy(c, d).start()

    def start_z(c):
        for d in (1, 3, 2):
            x_copy(c, d).wait_recv()
        x_sum[c] = core_sum[c, :, x] + x_in[c, 0] + x_in[c, 1] + x_in[c, 2]
        for u in range(2):
            z_copy(c, u).start()

    def all_halves(*accs):
        def step(h, carry):
            c, w = h // 2, h % 2
            half_chunk(accs, c, w, stat_scr, bins_scr, turn_scr)

            @pl.when(h == 1)
            def _():
                pl.semaphore_wait(barrier, len(greeted))

            @pl.when(w == 1)
            def _():
                turn_chunk(c, turn_scr, hist)

            @pl.when((w == 1) & (c < 3))
            def _():
                core_copy(c).start()

            @pl.when((w == 1) & (c == 3))
            def _():
                for u in range(2):
                    last_core_copy(u).start()

            @pl.when(((w == 1) & (c >= 1) & (c < 3)) | (h == 6))
            def _():
                start_x(c - 1)

            return carry

        lax.fori_loop(0, 8, step, 0)

    pl.run_scoped(all_halves, *[pltpu.ACC(q % 2)((16, TILE), F32) for q in range(PAIRS)])

    for u in range(2):
        last_core_copy(u).wait_recv()
        core_sum[3, u] = hist[3, core, u] + core_in[3, u]
        for d in (2, 1, 3, 0):
            if u == 0:
                last_z_copy(d).start()
            elif d:
                last_x_copy(d).start()
    for c in range(3):
        start_z(c)
    block = core_sum[3, 1, x]
    for c in range(2):
        for u in range(2):
            z_copy(c, u).wait_recv()
            block = block + z_in[2 - c if u else 3 + c]
    for d in range(NX):
        last_z_copy(d).wait_recv()
        block = block + last_z[d]
        if d:
            last_x_copy(d).wait_recv()
            block = block + last_x[d - 1]
    for u in range(2):
        z_copy(2, u).wait_recv()
        block = block + z_in[0 if u else 5]

    gain = finish(block)
    top = jnp.max(gain, axis=0, keepdims=True)

    def wait_sends():
        for u in range(2):
            last_core_copy(u).wait_send()
        for c in range(3):
            core_copy(c).wait_send()
            for d in range(1, NX):
                x_copy(c, d).wait_send()
            for u in range(2):
                z_copy(c, u).wait_send()
        for d in range(NX):
            last_z_copy(d).wait_send()
            if d:
                last_x_copy(d).wait_send()

    near_last = (4, 3, 5, 2, 6, 1, 7)
    rounds = (
        [other],
        [x_peer[d] for d in (2, 1, 3)],
        [at(0, d, core) for d in near_last],
        [y_peer[d] for d in near_last],
    )
    top_copies = []
    for stage, peers in enumerate(rounds):
        top_out[stage] = top
        sent = []
        for k, peer in enumerate(peers):
            s = copy(top_out.at[stage], top_in.at[stage, k], top_send.at[stage, k], top_recv.at[stage, k], peer)
            s.start()
            sent.append(s)
        if stage == 0:
            store_gain(gain, gain_ref)
        if stage == 2:
            wait_sends()
        if stage:
            for s in top_copies:
                s.wait_send()
            top_copies = []
        for s in reversed(sent):
            s.wait_recv()
        for k in range(len(sent)):
            top = jnp.maximum(top, top_in[stage, k])
        top_copies += sent
    best_ref[...] = top
    for s in top_copies:
        s.wait_send()


def write_kernel(gain_ref, top_ref, gain_hbm, best_ref, sem):
    write = pltpu.make_async_copy(gain_ref, gain_hbm, sem)
    write.start()
    for leaf in range(4):
        best_ref[leaf] = jnp.max(top_ref[:, 32 * leaf : 32 * (leaf + 1)])
    write.wait()


def body(bin_values, leaf_ids, treated, gradient, hessian):
    shape = (ROWS // 128, 128)
    dma = pltpu.SemaphoreType.DMA
    block = (8, 512)
    bin_values, leaf_ids, treated, gradient, hessian = (
        pltpu.with_memory_space_constraint(v, pltpu.HBM)
        for v in (bin_values, leaf_ids.reshape(shape), treated.reshape(shape), gradient.reshape(shape), hessian.reshape(shape))
    )
    gain, top = pl.pallas_call(
        kernel,
        out_shape=(jax.ShapeDtypeStruct((8, 128), F32), jax.ShapeDtypeStruct((1, 128), F32)),
        in_specs=[pl.BlockSpec(memory_space=pltpu.HBM)] * 5,
        out_specs=(pl.BlockSpec(memory_space=pltpu.VMEM),) * 2,
        scratch_shapes=[
            pltpu.VMEM((ROWS, FEATS), jnp.int32),
            pltpu.VMEM(shape, jnp.int32),
            pltpu.VMEM(shape, jnp.int32),
            pltpu.VMEM(shape, BF),
            pltpu.VMEM(shape, BF),
            pltpu.VMEM((16, ROWS), BF),
            pltpu.VMEM((4, ROWS, 128), jnp.int8),
            pltpu.VMEM((512, 128), F32),
            pltpu.VMEM((4, 2, 2, NX) + block, F32),
            pltpu.VMEM((4, 2, NX) + block, F32),
            pltpu.VMEM((4, 2, NX) + block, F32),
            pltpu.VMEM((3, NX - 1, 2) + block, F32),
            pltpu.VMEM((3, 2) + block, F32),
            pltpu.VMEM((6,) + block, F32),
            pltpu.VMEM((NX - 1,) + block, F32),
            pltpu.VMEM((NX,) + block, F32),
            pltpu.VMEM((4, 1, 128), F32),
            pltpu.VMEM((4, 7, 1, 128), F32),
            dma((8,)), dma((5,)), dma((5,)), dma((3, 3)), dma((3, 3)), dma((6,)), dma((6,)),
            dma((3,)), dma((3,)), dma((4,)), dma((4,)), dma((4, 7)), dma((4, 7)),
        ],
        compiler_params=pltpu.CompilerParams(collective_id=0, has_side_effects=True, vmem_limit_bytes=24 << 20),
    )(bin_values, leaf_ids, treated, gradient, hessian)
    vmem = pl.BlockSpec(memory_space=pltpu.VMEM)
    gain, best = pl.pallas_call(
        write_kernel,
        out_shape=(jax.ShapeDtypeStruct((8, 128), F32), jax.ShapeDtypeStruct((4,), F32)),
        in_specs=[vmem, vmem],
        out_specs=(pl.BlockSpec(memory_space=pltpu.HBM), pl.BlockSpec(memory_space=pltpu.SMEM)),
        scratch_shapes=[dma(())],
        compiler_params=pltpu.CompilerParams(vmem_limit_bytes=1 << 20),
    )(gain, top)
    return gain.reshape(4, 2, 128), best


def solution(mesh):
    in_specs = (P("row", "feat"), P("row"), P("row"), P("row"), P("row"))
    out_specs = (P(None, ("feat", "row"), None), P())
    return jax.shard_map(body, mesh=mesh, in_specs=in_specs, out_specs=out_specs, check_vma=False)
```

```python
import jax
import jax.numpy as jnp
from jax import lax
from jax.experimental import pallas as pl
from jax.experimental.pallas import tpu as pltpu
from jax.sharding import PartitionSpec as P

MESH = pl.DeviceIdType.MESH
BF = jnp.bfloat16
F32 = jnp.float32
F8 = jnp.float8_e4m3fn
ROWS = 2048
FEATS = 128
TILE = 256
TILES = ROWS // TILE
PAIRS = 8
NX, NZ, NY = 4, 8, 8


def load_stats(leaf_ref, arm_ref, grad_ref, hess_ref, stat_scr):
    stat = lax.broadcasted_iota(jnp.int32, (16, 128), 0)
    kind, leaf_of = stat // 4, stat % 4
    for c in range(ROWS // 128):
        grad = grad_ref[c : c + 1, :].astype(F32)
        hess = hess_ref[c : c + 1, :].astype(F32)
        keep = (leaf_ref[c : c + 1, :] == leaf_of) & ((arm_ref[c : c + 1, :] == 1) == (kind < 2))
        value = jnp.where(kind % 2 == 0, grad, hess)
        stat_scr[:, c * 128 : (c + 1) * 128] = jnp.where(keep, value, 0.0).astype(BF)


def lane_orders(z):
    feat = lax.broadcasted_iota(jnp.int32, (TILE, 128), 0)
    lane = lax.broadcasted_iota(jnp.int32, (TILE, 128), 1)
    owner = lane // 8
    core, u, x = owner // 8, owner // 4 % 2, owner % 4
    orders = []
    for c in range(4):
        far = lax.rem(z + jnp.where(u == 0, 4 + c, 3 - c), NZ)
        orders.append((feat == ((x * NZ + far) * 2 + core) * 2 + lane % 2).astype(F32).astype(BF))
    return [jnp.concatenate(orders[:2], axis=1), jnp.concatenate(orders[2:], axis=1)]


def spread_bins(accs, orders, loads, bins_ref, bins_scr):
    def drain(r):
        rows = slice(r * TILE, (r + 1) * TILE)
        for p in range(2):
            spread = pltpu.matmul_pop(accs[2 * (r % 2) + p]).astype(jnp.int32).astype(jnp.int8)
            bins_scr[2 * p, rows, :] = spread[:, :128]
            bins_scr[2 * p + 1, rows, :] = spread[:, 128:]

    for p in range(2):
        pltpu.matmul_push_rhs(orders[p], staging_register=0, mxu_index=p)
    for r in range(TILES):
        if r % 2 == 0:
            loads[r // 2].wait()
        block = bins_ref[r * TILE : (r + 1) * TILE, :].astype(F32).astype(BF)
        block = jnp.concatenate([block, block], axis=1)
        for p in range(2):
            pltpu.matmul_acc_lhs(accs[2 * (r % 2) + p], block, load_staged_rhs=0 if r == 0 else None)
        if r:
            drain(r - 1)
    drain(TILES - 1)


def half_chunk(accs, c, w, stat_scr, bins_scr, turn_scr):
    shape = (TILE // 32, 32, 128)
    one, zero = jnp.ones(shape, F8), jnp.zeros(shape, F8)
    group = lax.broadcasted_iota(jnp.int32, (32, 128), 1) % 8 // 2
    first = 2 * PAIRS * w
    last = [(group * 32 + (first + q)).astype(jnp.int8)[None] for q in range(2 * PAIRS)]
    for k in range(TILES):
        rows = slice(k * TILE, (k + 1) * TILE)
        bins = bins_scr[c, rows, :].reshape(shape)
        stat = stat_scr[:, rows]
        for q in range(PAIRS):
            hot = [jnp.where(bins <= last[2 * q + e], one, zero).reshape(TILE, 128) for e in range(2)]
            reg = (k * (PAIRS // 2) + q // 2) % 2
            pltpu.matmul_push_rhs(jnp.concatenate(hot, axis=1), staging_register=reg, mxu_index=q % 2)
            pltpu.matmul_acc_lhs(accs[q], stat, load_staged_rhs=reg)
    for q in range(PAIRS):
        sums = pltpu.matmul_pop(accs[q])
        for e in range(2):
            turn_scr[pl.ds(first + 2 * q + e, 16, stride=32), :] = sums[:, e * 128 : (e + 1) * 128]


def turn_chunk(c, turn_scr, hist):
    for t in range(4):
        turned = turn_scr[t * 128 : (t + 1) * 128, :].T
        hist[c, :, :, :, :, t * 128 : (t + 1) * 128] = turned.reshape(2, 2, NX, 8, 128)


def score(totals):
    grad_t, hess_t, grad_c, hess_c = (totals[8 * k : 8 * k + 8] for k in range(4))
    value_t = grad_t / (hess_t + 1.0)
    value_c = grad_c / (hess_c + 1.0)
    spread = value_t - value_c
    return grad_t * value_t + grad_c * value_c + (hess_t + hess_c) * spread * spread


def finish(block):
    left = jnp.concatenate([block[:, 128 * k : 128 * (k + 1)] for k in range(4)], axis=0)
    leaf = lax.broadcasted_iota(jnp.int32, (32, 128), 1) // 32
    sub = lax.broadcasted_iota(jnp.int32, (32, 128), 0) % 8
    last = jnp.where(sub >= 6, left, 0.0)
    last = last + jnp.where((sub >= 4) & (sub < 6), pltpu.roll(last, 30, 0), 0.0)
    last = last + jnp.where(sub < 4, pltpu.roll(last, 28, 0), 0.0)
    parent = jnp.broadcast_to(last[:, 127:128], (32, 128))
    for k in range(3):
        parent = jnp.where(leaf == k, jnp.broadcast_to(last[:, 32 * k + 31 : 32 * k + 32], (32, 128)), parent)
    gain = score(left) + score(parent - left) - score(parent)
    return gain


def store_gain(gain, gain_ref):
    lane_block = lax.broadcasted_iota(jnp.int32, (8, 128), 1) // 32
    row_block = lax.broadcasted_iota(jnp.int32, (8, 128), 0) // 2
    out = gain
    for d in range(1, 4):
        moved = pltpu.roll(pltpu.roll(gain, 32 * d, 1), 8 - 2 * d, 0)
        out = jnp.where((lane_block + 4 - row_block) % 4 == d, moved, out)
    gain_ref[...] = out


def kernel(
    bins_hbm, leaf_hbm, arm_hbm, grad_hbm, hess_hbm, gain_ref, best_ref,
    bins_ref, leaf_ref, arm_ref, grad_ref, hess_ref, stat_scr, bins_scr, turn_scr,
    hist, core_in, core_sum, x_in, x_sum, z_in, last_x, last_z, top_out, top_in,
    load_sem, core_send, core_recv, x_send, x_recv, z_send, z_recv,
    last_x_send, last_x_recv, last_z_send, last_z_recv, top_send, top_recv,
):
    feat = lax.axis_index("feat")
    row = lax.axis_index("row")
    core = lax.rem(row, 2)
    z = lax.rem(row // 2, NZ)
    x = row // (2 * NZ)

    def at(dx, dz, core_):
        return (feat, (lax.rem(x + dx, NX) * NZ + lax.rem(z + dz, NZ)) * 2 + core_)

    other = at(0, 0, 1 - core)
    x_peer = [at(d, 0, core) for d in range(NX)]
    y_peer = [(lax.rem(feat + d, NY), row) for d in range(NY)]

    pairs = [(leaf_hbm, leaf_ref), (arm_hbm, arm_ref), (grad_hbm, grad_ref), (hess_hbm, hess_ref)]
    pairs += [(bins_hbm.at[pl.ds(k * 512, 512)], bins_ref.at[pl.ds(k * 512, 512)]) for k in range(4)]
    loads = [pltpu.make_async_copy(src, dst, load_sem.at[k]) for k, (src, dst) in enumerate(pairs)]
    for load in loads:
        load.start()
    barrier = pltpu.get_barrier_semaphore()
    far = (4, 3, 5, 2, 6, 1, 7)
    greeted = [at(0, d, core) for d in far] + [y_peer[d] for d in far]
    greeted += [at(d, e, core) for d in (2, 1, 3) for e in (1, NZ - 1, 0)] + [other]
    for peer in greeted:
        pl.semaphore_signal(barrier, inc=1, device_id=peer, device_id_type=MESH)

    for load in loads[:4]:
        load.wait()
    load_stats(leaf_ref, arm_ref, grad_ref, hess_ref, stat_scr)
    orders = lane_orders(z)
    pl.run_scoped(
        lambda *accs: spread_bins(accs, orders, loads[4:], bins_ref, bins_scr),
        *[pltpu.ACC(q % 2)((TILE, TILE), F32) for q in range(4)],
    )

    def copy(src, dst, send, recv, peer):
        return pltpu.make_async_remote_copy(
            src_ref=src, dst_ref=dst, send_sem=send, recv_sem=recv, device_id=peer, device_id_type=MESH
        )

    def core_copy(c):
        return copy(hist.at[c, 1 - core], core_in.at[c], core_send.at[c], core_recv.at[c], other)

    def last_core_copy(u):
        k = 3 + u
        return copy(hist.at[3, 1 - core, u], core_in.at[3, u], core_send.at[k], core_recv.at[k], other)

    def x_copy(c, d):
        return copy(
            core_sum.at[c, :, lax.rem(x + d, NX)], x_in.at[c, d - 1], x_send.at[c, d - 1], x_recv.at[c, d - 1], x_peer[d]
        )

    def z_copy(c, u):
        d = 3 - c if u else 4 + c
        return copy(x_sum.at[c, u], z_in.at[d - 1], z_send.at[d - 1], z_recv.at[d - 1], at(0, d, core))

    def last_x_copy(d):
        return copy(
            core_sum.at[3, 1, lax.rem(x + d, NX)], last_x.at[d - 1], last_x_send.at[d - 1], last_x_recv.at[d - 1], x_peer[d]
        )

    def last_z_copy(d):
        return copy(
            core_sum.at[3, 0, lax.rem(x + d, NX)], last_z.at[d], last_z_send.at[d], last_z_recv.at[d], at(d, NZ - 1, core)
        )

    def add_core(c):
        core_copy(c).wait_recv()
        core_sum[c] = hist[c, core] + core_in[c]

    def start_x(c):
        add_core(c)
        for d in (2, 1, 3):
            x_copy(c, d).start()

    def start_z(c):
        for d in (1, 3, 2):
            x_copy(c, d).wait_recv()
        x_sum[c] = core_sum[c, :, x] + x_in[c, 0] + x_in[c, 1] + x_in[c, 2]
        for u in range(2):
            z_copy(c, u).start()

    def all_halves(*accs):
        def step(h, carry):
            c, w = h // 2, h % 2
            half_chunk(accs, c, w, stat_scr, bins_scr, turn_scr)

            @pl.when(w == 1)
            def _():
                turn_chunk(c, turn_scr, hist)

            @pl.when(h == 2)
            def _():
                pl.semaphore_wait(barrier, len(greeted))
                core_copy(0).start()

            @pl.when((h == 3) | (h == 5))
            def _():
                core_copy(c).start()

            @pl.when(h == 7)
            def _():
                for u in range(2):
                    last_core_copy(u).start()

            @pl.when((h == 4) | (h == 5) | (h == 6))
            def _():
                start_x(h - 4)

            return carry

        lax.fori_loop(0, 8, step, 0)

    pl.run_scoped(all_halves, *[pltpu.ACC(q % 2)((16, TILE), F32) for q in range(PAIRS)])

    for u in range(2):
        last_core_copy(u).wait_recv()
        core_sum[3, u] = hist[3, core, u] + core_in[3, u]
        for d in (2, 1, 3, 0):
            if u == 0:
                last_z_copy(d).start()
            elif d:
                last_x_copy(d).start()
    for c in range(3):
        start_z(c)
    block = core_sum[3, 1, x]
    for c in range(2):
        for u in range(2):
            z_copy(c, u).wait_recv()
            block = block + z_in[2 - c if u else 3 + c]
    for d in range(NX):
        last_z_copy(d).wait_recv()
        block = block + last_z[d]
        if d:
            last_x_copy(d).wait_recv()
            block = block + last_x[d - 1]
    for u in range(2):
        z_copy(2, u).wait_recv()
        block = block + z_in[0 if u else 5]

    gain = finish(block)
    top = jnp.max(gain, axis=0, keepdims=True)

    def wait_sends():
        for u in range(2):
            last_core_copy(u).wait_send()
        for c in range(3):
            core_copy(c).wait_send()
            for d in range(1, NX):
                x_copy(c, d).wait_send()
            for u in range(2):
                z_copy(c, u).wait_send()
        for d in range(NX):
            last_z_copy(d).wait_send()
            if d:
                last_x_copy(d).wait_send()

    rounds = (
        [other],
        [x_peer[d] for d in (2, 1, 3)],
        [at(0, d, core) for d in far],
        [y_peer[d] for d in far],
    )
    top_copies = []
    for stage, peers in enumerate(rounds):
        top_out[stage] = top
        sent = []
        for k, peer in enumerate(peers):
            s = copy(top_out.at[stage], top_in.at[stage, k], top_send.at[stage, k], top_recv.at[stage, k], peer)
            s.start()
            sent.append(s)
        if stage == 0:
            store_gain(gain, gain_ref)
        if stage == 2:
            wait_sends()
        if stage:
            for s in top_copies:
                s.wait_send()
            top_copies = []
        for s in reversed(sent):
            s.wait_recv()
        for k in range(len(sent)):
            top = jnp.maximum(top, top_in[stage, k])
        top_copies += sent
    best_ref[...] = top
    for s in top_copies:
        s.wait_send()


def write_kernel(gain_ref, top_ref, gain_hbm, best_ref, sem):
    write = pltpu.make_async_copy(gain_ref, gain_hbm, sem)
    write.start()
    for leaf in range(4):
        best_ref[leaf] = jnp.max(top_ref[:, 32 * leaf : 32 * (leaf + 1)])
    write.wait()


def body(bin_values, leaf_ids, treated, gradient, hessian):
    shape = (ROWS // 128, 128)
    dma = pltpu.SemaphoreType.DMA
    block = (8, 512)
    bin_values, leaf_ids, treated, gradient, hessian = (
        pltpu.with_memory_space_constraint(v, pltpu.HBM)
        for v in (bin_values, leaf_ids.reshape(shape), treated.reshape(shape), gradient.reshape(shape), hessian.reshape(shape))
    )
    gain, top = pl.pallas_call(
        kernel,
        out_shape=(jax.ShapeDtypeStruct((8, 128), F32), jax.ShapeDtypeStruct((1, 128), F32)),
        in_specs=[pl.BlockSpec(memory_space=pltpu.HBM)] * 5,
        out_specs=(pl.BlockSpec(memory_space=pltpu.VMEM),) * 2,
        scratch_shapes=[
            pltpu.VMEM((ROWS, FEATS), jnp.int32),
            pltpu.VMEM(shape, jnp.int32),
            pltpu.VMEM(shape, jnp.int32),
            pltpu.VMEM(shape, BF),
            pltpu.VMEM(shape, BF),
            pltpu.VMEM((16, ROWS), BF),
            pltpu.VMEM((4, ROWS, 128), jnp.int8),
            pltpu.VMEM((512, 128), F32),
            pltpu.VMEM((4, 2, 2, NX) + block, F32),
            pltpu.VMEM((4, 2, NX) + block, F32),
            pltpu.VMEM((4, 2, NX) + block, F32),
            pltpu.VMEM((3, NX - 1, 2) + block, F32),
            pltpu.VMEM((3, 2) + block, F32),
            pltpu.VMEM((6,) + block, F32),
            pltpu.VMEM((NX - 1,) + block, F32),
            pltpu.VMEM((NX,) + block, F32),
            pltpu.VMEM((4, 1, 128), F32),
            pltpu.VMEM((4, 7, 1, 128), F32),
            dma((8,)), dma((5,)), dma((5,)), dma((3, 3)), dma((3, 3)), dma((6,)), dma((6,)),
            dma((3,)), dma((3,)), dma((4,)), dma((4,)), dma((4, 7)), dma((4, 7)),
        ],
        compiler_params=pltpu.CompilerParams(collective_id=0, has_side_effects=True, vmem_limit_bytes=24 << 20),
    )(bin_values, leaf_ids, treated, gradient, hessian)
    vmem = pl.BlockSpec(memory_space=pltpu.VMEM)
    gain, best = pl.pallas_call(
        write_kernel,
        out_shape=(jax.ShapeDtypeStruct((8, 128), F32), jax.ShapeDtypeStruct((4,), F32)),
        in_specs=[vmem, vmem],
        out_specs=(pl.BlockSpec(memory_space=pltpu.HBM), pl.BlockSpec(memory_space=pltpu.SMEM)),
        scratch_shapes=[dma(())],
        compiler_params=pltpu.CompilerParams(vmem_limit_bytes=1 << 20),
    )(gain, top)
    return gain.reshape(4, 2, 128), best


def solution(mesh):
    in_specs = (P("row", "feat"), P("row"), P("row"), P("row"), P("row"))
    out_specs = (P(None, ("feat", "row"), None), P())
    return jax.shard_map(body, mesh=mesh, in_specs=in_specs, out_specs=out_specs, check_vma=False)
```

```python
import jax
import jax.numpy as jnp
from jax import lax
from jax.experimental import pallas as pl
from jax.experimental.pallas import tpu as pltpu
from jax.sharding import PartitionSpec as P

MESH = pl.DeviceIdType.MESH
BF = jnp.bfloat16
F32 = jnp.float32
F8 = jnp.float8_e4m3fn
ROWS = 2048
FEATS = 128
TILE = 256
TILES = ROWS // TILE
PAIRS = 8
NX, NZ, NY = 4, 8, 8


def load_stats(leaf_ref, arm_ref, grad_ref, hess_ref, stat_scr):
    stat = lax.broadcasted_iota(jnp.int32, (16, 128), 0)
    kind, leaf_of = stat // 4, stat % 4
    for c in range(ROWS // 128):
        grad = grad_ref[c : c + 1, :].astype(F32)
        hess = hess_ref[c : c + 1, :].astype(F32)
        keep = (leaf_ref[c : c + 1, :] == leaf_of) & ((arm_ref[c : c + 1, :] == 1) == (kind < 2))
        value = jnp.where(kind % 2 == 0, grad, hess)
        stat_scr[:, c * 128 : (c + 1) * 128] = jnp.where(keep, value, 0.0).astype(BF)


def lane_orders(z):
    feat = lax.broadcasted_iota(jnp.int32, (TILE, 128), 0)
    lane = lax.broadcasted_iota(jnp.int32, (TILE, 128), 1)
    owner = lane // 8
    core, u, x = owner // 8, owner // 4 % 2, owner % 4
    orders = []
    for c in range(4):
        far = lax.rem(z + jnp.where(u == 0, 4 + c, 3 - c), NZ)
        orders.append((feat == ((x * NZ + far) * 2 + core) * 2 + lane % 2).astype(F32).astype(BF))
    return [jnp.concatenate(orders[:2], axis=1), jnp.concatenate(orders[2:], axis=1)]


def spread_bins(accs, orders, loads, bins_ref, bins_scr):
    def drain(r):
        rows = slice(r * TILE, (r + 1) * TILE)
        for p in range(2):
            spread = pltpu.matmul_pop(accs[2 * (r % 2) + p]).astype(jnp.int32).astype(jnp.int8)
            bins_scr[2 * p, rows, :] = spread[:, :128]
            bins_scr[2 * p + 1, rows, :] = spread[:, 128:]

    for p in range(2):
        pltpu.matmul_push_rhs(orders[p], staging_register=0, mxu_index=p)
    for r in range(TILES):
        if r % 2 == 0:
            loads[r // 2].wait()
        block = bins_ref[r * TILE : (r + 1) * TILE, :].astype(F32).astype(BF)
        block = jnp.concatenate([block, block], axis=1)
        for p in range(2):
            pltpu.matmul_acc_lhs(accs[2 * (r % 2) + p], block, load_staged_rhs=0 if r == 0 else None)
        if r:
            drain(r - 1)
    drain(TILES - 1)


def half_chunk(accs, c, w, stat_scr, bins_scr, turn_scr):
    shape = (TILE // 32, 32, 128)
    one, zero = jnp.ones(shape, F8), jnp.zeros(shape, F8)
    group = lax.broadcasted_iota(jnp.int32, (32, 128), 1) % 8 // 2
    first = 2 * PAIRS * w
    last = [(group * 32 + (first + q)).astype(jnp.int8)[None] for q in range(2 * PAIRS)]
    for k in range(TILES):
        rows = slice(k * TILE, (k + 1) * TILE)
        bins = bins_scr[c, rows, :].reshape(shape)
        stat = stat_scr[:, rows]
        for q in range(PAIRS):
            hot = [jnp.where(bins <= last[2 * q + e], one, zero).reshape(TILE, 128) for e in range(2)]
            reg = (k * (PAIRS // 2) + q // 2) % 2
            pltpu.matmul_push_rhs(jnp.concatenate(hot, axis=1), staging_register=reg, mxu_index=q % 2)
            pltpu.matmul_acc_lhs(accs[q], stat, load_staged_rhs=reg)
    for q in range(PAIRS):
        sums = pltpu.matmul_pop(accs[q])
        for e in range(2):
            turn_scr[pl.ds(first + 2 * q + e, 16, stride=32), :] = sums[:, e * 128 : (e + 1) * 128]


def turn_chunk(c, turn_scr, hist):
    for t in range(4):
        turned = turn_scr[t * 128 : (t + 1) * 128, :].T
        hist[c, :, :, :, :, t * 128 : (t + 1) * 128] = turned.reshape(2, 2, NX, 8, 128)


def score(totals):
    grad_t, hess_t, grad_c, hess_c = (totals[8 * k : 8 * k + 8] for k in range(4))
    value_t = grad_t / (hess_t + 1.0)
    value_c = grad_c / (hess_c + 1.0)
    spread = value_t - value_c
    return grad_t * value_t + grad_c * value_c + (hess_t + hess_c) * spread * spread


def finish(block):
    left = jnp.concatenate([block[:, 128 * k : 128 * (k + 1)] for k in range(4)], axis=0)
    leaf = lax.broadcasted_iota(jnp.int32, (32, 128), 1) // 32
    sub = lax.broadcasted_iota(jnp.int32, (32, 128), 0) % 8
    last = jnp.where(sub >= 6, left, 0.0)
    last = last + jnp.where((sub >= 4) & (sub < 6), pltpu.roll(last, 30, 0), 0.0)
    last = last + jnp.where(sub < 4, pltpu.roll(last, 28, 0), 0.0)
    parent = jnp.broadcast_to(last[:, 127:128], (32, 128))
    for k in range(3):
        parent = jnp.where(leaf == k, jnp.broadcast_to(last[:, 32 * k + 31 : 32 * k + 32], (32, 128)), parent)
    gain = score(left) + score(parent - left) - score(parent)
    return gain


def store_gain(gain, gain_ref):
    lane_block = lax.broadcasted_iota(jnp.int32, (8, 128), 1) // 32
    row_block = lax.broadcasted_iota(jnp.int32, (8, 128), 0) // 2
    out = gain
    for d in range(1, 4):
        moved = pltpu.roll(pltpu.roll(gain, 32 * d, 1), 8 - 2 * d, 0)
        out = jnp.where((lane_block + 4 - row_block) % 4 == d, moved, out)
    gain_ref[...] = out


def kernel(
    bins_hbm, leaf_hbm, arm_hbm, grad_hbm, hess_hbm, gain_ref, best_ref,
    bins_ref, leaf_ref, arm_ref, grad_ref, hess_ref, stat_scr, bins_scr, turn_scr,
    hist, core_in, core_sum, x_in, x_sum, z_in, last_x, last_z, top_out, top_in,
    load_sem, core_send, core_recv, x_send, x_recv, z_send, z_recv,
    last_x_send, last_x_recv, last_z_send, last_z_recv, top_send, top_recv,
):
    feat = lax.axis_index("feat")
    row = lax.axis_index("row")
    core = lax.rem(row, 2)
    z = lax.rem(row // 2, NZ)
    x = row // (2 * NZ)

    def at(dx, dz, core_):
        return (feat, (lax.rem(x + dx, NX) * NZ + lax.rem(z + dz, NZ)) * 2 + core_)

    other = at(0, 0, 1 - core)
    x_peer = [at(d, 0, core) for d in range(NX)]
    y_peer = [(lax.rem(feat + d, NY), row) for d in range(NY)]

    pairs = [(leaf_hbm, leaf_ref), (arm_hbm, arm_ref), (grad_hbm, grad_ref), (hess_hbm, hess_ref)]
    pairs += [(bins_hbm.at[pl.ds(k * 512, 512)], bins_ref.at[pl.ds(k * 512, 512)]) for k in range(4)]
    loads = [pltpu.make_async_copy(src, dst, load_sem.at[k]) for k, (src, dst) in enumerate(pairs)]
    for load in loads:
        load.start()
    barrier = pltpu.get_barrier_semaphore()
    far = (4, 3, 5, 2, 6, 1, 7)
    greeted = [at(0, d, core) for d in far] + [y_peer[d] for d in far]
    greeted += [at(d, e, core) for d in (2, 1, 3) for e in (1, NZ - 1, 0)] + [other]
    for peer in greeted:
        pl.semaphore_signal(barrier, inc=1, device_id=peer, device_id_type=MESH)

    for load in loads[:4]:
        load.wait()
    load_stats(leaf_ref, arm_ref, grad_ref, hess_ref, stat_scr)
    orders = lane_orders(z)
    pl.run_scoped(
        lambda *accs: spread_bins(accs, orders, loads[4:], bins_ref, bins_scr),
        *[pltpu.ACC(q % 2)((TILE, TILE), F32) for q in range(4)],
    )

    def copy(src, dst, send, recv, peer):
        return pltpu.make_async_remote_copy(
            src_ref=src, dst_ref=dst, send_sem=send, recv_sem=recv, device_id=peer, device_id_type=MESH
        )

    def core_copy(c):
        return copy(hist.at[c, 1 - core], core_in.at[c], core_send.at[c], core_recv.at[c], other)

    def last_core_copy(u):
        k = 3 + u
        return copy(hist.at[3, 1 - core, u], core_in.at[3, u], core_send.at[k], core_recv.at[k], other)

    def x_copy(c, d):
        return copy(
            core_sum.at[c, :, lax.rem(x + d, NX)], x_in.at[c, d - 1], x_send.at[c, d - 1], x_recv.at[c, d - 1], x_peer[d]
        )

    def z_copy(c, u):
        d = 3 - c if u else 4 + c
        return copy(x_sum.at[c, u], z_in.at[d - 1], z_send.at[d - 1], z_recv.at[d - 1], at(0, d, core))

    def last_x_copy(d):
        return copy(
            core_sum.at[3, 1, lax.rem(x + d, NX)], last_x.at[d - 1], last_x_send.at[d - 1], last_x_recv.at[d - 1], x_peer[d]
        )

    def last_z_copy(d):
        return copy(
            core_sum.at[3, 0, lax.rem(x + d, NX)], last_z.at[d], last_z_send.at[d], last_z_recv.at[d], at(d, NZ - 1, core)
        )

    def add_core(c):
        core_copy(c).wait_recv()
        core_sum[c] = hist[c, core] + core_in[c]

    def start_x(c):
        add_core(c)
        for d in (2, 1, 3):
            x_copy(c, d).start()

    def start_z(c):
        for d in (1, 3, 2):
            x_copy(c, d).wait_recv()
        x_sum[c] = core_sum[c, :, x] + x_in[c, 0] + x_in[c, 1] + x_in[c, 2]
        for u in range(2):
            z_copy(c, u).start()

    def all_halves(*accs):
        def step(h, carry):
            c, w = h // 2, h % 2
            half_chunk(accs, c, w, stat_scr, bins_scr, turn_scr)

            @pl.when(h == 1)
            def _():
                pl.semaphore_wait(barrier, len(greeted))

            @pl.when(w == 1)
            def _():
                turn_chunk(c, turn_scr, hist)

            @pl.when((w == 1) & (c < 3))
            def _():
                core_copy(c).start()

            @pl.when((w == 1) & (c == 3))
            def _():
                for u in range(2):
                    last_core_copy(u).start()

            @pl.when(((w == 1) & (c >= 1) & (c < 3)) | (h == 6))
            def _():
                start_x(c - 1)

            return carry

        lax.fori_loop(0, 8, step, 0)

    pl.run_scoped(all_halves, *[pltpu.ACC(q % 2)((16, TILE), F32) for q in range(PAIRS)])

    start_z(0)
    for u in range(2):
        last_core_copy(u).wait_recv()
        core_sum[3, u] = hist[3, core, u] + core_in[3, u]
        for d in (2, 1, 3, 0):
            if u == 0:
                last_z_copy(d).start()
            elif d:
                last_x_copy(d).start()
    for c in range(1, 3):
        start_z(c)
    block = core_sum[3, 1, x]
    for c in range(2):
        for u in range(2):
            z_copy(c, u).wait_recv()
            block = block + z_in[2 - c if u else 3 + c]
    for d in range(NX):
        last_z_copy(d).wait_recv()
        block = block + last_z[d]
        if d:
            last_x_copy(d).wait_recv()
            block = block + last_x[d - 1]
    for u in range(2):
        z_copy(2, u).wait_recv()
        block = block + z_in[0 if u else 5]

    gain = finish(block)
    top = jnp.max(gain, axis=0, keepdims=True)

    def wait_sends():
        for u in range(2):
            last_core_copy(u).wait_send()
        for c in range(3):
            core_copy(c).wait_send()
            for d in range(1, NX):
                x_copy(c, d).wait_send()
            for u in range(2):
                z_copy(c, u).wait_send()
        for d in range(NX):
            last_z_copy(d).wait_send()
            if d:
                last_x_copy(d).wait_send()

    rounds = (
        [other],
        [x_peer[d] for d in (2, 1, 3)],
        [at(0, d, core) for d in far],
        [y_peer[d] for d in far],
    )
    top_copies = []
    for stage, peers in enumerate(rounds):
        top_out[stage] = top
        sent = []
        for k, peer in enumerate(peers):
            s = copy(top_out.at[stage], top_in.at[stage, k], top_send.at[stage, k], top_recv.at[stage, k], peer)
            s.start()
            sent.append(s)
        if stage == 0:
            store_gain(gain, gain_ref)
        if stage == 2:
            wait_sends()
        if stage:
            for s in top_copies:
                s.wait_send()
            top_copies = []
        for s in reversed(sent):
            s.wait_recv()
        for k in range(len(sent)):
            top = jnp.maximum(top, top_in[stage, k])
        top_copies += sent
    best_ref[...] = top
    for s in top_copies:
        s.wait_send()


def write_kernel(gain_ref, top_ref, gain_hbm, best_ref, sem):
    write = pltpu.make_async_copy(gain_ref, gain_hbm, sem)
    write.start()
    for leaf in range(4):
        best_ref[leaf] = jnp.max(top_ref[:, 32 * leaf : 32 * (leaf + 1)])
    write.wait()


def body(bin_values, leaf_ids, treated, gradient, hessian):
    shape = (ROWS // 128, 128)
    dma = pltpu.SemaphoreType.DMA
    block = (8, 512)
    bin_values, leaf_ids, treated, gradient, hessian = (
        pltpu.with_memory_space_constraint(v, pltpu.HBM)
        for v in (bin_values, leaf_ids.reshape(shape), treated.reshape(shape), gradient.reshape(shape), hessian.reshape(shape))
    )
    gain, top = pl.pallas_call(
        kernel,
        out_shape=(jax.ShapeDtypeStruct((8, 128), F32), jax.ShapeDtypeStruct((1, 128), F32)),
        in_specs=[pl.BlockSpec(memory_space=pltpu.HBM)] * 5,
        out_specs=(pl.BlockSpec(memory_space=pltpu.VMEM),) * 2,
        scratch_shapes=[
            pltpu.VMEM((ROWS, FEATS), jnp.int32),
            pltpu.VMEM(shape, jnp.int32),
            pltpu.VMEM(shape, jnp.int32),
            pltpu.VMEM(shape, BF),
            pltpu.VMEM(shape, BF),
            pltpu.VMEM((16, ROWS), BF),
            pltpu.VMEM((4, ROWS, 128), jnp.int8),
            pltpu.VMEM((512, 128), F32),
            pltpu.VMEM((4, 2, 2, NX) + block, F32),
            pltpu.VMEM((4, 2, NX) + block, F32),
            pltpu.VMEM((4, 2, NX) + block, F32),
            pltpu.VMEM((3, NX - 1, 2) + block, F32),
            pltpu.VMEM((3, 2) + block, F32),
            pltpu.VMEM((6,) + block, F32),
            pltpu.VMEM((NX - 1,) + block, F32),
            pltpu.VMEM((NX,) + block, F32),
            pltpu.VMEM((4, 1, 128), F32),
            pltpu.VMEM((4, 7, 1, 128), F32),
            dma((8,)), dma((5,)), dma((5,)), dma((3, 3)), dma((3, 3)), dma((6,)), dma((6,)),
            dma((3,)), dma((3,)), dma((4,)), dma((4,)), dma((4, 7)), dma((4, 7)),
        ],
        compiler_params=pltpu.CompilerParams(collective_id=0, has_side_effects=True, vmem_limit_bytes=24 << 20),
    )(bin_values, leaf_ids, treated, gradient, hessian)
    vmem = pl.BlockSpec(memory_space=pltpu.VMEM)
    gain, best = pl.pallas_call(
        write_kernel,
        out_shape=(jax.ShapeDtypeStruct((8, 128), F32), jax.ShapeDtypeStruct((4,), F32)),
        in_specs=[vmem, vmem],
        out_specs=(pl.BlockSpec(memory_space=pltpu.HBM), pl.BlockSpec(memory_space=pltpu.SMEM)),
        scratch_shapes=[dma(())],
        compiler_params=pltpu.CompilerParams(vmem_limit_bytes=1 << 20),
    )(gain, top)
    return gain.reshape(4, 2, 128), best


def solution(mesh):
    in_specs = (P("row", "feat"), P("row"), P("row"), P("row"), P("row"))
    out_specs = (P(None, ("feat", "row"), None), P())
    return jax.shard_map(body, mesh=mesh, in_specs=in_specs, out_specs=out_specs, check_vma=False)
```

```python
import jax
import jax.numpy as jnp
from jax import lax
from jax.experimental import pallas as pl
from jax.experimental.pallas import tpu as pltpu
from jax.sharding import PartitionSpec as P

MESH = pl.DeviceIdType.MESH
BF = jnp.bfloat16
F32 = jnp.float32
F8 = jnp.float8_e4m3fn
ROWS = 2048
FEATS = 128
TILE = 256
TILES = ROWS // TILE
PAIRS = 16
NX, NZ, NY = 4, 8, 8


def load_stats(leaf_ref, arm_ref, grad_ref, hess_ref, stat_scr):
    stat = lax.broadcasted_iota(jnp.int32, (16, 128), 0)
    kind, leaf_of = stat // 4, stat % 4
    for c in range(ROWS // 128):
        grad = grad_ref[c : c + 1, :].astype(F32)
        hess = hess_ref[c : c + 1, :].astype(F32)
        keep = (leaf_ref[c : c + 1, :] == leaf_of) & ((arm_ref[c : c + 1, :] == 1) == (kind < 2))
        value = jnp.where(kind % 2 == 0, grad, hess)
        stat_scr[:, c * 128 : (c + 1) * 128] = jnp.where(keep, value, 0.0).astype(BF)


def lane_orders(z):
    feat = lax.broadcasted_iota(jnp.int32, (TILE, 128), 0)
    lane = lax.broadcasted_iota(jnp.int32, (TILE, 128), 1)
    owner = lane // 8
    core, u, x = owner // 8, owner // 4 % 2, owner % 4
    orders = []
    for c in range(4):
        far = lax.rem(z + jnp.where(u == 0, 4 + c, 3 - c), NZ)
        orders.append((feat == ((x * NZ + far) * 2 + core) * 2 + lane % 2).astype(F32).astype(BF))
    return [jnp.concatenate(orders[:2], axis=1), jnp.concatenate(orders[2:], axis=1)]


def spread_bins(accs, orders, loads, bins_ref, bins_scr):
    def drain(r):
        rows = slice(r * TILE, (r + 1) * TILE)
        for p in range(2):
            spread = pltpu.matmul_pop(accs[2 * (r % 2) + p]).astype(jnp.int32).astype(jnp.int8)
            bins_scr[2 * p, rows, :] = spread[:, :128]
            bins_scr[2 * p + 1, rows, :] = spread[:, 128:]

    for p in range(2):
        pltpu.matmul_push_rhs(orders[p], staging_register=0, mxu_index=p)
    for r in range(TILES):
        if r % 2 == 0:
            loads[r // 2].wait()
        block = bins_ref[r * TILE : (r + 1) * TILE, :].astype(F32).astype(BF)
        block = jnp.concatenate([block, block], axis=1)
        for p in range(2):
            pltpu.matmul_acc_lhs(accs[2 * (r % 2) + p], block, load_staged_rhs=0 if r == 0 else None)
        if r:
            drain(r - 1)
    drain(TILES - 1)


def sum_chunk(accs, c, stat_scr, bins_scr, turn_scr):
    shape = (TILE // 32, 32, 128)
    one, zero = jnp.ones(shape, F8), jnp.zeros(shape, F8)
    group = lax.broadcasted_iota(jnp.int32, (32, 128), 1) % 8 // 2
    last = [(group * 32 + q).astype(jnp.int8)[None] for q in range(2 * PAIRS)]
    for k in range(TILES):
        rows = slice(k * TILE, (k + 1) * TILE)
        bins = bins_scr[c, rows, :].reshape(shape)
        stat = stat_scr[:, rows]
        for q in range(PAIRS):
            hot = [jnp.where(bins <= last[2 * q + e], one, zero).reshape(TILE, 128) for e in range(2)]
            reg = (k * (PAIRS // 2) + q // 2) % 2
            pltpu.matmul_push_rhs(jnp.concatenate(hot, axis=1), staging_register=reg, mxu_index=q % 2)
            pltpu.matmul_acc_lhs(accs[q], stat, load_staged_rhs=reg)
    for q in range(PAIRS):
        sums = pltpu.matmul_pop(accs[q])
        for e in range(2):
            turn_scr[pl.ds(2 * q + e, 16, stride=32), :] = sums[:, e * 128 : (e + 1) * 128]


def turn_chunk(c, turn_scr, hist):
    for t in range(4):
        turned = turn_scr[t * 128 : (t + 1) * 128, :].T
        hist[c, :, :, :, :, t * 128 : (t + 1) * 128] = turned.reshape(2, 2, NX, 8, 128)


def score(totals):
    grad_t, hess_t, grad_c, hess_c = (totals[8 * k : 8 * k + 8] for k in range(4))
    value_t = grad_t / (hess_t + 1.0)
    value_c = grad_c / (hess_c + 1.0)
    spread = value_t - value_c
    return grad_t * value_t + grad_c * value_c + (hess_t + hess_c) * spread * spread


def finish(block):
    left = jnp.concatenate([block[:, 128 * k : 128 * (k + 1)] for k in range(4)], axis=0)
    leaf = lax.broadcasted_iota(jnp.int32, (32, 128), 1) // 32
    sub = lax.broadcasted_iota(jnp.int32, (32, 128), 0) % 8
    last = jnp.where(sub >= 6, left, 0.0)
    last = last + jnp.where((sub >= 4) & (sub < 6), pltpu.roll(last, 30, 0), 0.0)
    last = last + jnp.where(sub < 4, pltpu.roll(last, 28, 0), 0.0)
    parent = jnp.broadcast_to(last[:, 127:128], (32, 128))
    for k in range(3):
        parent = jnp.where(leaf == k, jnp.broadcast_to(last[:, 32 * k + 31 : 32 * k + 32], (32, 128)), parent)
    gain = score(left) + score(parent - left) - score(parent)
    return gain


def store_gain(gain, gain_ref):
    lane_block = lax.broadcasted_iota(jnp.int32, (8, 128), 1) // 32
    row_block = lax.broadcasted_iota(jnp.int32, (8, 128), 0) // 2
    out = gain
    for d in range(1, 4):
        moved = pltpu.roll(pltpu.roll(gain, 32 * d, 1), 8 - 2 * d, 0)
        out = jnp.where((lane_block + 4 - row_block) % 4 == d, moved, out)
    gain_ref[...] = out


def kernel(
    bins_hbm, leaf_hbm, arm_hbm, grad_hbm, hess_hbm, gain_ref, best_ref,
    bins_ref, leaf_ref, arm_ref, grad_ref, hess_ref, stat_scr, bins_scr, turn_scr,
    hist, core_in, core_sum, x_in, x_sum, z_in, last_x, last_z, top_out, top_in,
    load_sem, core_send, core_recv, x_send, x_recv, z_send, z_recv,
    last_x_send, last_x_recv, last_z_send, last_z_recv, top_send, top_recv,
):
    feat = lax.axis_index("feat")
    row = lax.axis_index("row")
    core = lax.rem(row, 2)
    z = lax.rem(row // 2, NZ)
    x = row // (2 * NZ)

    def at(dx, dz, core_):
        return (feat, (lax.rem(x + dx, NX) * NZ + lax.rem(z + dz, NZ)) * 2 + core_)

    other = at(0, 0, 1 - core)
    x_peer = [at(d, 0, core) for d in range(NX)]
    y_peer = [(lax.rem(feat + d, NY), row) for d in range(NY)]

    pairs = [(leaf_hbm, leaf_ref), (arm_hbm, arm_ref), (grad_hbm, grad_ref), (hess_hbm, hess_ref)]
    pairs += [(bins_hbm.at[pl.ds(k * 512, 512)], bins_ref.at[pl.ds(k * 512, 512)]) for k in range(4)]
    loads = [pltpu.make_async_copy(src, dst, load_sem.at[k]) for k, (src, dst) in enumerate(pairs)]
    for load in loads:
        load.start()
    barrier = pltpu.get_barrier_semaphore()
    far = (4, 3, 5, 2, 6, 1, 7)
    greeted = [at(0, d, core) for d in far] + [y_peer[d] for d in far]
    greeted += [at(d, e, core) for d in (2, 1, 3) for e in (1, NZ - 1, 0)] + [other]
    for peer in greeted:
        pl.semaphore_signal(barrier, inc=1, device_id=peer, device_id_type=MESH)

    for load in loads[:4]:
        load.wait()
    load_stats(leaf_ref, arm_ref, grad_ref, hess_ref, stat_scr)
    orders = lane_orders(z)
    pl.run_scoped(
        lambda *accs: spread_bins(accs, orders, loads[4:], bins_ref, bins_scr),
        *[pltpu.ACC(q % 2)((TILE, TILE), F32) for q in range(4)],
    )

    def copy(src, dst, send, recv, peer):
        return pltpu.make_async_remote_copy(
            src_ref=src, dst_ref=dst, send_sem=send, recv_sem=recv, device_id=peer, device_id_type=MESH
        )

    def core_copy(c):
        return copy(hist.at[c, 1 - core], core_in.at[c], core_send.at[c], core_recv.at[c], other)

    def last_core_copy(u):
        k = 3 + u
        return copy(hist.at[3, 1 - core, u], core_in.at[3, u], core_send.at[k], core_recv.at[k], other)

    def x_copy(c, d):
        return copy(
            core_sum.at[c, :, lax.rem(x + d, NX)], x_in.at[c, d - 1], x_send.at[c, d - 1], x_recv.at[c, d - 1], x_peer[d]
        )

    def z_copy(c, u):
        d = 3 - c if u else 4 + c
        return copy(x_sum.at[c, u], z_in.at[d - 1], z_send.at[d - 1], z_recv.at[d - 1], at(0, d, core))

    def last_x_copy(d):
        return copy(
            core_sum.at[3, 1, lax.rem(x + d, NX)], last_x.at[d - 1], last_x_send.at[d - 1], last_x_recv.at[d - 1], x_peer[d]
        )

    def last_z_copy(d):
        return copy(
            core_sum.at[3, 0, lax.rem(x + d, NX)], last_z.at[d], last_z_send.at[d], last_z_recv.at[d], at(d, NZ - 1, core)
        )

    def add_core(c):
        core_copy(c).wait_recv()
        core_sum[c] = hist[c, core] + core_in[c]

    def start_x(c):
        add_core(c)
        for d in (2, 1, 3):
            x_copy(c, d).start()

    def start_z(c):
        for d in (1, 3, 2):
            x_copy(c, d).wait_recv()
        x_sum[c] = core_sum[c, :, x] + x_in[c, 0] + x_in[c, 1] + x_in[c, 2]
        for u in range(2):
            z_copy(c, u).start()

    def all_chunks(*accs):
        def step(c, carry):
            sum_chunk(accs, c, stat_scr, bins_scr, turn_scr)

            @pl.when(c == 0)
            def _():
                pl.semaphore_wait(barrier, len(greeted))

            @pl.when(c > 0)
            def _():
                start_x(c - 1)

            turn_chunk(c, turn_scr, hist)

            @pl.when(c < 3)
            def _():
                core_copy(c).start()

            @pl.when(c == 3)
            def _():
                for u in range(2):
                    last_core_copy(u).start()

            return carry

        lax.fori_loop(0, 4, step, 0)

    pl.run_scoped(all_chunks, *[pltpu.ACC(q % 2)((16, TILE), F32) for q in range(PAIRS)])

    start_z(0)
    for u in range(2):
        last_core_copy(u).wait_recv()
        core_sum[3, u] = hist[3, core, u] + core_in[3, u]
        for d in (2, 1, 3, 0):
            if u == 0:
                last_z_copy(d).start()
            elif d:
                last_x_copy(d).start()
    for c in range(1, 3):
        start_z(c)
    block = core_sum[3, 1, x]
    for c in range(2):
        for u in range(2):
            z_copy(c, u).wait_recv()
            block = block + z_in[2 - c if u else 3 + c]
    for d in range(NX):
        last_z_copy(d).wait_recv()
        block = block + last_z[d]
        if d:
            last_x_copy(d).wait_recv()
            block = block + last_x[d - 1]
    for u in range(2):
        z_copy(2, u).wait_recv()
        block = block + z_in[0 if u else 5]

    gain = finish(block)
    top = jnp.max(gain, axis=0, keepdims=True)

    def wait_sends():
        for u in range(2):
            last_core_copy(u).wait_send()
        for c in range(3):
            core_copy(c).wait_send()
            for d in range(1, NX):
                x_copy(c, d).wait_send()
            for u in range(2):
                z_copy(c, u).wait_send()
        for d in range(NX):
            last_z_copy(d).wait_send()
            if d:
                last_x_copy(d).wait_send()

    rounds = (
        [other],
        [x_peer[d] for d in (2, 1, 3)],
        [at(0, d, core) for d in far],
        [y_peer[d] for d in far],
    )
    top_copies = []
    for stage, peers in enumerate(rounds):
        top_out[stage] = top
        sent = []
        for k, peer in enumerate(peers):
            s = copy(top_out.at[stage], top_in.at[stage, k], top_send.at[stage, k], top_recv.at[stage, k], peer)
            s.start()
            sent.append(s)
        if stage == 0:
            store_gain(gain, gain_ref)
        if stage == 2:
            wait_sends()
        if stage:
            for s in top_copies:
                s.wait_send()
            top_copies = []
        for s in reversed(sent):
            s.wait_recv()
        for k in range(len(sent)):
            top = jnp.maximum(top, top_in[stage, k])
        top_copies += sent
    best_ref[...] = top
    for s in top_copies:
        s.wait_send()


def write_kernel(gain_ref, top_ref, gain_hbm, best_ref, sem):
    write = pltpu.make_async_copy(gain_ref, gain_hbm, sem)
    write.start()
    for leaf in range(4):
        best_ref[leaf] = jnp.max(top_ref[:, 32 * leaf : 32 * (leaf + 1)])
    write.wait()


def body(bin_values, leaf_ids, treated, gradient, hessian):
    shape = (ROWS // 128, 128)
    dma = pltpu.SemaphoreType.DMA
    block = (8, 512)
    bin_values, leaf_ids, treated, gradient, hessian = (
        pltpu.with_memory_space_constraint(v, pltpu.HBM)
        for v in (bin_values, leaf_ids.reshape(shape), treated.reshape(shape), gradient.reshape(shape), hessian.reshape(shape))
    )
    gain, top = pl.pallas_call(
        kernel,
        out_shape=(jax.ShapeDtypeStruct((8, 128), F32), jax.ShapeDtypeStruct((1, 128), F32)),
        in_specs=[pl.BlockSpec(memory_space=pltpu.HBM)] * 5,
        out_specs=(pl.BlockSpec(memory_space=pltpu.VMEM),) * 2,
        scratch_shapes=[
            pltpu.VMEM((ROWS, FEATS), jnp.int32),
            pltpu.VMEM(shape, jnp.int32),
            pltpu.VMEM(shape, jnp.int32),
            pltpu.VMEM(shape, BF),
            pltpu.VMEM(shape, BF),
            pltpu.VMEM((16, ROWS), BF),
            pltpu.VMEM((4, ROWS, 128), jnp.int8),
            pltpu.VMEM((512, 128), F32),
            pltpu.VMEM((4, 2, 2, NX) + block, F32),
            pltpu.VMEM((4, 2, NX) + block, F32),
            pltpu.VMEM((4, 2, NX) + block, F32),
            pltpu.VMEM((3, NX - 1, 2) + block, F32),
            pltpu.VMEM((3, 2) + block, F32),
            pltpu.VMEM((6,) + block, F32),
            pltpu.VMEM((NX - 1,) + block, F32),
            pltpu.VMEM((NX,) + block, F32),
            pltpu.VMEM((4, 1, 128), F32),
            pltpu.VMEM((4, 7, 1, 128), F32),
            dma((8,)), dma((5,)), dma((5,)), dma((3, 3)), dma((3, 3)), dma((6,)), dma((6,)),
            dma((3,)), dma((3,)), dma((4,)), dma((4,)), dma((4, 7)), dma((4, 7)),
        ],
        compiler_params=pltpu.CompilerParams(collective_id=0, has_side_effects=True, vmem_limit_bytes=24 << 20),
    )(bin_values, leaf_ids, treated, gradient, hessian)
    vmem = pl.BlockSpec(memory_space=pltpu.VMEM)
    gain, best = pl.pallas_call(
        write_kernel,
        out_shape=(jax.ShapeDtypeStruct((8, 128), F32), jax.ShapeDtypeStruct((4,), F32)),
        in_specs=[vmem, vmem],
        out_specs=(pl.BlockSpec(memory_space=pltpu.HBM), pl.BlockSpec(memory_space=pltpu.SMEM)),
        scratch_shapes=[dma(())],
        compiler_params=pltpu.CompilerParams(vmem_limit_bytes=1 << 20),
    )(gain, top)
    return gain.reshape(4, 2, 128), best


def solution(mesh):
    in_specs = (P("row", "feat"), P("row"), P("row"), P("row"), P("row"))
    out_specs = (P(None, ("feat", "row"), None), P())
    return jax.shard_map(body, mesh=mesh, in_specs=in_specs, out_specs=out_specs, check_vma=False)
```

```python
import jax
import jax.numpy as jnp
from jax import lax
from jax.experimental import pallas as pl
from jax.experimental.pallas import tpu as pltpu
from jax.sharding import PartitionSpec as P

MESH = pl.DeviceIdType.MESH
BF = jnp.bfloat16
F32 = jnp.float32
F8 = jnp.float8_e4m3fn
ROWS = 2048
FEATS = 128
TILE = 256
TILES = ROWS // TILE
PAIRS = 16
NX, NZ, NY = 4, 8, 8


def load_stats(leaf_ref, arm_ref, grad_ref, hess_ref, stat_scr):
    stat = lax.broadcasted_iota(jnp.int32, (16, 128), 0)
    kind, leaf_of = stat // 4, stat % 4
    for c in range(ROWS // 128):
        grad = grad_ref[c : c + 1, :].astype(F32)
        hess = hess_ref[c : c + 1, :].astype(F32)
        keep = (leaf_ref[c : c + 1, :] == leaf_of) & ((arm_ref[c : c + 1, :] == 1) == (kind < 2))
        value = jnp.where(kind % 2 == 0, grad, hess)
        stat_scr[:, c * 128 : (c + 1) * 128] = jnp.where(keep, value, 0.0).astype(BF)


def lane_orders(z):
    feat = lax.broadcasted_iota(jnp.int32, (TILE, 128), 0)
    lane = lax.broadcasted_iota(jnp.int32, (TILE, 128), 1)
    owner = lane // 8
    core, u, x = owner // 8, owner // 4 % 2, owner % 4
    orders = []
    for c in range(4):
        far = lax.rem(z + jnp.where(u == 0, 4 + c, 3 - c), NZ)
        orders.append((feat == ((x * NZ + far) * 2 + core) * 2 + lane % 2).astype(F32).astype(BF))
    return [jnp.concatenate(orders[:2], axis=1), jnp.concatenate(orders[2:], axis=1)]


def spread_bins(accs, orders, loads, bins_ref, bins_scr):
    def drain(r):
        rows = slice(r * TILE, (r + 1) * TILE)
        for p in range(2):
            spread = pltpu.matmul_pop(accs[2 * (r % 2) + p]).astype(jnp.int32).astype(jnp.int8)
            bins_scr[2 * p, rows, :] = spread[:, :128]
            bins_scr[2 * p + 1, rows, :] = spread[:, 128:]

    for p in range(2):
        pltpu.matmul_push_rhs(orders[p], staging_register=0, mxu_index=p)
    for r in range(TILES):
        if r % 2 == 0:
            loads[r // 2].wait()
        block = bins_ref[r * TILE : (r + 1) * TILE, :].astype(F32).astype(BF)
        block = jnp.concatenate([block, block], axis=1)
        for p in range(2):
            pltpu.matmul_acc_lhs(accs[2 * (r % 2) + p], block, load_staged_rhs=0 if r == 0 else None)
        if r:
            drain(r - 1)
    drain(TILES - 1)


def sum_chunk(accs, c, stat_scr, bins_scr, turn_scr):
    shape = (TILE // 32, 32, 128)
    one, zero = jnp.ones(shape, F8), jnp.zeros(shape, F8)
    group = lax.broadcasted_iota(jnp.int32, (32, 128), 1) % 8 // 2
    last = [(group * 32 + q).astype(jnp.int8)[None] for q in range(2 * PAIRS)]
    for k in range(TILES):
        rows = slice(k * TILE, (k + 1) * TILE)
        bins = bins_scr[c, rows, :].reshape(shape)
        stat = stat_scr[:, rows]
        for q in range(PAIRS):
            hot = [jnp.where(bins <= last[2 * q + e], one, zero).reshape(TILE, 128) for e in range(2)]
            reg = (k * (PAIRS // 2) + q // 2) % 2
            pltpu.matmul_push_rhs(jnp.concatenate(hot, axis=1), staging_register=reg, mxu_index=q % 2)
            pltpu.matmul_acc_lhs(accs[q], stat, load_staged_rhs=reg)
    for q in range(PAIRS):
        sums = pltpu.matmul_pop(accs[q])
        for e in range(2):
            turn_scr[pl.ds(2 * q + e, 16, stride=32), :] = sums[:, e * 128 : (e + 1) * 128]


def turn_chunk(c, turn_scr, hist):
    for t in range(4):
        turned = turn_scr[t * 128 : (t + 1) * 128, :].T
        hist[c, :, :, :, :, t * 128 : (t + 1) * 128] = turned.reshape(2, 2, NX, 8, 128)


def score(totals):
    grad_t, hess_t, grad_c, hess_c = (totals[8 * k : 8 * k + 8] for k in range(4))
    value_t = grad_t / (hess_t + 1.0)
    value_c = grad_c / (hess_c + 1.0)
    spread = value_t - value_c
    return grad_t * value_t + grad_c * value_c + (hess_t + hess_c) * spread * spread


def finish(block):
    left = jnp.concatenate([block[:, 128 * k : 128 * (k + 1)] for k in range(4)], axis=0)
    leaf = lax.broadcasted_iota(jnp.int32, (32, 128), 1) // 32
    sub = lax.broadcasted_iota(jnp.int32, (32, 128), 0) % 8
    last = jnp.where(sub >= 6, left, 0.0)
    last = last + jnp.where((sub >= 4) & (sub < 6), pltpu.roll(last, 30, 0), 0.0)
    last = last + jnp.where(sub < 4, pltpu.roll(last, 28, 0), 0.0)
    parent = jnp.broadcast_to(last[:, 127:128], (32, 128))
    for k in range(3):
        parent = jnp.where(leaf == k, jnp.broadcast_to(last[:, 32 * k + 31 : 32 * k + 32], (32, 128)), parent)
    gain = score(left) + score(parent - left) - score(parent)
    return gain


def store_gain(gain, gain_ref):
    lane_block = lax.broadcasted_iota(jnp.int32, (8, 128), 1) // 32
    row_block = lax.broadcasted_iota(jnp.int32, (8, 128), 0) // 2
    out = gain
    for d in range(1, 4):
        moved = pltpu.roll(pltpu.roll(gain, 32 * d, 1), 8 - 2 * d, 0)
        out = jnp.where((lane_block + 4 - row_block) % 4 == d, moved, out)
    gain_ref[...] = out


def kernel(
    bins_hbm, leaf_hbm, arm_hbm, grad_hbm, hess_hbm, gain_ref, best_ref,
    bins_ref, leaf_ref, arm_ref, grad_ref, hess_ref, stat_scr, bins_scr, turn_scr,
    hist, core_in, core_sum, x_in, x_sum, z_in, last_x, last_z, top_out, top_in,
    load_sem, core_send, core_recv, x_send, x_recv, z_send, z_recv,
    last_x_send, last_x_recv, last_z_send, last_z_recv, top_send, top_recv,
):
    feat = lax.axis_index("feat")
    row = lax.axis_index("row")
    core = lax.rem(row, 2)
    z = lax.rem(row // 2, NZ)
    x = row // (2 * NZ)

    def at(dx, dz, core_):
        return (feat, (lax.rem(x + dx, NX) * NZ + lax.rem(z + dz, NZ)) * 2 + core_)

    other = at(0, 0, 1 - core)
    x_peer = [at(d, 0, core) for d in range(NX)]
    y_peer = [(lax.rem(feat + d, NY), row) for d in range(NY)]

    pairs = [(leaf_hbm, leaf_ref), (arm_hbm, arm_ref), (grad_hbm, grad_ref), (hess_hbm, hess_ref)]
    pairs += [(bins_hbm.at[pl.ds(k * 512, 512)], bins_ref.at[pl.ds(k * 512, 512)]) for k in range(4)]
    loads = [pltpu.make_async_copy(src, dst, load_sem.at[k]) for k, (src, dst) in enumerate(pairs)]
    for load in loads:
        load.start()
    barrier = pltpu.get_barrier_semaphore()
    far = (4, 3, 5, 2, 6, 1, 7)
    greeted = [at(0, d, core) for d in far] + [y_peer[d] for d in far]
    greeted += [at(d, e, core) for d in (2, 1, 3) for e in (1, NZ - 1, 0)] + [other]
    for peer in greeted:
        pl.semaphore_signal(barrier, inc=1, device_id=peer, device_id_type=MESH)

    for load in loads[:4]:
        load.wait()
    load_stats(leaf_ref, arm_ref, grad_ref, hess_ref, stat_scr)
    orders = lane_orders(z)
    pl.run_scoped(
        lambda *accs: spread_bins(accs, orders, loads[4:], bins_ref, bins_scr),
        *[pltpu.ACC(q % 2)((TILE, TILE), F32) for q in range(4)],
    )

    def copy(src, dst, send, recv, peer):
        return pltpu.make_async_remote_copy(
            src_ref=src, dst_ref=dst, send_sem=send, recv_sem=recv, device_id=peer, device_id_type=MESH
        )

    def core_copy(c):
        return copy(hist.at[c, 1 - core], core_in.at[c], core_send.at[c], core_recv.at[c], other)

    def last_core_copy(u):
        k = 3 + u
        return copy(hist.at[3, 1 - core, u], core_in.at[3, u], core_send.at[k], core_recv.at[k], other)

    def x_copy(c, d):
        return copy(
            core_sum.at[c, :, lax.rem(x + d, NX)], x_in.at[c, d - 1], x_send.at[c, d - 1], x_recv.at[c, d - 1], x_peer[d]
        )

    def near_x_copy(u, d):
        k = 2 + u
        return copy(
            core_sum.at[2, u, lax.rem(x + d, NX)], x_in.at[2, d - 1, u], x_send.at[k, d - 1], x_recv.at[k, d - 1], x_peer[d]
        )

    def z_copy(c, u):
        d = 3 - c if u else 4 + c
        return copy(x_sum.at[c, u], z_in.at[d - 1], z_send.at[d - 1], z_recv.at[d - 1], at(0, d, core))

    def last_x_copy(d):
        return copy(
            core_sum.at[3, 1, lax.rem(x + d, NX)], last_x.at[d - 1], last_x_send.at[d - 1], last_x_recv.at[d - 1], x_peer[d]
        )

    def last_z_copy(d):
        return copy(
            core_sum.at[3, 0, lax.rem(x + d, NX)], last_z.at[d], last_z_send.at[d], last_z_recv.at[d], at(d, NZ - 1, core)
        )

    def add_core(c):
        core_copy(c).wait_recv()
        core_sum[c] = hist[c, core] + core_in[c]

    def start_x(c):
        add_core(c)
        for d in (2, 1, 3):
            x_copy(c, d).start()

    def start_z(c):
        for d in (1, 3, 2):
            x_copy(c, d).wait_recv()
        x_sum[c] = core_sum[c, :, x] + x_in[c, 0] + x_in[c, 1] + x_in[c, 2]
        for u in range(2):
            z_copy(c, u).start()

    def start_near_x():
        add_core(2)
        for u in range(2):
            for d in (2, 1, 3):
                near_x_copy(u, d).start()

    def start_near_z():
        for u in range(2):
            for d in (1, 3, 2):
                near_x_copy(u, d).wait_recv()
            x_sum[2, u] = core_sum[2, u, x] + x_in[2, 0, u] + x_in[2, 1, u] + x_in[2, 2, u]
            z_copy(2, u).start()

    def all_chunks(*accs):
        def step(c, carry):
            sum_chunk(accs, c, stat_scr, bins_scr, turn_scr)

            @pl.when(c == 0)
            def _():
                pl.semaphore_wait(barrier, len(greeted))

            @pl.when((c > 0) & (c < 3))
            def _():
                start_x(c - 1)

            @pl.when(c == 3)
            def _():
                start_near_x()

            turn_chunk(c, turn_scr, hist)

            @pl.when(c < 3)
            def _():
                core_copy(c).start()

            @pl.when(c == 3)
            def _():
                for u in range(2):
                    last_core_copy(u).start()

            return carry

        lax.fori_loop(0, 4, step, 0)

    pl.run_scoped(all_chunks, *[pltpu.ACC(q % 2)((16, TILE), F32) for q in range(PAIRS)])

    start_z(0)
    for u in range(2):
        last_core_copy(u).wait_recv()
        core_sum[3, u] = hist[3, core, u] + core_in[3, u]
        for d in (2, 1, 3, 0):
            if u == 0:
                last_z_copy(d).start()
            elif d:
                last_x_copy(d).start()
    start_z(1)
    start_near_z()
    block = core_sum[3, 1, x]
    for c in range(2):
        for u in range(2):
            z_copy(c, u).wait_recv()
            block = block + z_in[2 - c if u else 3 + c]
    for d in range(NX):
        last_z_copy(d).wait_recv()
        block = block + last_z[d]
        if d:
            last_x_copy(d).wait_recv()
            block = block + last_x[d - 1]
    for u in range(2):
        z_copy(2, u).wait_recv()
        block = block + z_in[0 if u else 5]

    gain = finish(block)
    top = jnp.max(gain, axis=0, keepdims=True)

    def wait_sends():
        for u in range(2):
            last_core_copy(u).wait_send()
        for c in range(3):
            core_copy(c).wait_send()
            for d in range(1, NX):
                if c < 2:
                    x_copy(c, d).wait_send()
                else:
                    for u in range(2):
                        near_x_copy(u, d).wait_send()
            for u in range(2):
                z_copy(c, u).wait_send()
        for d in range(NX):
            last_z_copy(d).wait_send()
            if d:
                last_x_copy(d).wait_send()

    rounds = (
        [other],
        [x_peer[d] for d in (2, 1, 3)],
        [at(0, d, core) for d in far],
        [y_peer[d] for d in far],
    )
    top_copies = []
    for stage, peers in enumerate(rounds):
        top_out[stage] = top
        sent = []
        for k, peer in enumerate(peers):
            s = copy(top_out.at[stage], top_in.at[stage, k], top_send.at[stage, k], top_recv.at[stage, k], peer)
            s.start()
            sent.append(s)
        if stage == 0:
            store_gain(gain, gain_ref)
        if stage == 2:
            wait_sends()
        if stage:
            for s in top_copies:
                s.wait_send()
            top_copies = []
        for s in reversed(sent):
            s.wait_recv()
        for k in range(len(sent)):
            top = jnp.maximum(top, top_in[stage, k])
        top_copies += sent
    best_ref[...] = top
    for s in top_copies:
        s.wait_send()


def write_kernel(gain_ref, top_ref, gain_hbm, best_ref, sem):
    write = pltpu.make_async_copy(gain_ref, gain_hbm, sem)
    write.start()
    for leaf in range(4):
        best_ref[leaf] = jnp.max(top_ref[:, 32 * leaf : 32 * (leaf + 1)])
    write.wait()


def body(bin_values, leaf_ids, treated, gradient, hessian):
    shape = (ROWS // 128, 128)
    dma = pltpu.SemaphoreType.DMA
    block = (8, 512)
    bin_values, leaf_ids, treated, gradient, hessian = (
        pltpu.with_memory_space_constraint(v, pltpu.HBM)
        for v in (bin_values, leaf_ids.reshape(shape), treated.reshape(shape), gradient.reshape(shape), hessian.reshape(shape))
    )
    gain, top = pl.pallas_call(
        kernel,
        out_shape=(jax.ShapeDtypeStruct((8, 128), F32), jax.ShapeDtypeStruct((1, 128), F32)),
        in_specs=[pl.BlockSpec(memory_space=pltpu.HBM)] * 5,
        out_specs=(pl.BlockSpec(memory_space=pltpu.VMEM),) * 2,
        scratch_shapes=[
            pltpu.VMEM((ROWS, FEATS), jnp.int32),
            pltpu.VMEM(shape, jnp.int32),
            pltpu.VMEM(shape, jnp.int32),
            pltpu.VMEM(shape, BF),
            pltpu.VMEM(shape, BF),
            pltpu.VMEM((16, ROWS), BF),
            pltpu.VMEM((4, ROWS, 128), jnp.int8),
            pltpu.VMEM((512, 128), F32),
            pltpu.VMEM((4, 2, 2, NX) + block, F32),
            pltpu.VMEM((4, 2, NX) + block, F32),
            pltpu.VMEM((4, 2, NX) + block, F32),
            pltpu.VMEM((3, NX - 1, 2) + block, F32),
            pltpu.VMEM((3, 2) + block, F32),
            pltpu.VMEM((6,) + block, F32),
            pltpu.VMEM((NX - 1,) + block, F32),
            pltpu.VMEM((NX,) + block, F32),
            pltpu.VMEM((4, 1, 128), F32),
            pltpu.VMEM((4, 7, 1, 128), F32),
            dma((8,)), dma((5,)), dma((5,)), dma((4, 3)), dma((4, 3)), dma((6,)), dma((6,)),
            dma((3,)), dma((3,)), dma((4,)), dma((4,)), dma((4, 7)), dma((4, 7)),
        ],
        compiler_params=pltpu.CompilerParams(collective_id=0, has_side_effects=True, vmem_limit_bytes=24 << 20),
    )(bin_values, leaf_ids, treated, gradient, hessian)
    vmem = pl.BlockSpec(memory_space=pltpu.VMEM)
    gain, best = pl.pallas_call(
        write_kernel,
        out_shape=(jax.ShapeDtypeStruct((8, 128), F32), jax.ShapeDtypeStruct((4,), F32)),
        in_specs=[vmem, vmem],
        out_specs=(pl.BlockSpec(memory_space=pltpu.HBM), pl.BlockSpec(memory_space=pltpu.SMEM)),
        scratch_shapes=[dma(())],
        compiler_params=pltpu.CompilerParams(vmem_limit_bytes=1 << 20),
    )(gain, top)
    return gain.reshape(4, 2, 128), best


def solution(mesh):
    in_specs = (P("row", "feat"), P("row"), P("row"), P("row"), P("row"))
    out_specs = (P(None, ("feat", "row"), None), P())
    return jax.shard_map(body, mesh=mesh, in_specs=in_specs, out_specs=out_specs, check_vma=False)
```

```python
import jax
import jax.numpy as jnp
from jax import lax
from jax.experimental import pallas as pl
from jax.experimental.pallas import tpu as pltpu
from jax.sharding import PartitionSpec as P

MESH = pl.DeviceIdType.MESH
BF = jnp.bfloat16
F32 = jnp.float32
F8 = jnp.float8_e4m3fn
ROWS = 2048
FEATS = 128
TILE = 256
TILES = ROWS // TILE
PAIRS = 16
NX, NZ, NY = 4, 8, 8


def load_stats(leaf_ref, arm_ref, grad_ref, hess_ref, stat_scr):
    stat = lax.broadcasted_iota(jnp.int32, (16, 128), 0)
    kind, leaf_of = stat // 4, stat % 4
    for c in range(ROWS // 128):
        grad = grad_ref[c : c + 1, :].astype(F32)
        hess = hess_ref[c : c + 1, :].astype(F32)
        keep = (leaf_ref[c : c + 1, :] == leaf_of) & ((arm_ref[c : c + 1, :] == 1) == (kind < 2))
        value = jnp.where(kind % 2 == 0, grad, hess)
        stat_scr[:, c * 128 : (c + 1) * 128] = jnp.where(keep, value, 0.0).astype(BF)


def lane_orders(z):
    feat = lax.broadcasted_iota(jnp.int32, (TILE, 128), 0)
    lane = lax.broadcasted_iota(jnp.int32, (TILE, 128), 1)
    owner = lane // 8
    core, u, x = owner // 8, owner // 4 % 2, owner % 4
    orders = []
    for c in range(4):
        far = lax.rem(z + jnp.where(u == 0, 4 + c, 3 - c), NZ)
        orders.append((feat == ((x * NZ + far) * 2 + core) * 2 + lane % 2).astype(F32).astype(BF))
    return [jnp.concatenate(orders[:2], axis=1), jnp.concatenate(orders[2:], axis=1)]


def spread_bins(accs, orders, loads, bins_ref, bins_scr):
    def drain(r):
        rows = slice(r * TILE, (r + 1) * TILE)
        for p in range(2):
            spread = pltpu.matmul_pop(accs[2 * (r % 2) + p]).astype(jnp.int32).astype(jnp.int8)
            bins_scr[2 * p, rows, :] = spread[:, :128]
            bins_scr[2 * p + 1, rows, :] = spread[:, 128:]

    for p in range(2):
        pltpu.matmul_push_rhs(orders[p], staging_register=0, mxu_index=p)
    for r in range(TILES):
        if r % 2 == 0:
            loads[r // 2].wait()
        block = bins_ref[r * TILE : (r + 1) * TILE, :].astype(F32).astype(BF)
        block = jnp.concatenate([block, block], axis=1)
        for p in range(2):
            pltpu.matmul_acc_lhs(accs[2 * (r % 2) + p], block, load_staged_rhs=0 if r == 0 else None)
        if r:
            drain(r - 1)
    drain(TILES - 1)


def sum_chunk(accs, c, stat_scr, bins_scr, turn_scr):
    shape = (TILE // 32, 32, 128)
    one, zero = jnp.ones(shape, F8), jnp.zeros(shape, F8)
    group = lax.broadcasted_iota(jnp.int32, (32, 128), 1) % 8 // 2
    last = [(group * 32 + q).astype(jnp.int8)[None] for q in range(2 * PAIRS)]
    for k in range(TILES):
        rows = slice(k * TILE, (k + 1) * TILE)
        bins = bins_scr[c, rows, :].reshape(shape)
        stat = stat_scr[:, rows]
        for q in range(PAIRS):
            hot = [jnp.where(bins <= last[2 * q + e], one, zero).reshape(TILE, 128) for e in range(2)]
            reg = (k * (PAIRS // 2) + q // 2) % 2
            pltpu.matmul_push_rhs(jnp.concatenate(hot, axis=1), staging_register=reg, mxu_index=q % 2)
            pltpu.matmul_acc_lhs(accs[q], stat, load_staged_rhs=reg)
    for q in range(PAIRS):
        sums = pltpu.matmul_pop(accs[q])
        for e in range(2):
            turn_scr[pl.ds(2 * q + e, 16, stride=32), :] = sums[:, e * 128 : (e + 1) * 128]


def turn_chunk(c, turn_scr, hist):
    for t in range(4):
        turned = turn_scr[t * 128 : (t + 1) * 128, :].T
        hist[c, :, :, :, :, t * 128 : (t + 1) * 128] = turned.reshape(2, 2, NX, 8, 128)


def score(totals):
    grad_t, hess_t, grad_c, hess_c = (totals[8 * k : 8 * k + 8] for k in range(4))
    value_t = grad_t / (hess_t + 1.0)
    value_c = grad_c / (hess_c + 1.0)
    spread = value_t - value_c
    return grad_t * value_t + grad_c * value_c + (hess_t + hess_c) * spread * spread


def finish(block):
    left = jnp.concatenate([block[:, 128 * k : 128 * (k + 1)] for k in range(4)], axis=0)
    leaf = lax.broadcasted_iota(jnp.int32, (32, 128), 1) // 32
    sub = lax.broadcasted_iota(jnp.int32, (32, 128), 0) % 8
    last = jnp.where(sub >= 6, left, 0.0)
    last = last + jnp.where((sub >= 4) & (sub < 6), pltpu.roll(last, 30, 0), 0.0)
    last = last + jnp.where(sub < 4, pltpu.roll(last, 28, 0), 0.0)
    parent = jnp.broadcast_to(last[:, 127:128], (32, 128))
    for k in range(3):
        parent = jnp.where(leaf == k, jnp.broadcast_to(last[:, 32 * k + 31 : 32 * k + 32], (32, 128)), parent)
    gain = score(left) + score(parent - left) - score(parent)
    return gain


def store_gain(gain, gain_ref):
    lane_block = lax.broadcasted_iota(jnp.int32, (8, 128), 1) // 32
    row_block = lax.broadcasted_iota(jnp.int32, (8, 128), 0) // 2
    out = gain
    for d in range(1, 4):
        moved = pltpu.roll(pltpu.roll(gain, 32 * d, 1), 8 - 2 * d, 0)
        out = jnp.where((lane_block + 4 - row_block) % 4 == d, moved, out)
    gain_ref[...] = out


def kernel(
    bins_hbm, leaf_hbm, arm_hbm, grad_hbm, hess_hbm, gain_ref, best_ref,
    bins_ref, leaf_ref, arm_ref, grad_ref, hess_ref, stat_scr, bins_scr, turn_scr,
    hist, core_in, core_sum, x_in, x_sum, z_in, last_x, last_z, top_out, top_in,
    load_sem, core_send, core_recv, x_send, x_recv, z_send, z_recv,
    last_x_send, last_x_recv, last_z_send, last_z_recv, top_send, top_recv,
):
    feat = lax.axis_index("feat")
    row = lax.axis_index("row")
    core = lax.rem(row, 2)
    z = lax.rem(row // 2, NZ)
    x = row // (2 * NZ)

    def at(dx, dz, core_):
        return (feat, (lax.rem(x + dx, NX) * NZ + lax.rem(z + dz, NZ)) * 2 + core_)

    other = at(0, 0, 1 - core)
    x_peer = [at(d, 0, core) for d in range(NX)]
    y_peer = [(lax.rem(feat + d, NY), row) for d in range(NY)]

    pairs = [(leaf_hbm, leaf_ref), (arm_hbm, arm_ref), (grad_hbm, grad_ref), (hess_hbm, hess_ref)]
    pairs += [(bins_hbm.at[pl.ds(k * 512, 512)], bins_ref.at[pl.ds(k * 512, 512)]) for k in range(4)]
    loads = [pltpu.make_async_copy(src, dst, load_sem.at[k]) for k, (src, dst) in enumerate(pairs)]
    for load in loads:
        load.start()
    barrier = pltpu.get_barrier_semaphore()
    far = (4, 3, 5, 2, 6, 1, 7)
    greeted = [at(0, d, core) for d in far] + [y_peer[d] for d in far]
    greeted += [at(d, e, core) for d in (2, 1, 3) for e in (1, NZ - 1, 0)] + [other]
    for peer in greeted:
        pl.semaphore_signal(barrier, inc=1, device_id=peer, device_id_type=MESH)

    for load in loads[:4]:
        load.wait()
    load_stats(leaf_ref, arm_ref, grad_ref, hess_ref, stat_scr)
    orders = lane_orders(z)
    pl.run_scoped(
        lambda *accs: spread_bins(accs, orders, loads[4:], bins_ref, bins_scr),
        *[pltpu.ACC(q % 2)((TILE, TILE), F32) for q in range(4)],
    )

    def copy(src, dst, send, recv, peer):
        return pltpu.make_async_remote_copy(
            src_ref=src, dst_ref=dst, send_sem=send, recv_sem=recv, device_id=peer, device_id_type=MESH
        )

    def core_copy(c):
        return copy(hist.at[c, 1 - core], core_in.at[c], core_send.at[c], core_recv.at[c], other)

    def last_core_copy(u):
        k = 3 + u
        return copy(hist.at[3, 1 - core, u], core_in.at[3, u], core_send.at[k], core_recv.at[k], other)

    def x_copy(c, d):
        return copy(
            core_sum.at[c, :, lax.rem(x + d, NX)], x_in.at[c, d - 1], x_send.at[c, d - 1], x_recv.at[c, d - 1], x_peer[d]
        )

    def z_copy(c, u):
        d = 3 - c if u else 4 + c
        return copy(x_sum.at[c, u], z_in.at[d - 1], z_send.at[d - 1], z_recv.at[d - 1], at(0, d, core))

    def last_x_copy(d):
        return copy(
            core_sum.at[3, 1, lax.rem(x + d, NX)], last_x.at[d - 1], last_x_send.at[d - 1], last_x_recv.at[d - 1], x_peer[d]
        )

    def last_z_copy(d):
        return copy(
            core_sum.at[3, 0, lax.rem(x + d, NX)], last_z.at[d], last_z_send.at[d], last_z_recv.at[d], at(d, NZ - 1, core)
        )

    def add_core(c):
        core_copy(c).wait_recv()
        core_sum[c] = hist[c, core] + core_in[c]

    def start_x(c):
        add_core(c)
        for d in (2, 1, 3):
            x_copy(c, d).start()

    def start_z(c):
        for d in (1, 3, 2):
            x_copy(c, d).wait_recv()
        x_sum[c] = core_sum[c, :, x] + x_in[c, 0] + x_in[c, 1] + x_in[c, 2]
        for u in range(2):
            z_copy(c, u).start()

    def all_chunks(*accs):
        def step(c, carry):
            sum_chunk(accs, c, stat_scr, bins_scr, turn_scr)

            @pl.when(c == 0)
            def _():
                pl.semaphore_wait(barrier, len(greeted))

            turn_chunk(c, turn_scr, hist)

            @pl.when(c < 3)
            def _():
                core_copy(c).start()

            @pl.when(c == 3)
            def _():
                for u in range(2):
                    last_core_copy(u).start()

            @pl.when(c > 0)
            def _():
                start_x(c - 1)

            return carry

        lax.fori_loop(0, 4, step, 0)

    pl.run_scoped(all_chunks, *[pltpu.ACC(q % 2)((16, TILE), F32) for q in range(PAIRS)])

    start_z(0)
    for u in range(2):
        last_core_copy(u).wait_recv()
        core_sum[3, u] = hist[3, core, u] + core_in[3, u]
        for d in (2, 1, 3, 0):
            if u == 0:
                last_z_copy(d).start()
            elif d:
                last_x_copy(d).start()
    for c in range(1, 3):
        start_z(c)
    block = core_sum[3, 1, x]
    for c in range(2):
        for u in range(2):
            z_copy(c, u).wait_recv()
            block = block + z_in[2 - c if u else 3 + c]
    for d in range(NX):
        last_z_copy(d).wait_recv()
        block = block + last_z[d]
        if d:
            last_x_copy(d).wait_recv()
            block = block + last_x[d - 1]
    for u in range(2):
        z_copy(2, u).wait_recv()
        block = block + z_in[0 if u else 5]

    gain = finish(block)
    top = jnp.max(gain, axis=0, keepdims=True)

    def wait_sends():
        for u in range(2):
            last_core_copy(u).wait_send()
        for c in range(3):
            core_copy(c).wait_send()
            for d in range(1, NX):
                x_copy(c, d).wait_send()
            for u in range(2):
                z_copy(c, u).wait_send()
        for d in range(NX):
            last_z_copy(d).wait_send()
            if d:
                last_x_copy(d).wait_send()

    rounds = (
        [other],
        [x_peer[d] for d in (2, 1, 3)],
        [at(0, d, core) for d in far],
        [y_peer[d] for d in far],
    )
    top_copies = []
    for stage, peers in enumerate(rounds):
        top_out[stage] = top
        sent = []
        for k, peer in enumerate(peers):
            s = copy(top_out.at[stage], top_in.at[stage, k], top_send.at[stage, k], top_recv.at[stage, k], peer)
            s.start()
            sent.append(s)
        if stage == 0:
            store_gain(gain, gain_ref)
        if stage == 2:
            wait_sends()
        if stage:
            for s in top_copies:
                s.wait_send()
            top_copies = []
        for s in reversed(sent):
            s.wait_recv()
        for k in range(len(sent)):
            top = jnp.maximum(top, top_in[stage, k])
        top_copies += sent
    best_ref[...] = top
    for s in top_copies:
        s.wait_send()


def write_kernel(gain_ref, top_ref, gain_hbm, best_ref, sem):
    write = pltpu.make_async_copy(gain_ref, gain_hbm, sem)
    write.start()
    for leaf in range(4):
        best_ref[leaf] = jnp.max(top_ref[:, 32 * leaf : 32 * (leaf + 1)])
    write.wait()


def body(bin_values, leaf_ids, treated, gradient, hessian):
    shape = (ROWS // 128, 128)
    dma = pltpu.SemaphoreType.DMA
    block = (8, 512)
    bin_values, leaf_ids, treated, gradient, hessian = (
        pltpu.with_memory_space_constraint(v, pltpu.HBM)
        for v in (bin_values, leaf_ids.reshape(shape), treated.reshape(shape), gradient.reshape(shape), hessian.reshape(shape))
    )
    gain, top = pl.pallas_call(
        kernel,
        out_shape=(jax.ShapeDtypeStruct((8, 128), F32), jax.ShapeDtypeStruct((1, 128), F32)),
        in_specs=[pl.BlockSpec(memory_space=pltpu.HBM)] * 5,
        out_specs=(pl.BlockSpec(memory_space=pltpu.VMEM),) * 2,
        scratch_shapes=[
            pltpu.VMEM((ROWS, FEATS), jnp.int32),
            pltpu.VMEM(shape, jnp.int32),
            pltpu.VMEM(shape, jnp.int32),
            pltpu.VMEM(shape, BF),
            pltpu.VMEM(shape, BF),
            pltpu.VMEM((16, ROWS), BF),
            pltpu.VMEM((4, ROWS, 128), jnp.int8),
            pltpu.VMEM((512, 128), F32),
            pltpu.VMEM((4, 2, 2, NX) + block, F32),
            pltpu.VMEM((4, 2, NX) + block, F32),
            pltpu.VMEM((4, 2, NX) + block, F32),
            pltpu.VMEM((3, NX - 1, 2) + block, F32),
            pltpu.VMEM((3, 2) + block, F32),
            pltpu.VMEM((6,) + block, F32),
            pltpu.VMEM((NX - 1,) + block, F32),
            pltpu.VMEM((NX,) + block, F32),
            pltpu.VMEM((4, 1, 128), F32),
            pltpu.VMEM((4, 7, 1, 128), F32),
            dma((8,)), dma((5,)), dma((5,)), dma((3, 3)), dma((3, 3)), dma((6,)), dma((6,)),
            dma((3,)), dma((3,)), dma((4,)), dma((4,)), dma((4, 7)), dma((4, 7)),
        ],
        compiler_params=pltpu.CompilerParams(collective_id=0, has_side_effects=True, vmem_limit_bytes=24 << 20),
    )(bin_values, leaf_ids, treated, gradient, hessian)
    vmem = pl.BlockSpec(memory_space=pltpu.VMEM)
    gain, best = pl.pallas_call(
        write_kernel,
        out_shape=(jax.ShapeDtypeStruct((8, 128), F32), jax.ShapeDtypeStruct((4,), F32)),
        in_specs=[vmem, vmem],
        out_specs=(pl.BlockSpec(memory_space=pltpu.HBM), pl.BlockSpec(memory_space=pltpu.SMEM)),
        scratch_shapes=[dma(())],
        compiler_params=pltpu.CompilerParams(vmem_limit_bytes=1 << 20),
    )(gain, top)
    return gain.reshape(4, 2, 128), best


def solution(mesh):
    in_specs = (P("row", "feat"), P("row"), P("row"), P("row"), P("row"))
    out_specs = (P(None, ("feat", "row"), None), P())
    return jax.shard_map(body, mesh=mesh, in_specs=in_specs, out_specs=out_specs, check_vma=False)
```

```python
import jax
import jax.numpy as jnp
from jax import lax
from jax.experimental import pallas as pl
from jax.experimental.pallas import tpu as pltpu
from jax.sharding import PartitionSpec as P

MESH = pl.DeviceIdType.MESH
BF = jnp.bfloat16
F32 = jnp.float32
F8 = jnp.float8_e4m3fn
ROWS = 2048
FEATS = 128
TILE = 256
TILES = ROWS // TILE
PAIRS = 16
NX, NZ, NY = 4, 8, 8


def load_stats(leaf_ref, arm_ref, grad_ref, hess_ref, stat_scr):
    stat = lax.broadcasted_iota(jnp.int32, (16, 128), 0)
    kind, leaf_of = stat // 4, stat % 4
    for c in range(ROWS // 128):
        grad = grad_ref[c : c + 1, :].astype(F32)
        hess = hess_ref[c : c + 1, :].astype(F32)
        keep = (leaf_ref[c : c + 1, :] == leaf_of) & ((arm_ref[c : c + 1, :] == 1) == (kind < 2))
        value = jnp.where(kind % 2 == 0, grad, hess)
        stat_scr[:, c * 128 : (c + 1) * 128] = jnp.where(keep, value, 0.0).astype(BF)


def lane_orders(z):
    feat = lax.broadcasted_iota(jnp.int32, (TILE, 128), 0)
    lane = lax.broadcasted_iota(jnp.int32, (TILE, 128), 1)
    owner = lane // 8
    core, u, x = owner // 8, owner // 4 % 2, owner % 4
    orders = []
    for c in range(4):
        far = lax.rem(z + jnp.where(u == 0, 4 + c, 3 - c), NZ)
        orders.append((feat == ((x * NZ + far) * 2 + core) * 2 + lane % 2).astype(F32).astype(BF))
    return [jnp.concatenate(orders[:2], axis=1), jnp.concatenate(orders[2:], axis=1)]


def spread_bins(accs, orders, loads, bins_ref, bins_scr):
    def drain(r):
        rows = slice(r * TILE, (r + 1) * TILE)
        for p in range(2):
            spread = pltpu.matmul_pop(accs[2 * (r % 2) + p]).astype(jnp.int32).astype(jnp.int8)
            bins_scr[2 * p, rows, :] = spread[:, :128]
            bins_scr[2 * p + 1, rows, :] = spread[:, 128:]

    for p in range(2):
        pltpu.matmul_push_rhs(orders[p], staging_register=0, mxu_index=p)
    for r in range(TILES):
        if r % 2 == 0:
            loads[r // 2].wait()
        block = bins_ref[r * TILE : (r + 1) * TILE, :].astype(F32).astype(BF)
        block = jnp.concatenate([block, block], axis=1)
        for p in range(2):
            pltpu.matmul_acc_lhs(accs[2 * (r % 2) + p], block, load_staged_rhs=0 if r == 0 else None)
        if r:
            drain(r - 1)
    drain(TILES - 1)


def sum_chunk(accs, c, stat_scr, bins_scr, turn_scr):
    shape = (TILE // 32, 32, 128)
    one, zero = jnp.ones(shape, F8), jnp.zeros(shape, F8)
    group = lax.broadcasted_iota(jnp.int32, (32, 128), 1) % 8 // 2
    last = [(group * 32 + q).astype(jnp.int8)[None] for q in range(2 * PAIRS)]
    for k in range(TILES):
        rows = slice(k * TILE, (k + 1) * TILE)
        bins = bins_scr[c, rows, :].reshape(shape)
        stat = stat_scr[:, rows]
        for q in range(PAIRS):
            hot = [jnp.where(bins <= last[2 * q + e], one, zero).reshape(TILE, 128) for e in range(2)]
            reg = (k * (PAIRS // 2) + q // 2) % 2
            pltpu.matmul_push_rhs(jnp.concatenate(hot, axis=1), staging_register=reg, mxu_index=q % 2)
            pltpu.matmul_acc_lhs(accs[q], stat, load_staged_rhs=reg)
    for q in range(PAIRS):
        sums = pltpu.matmul_pop(accs[q])
        for e in range(2):
            turn_scr[pl.ds(2 * q + e, 16, stride=32), :] = sums[:, e * 128 : (e + 1) * 128]


def turn_chunk(c, turn_scr, hist):
    for t in range(4):
        turned = turn_scr[t * 128 : (t + 1) * 128, :].T
        hist[c, :, :, :, :, t * 128 : (t + 1) * 128] = turned.reshape(2, 2, NX, 8, 128)


def score(totals):
    grad_t, hess_t, grad_c, hess_c = (totals[8 * k : 8 * k + 8] for k in range(4))
    value_t = grad_t / (hess_t + 1.0)
    value_c = grad_c / (hess_c + 1.0)
    spread = value_t - value_c
    return grad_t * value_t + grad_c * value_c + (hess_t + hess_c) * spread * spread


def finish(block):
    left = jnp.concatenate([block[:, 128 * k : 128 * (k + 1)] for k in range(4)], axis=0)
    leaf = lax.broadcasted_iota(jnp.int32, (32, 128), 1) // 32
    sub = lax.broadcasted_iota(jnp.int32, (32, 128), 0) % 8
    last = jnp.where(sub >= 6, left, 0.0)
    last = last + jnp.where((sub >= 4) & (sub < 6), pltpu.roll(last, 30, 0), 0.0)
    last = last + jnp.where(sub < 4, pltpu.roll(last, 28, 0), 0.0)
    parent = jnp.broadcast_to(last[:, 127:128], (32, 128))
    for k in range(3):
        parent = jnp.where(leaf == k, jnp.broadcast_to(last[:, 32 * k + 31 : 32 * k + 32], (32, 128)), parent)
    gain = score(left) + score(parent - left) - score(parent)
    return gain


def store_gain(gain, gain_ref):
    lane_block = lax.broadcasted_iota(jnp.int32, (8, 128), 1) // 32
    row_block = lax.broadcasted_iota(jnp.int32, (8, 128), 0) // 2
    out = gain
    for d in range(1, 4):
        moved = pltpu.roll(pltpu.roll(gain, 32 * d, 1), 8 - 2 * d, 0)
        out = jnp.where((lane_block + 4 - row_block) % 4 == d, moved, out)
    gain_ref[...] = out


def kernel(
    bins_hbm, leaf_hbm, arm_hbm, grad_hbm, hess_hbm, gain_ref, best_ref,
    bins_ref, leaf_ref, arm_ref, grad_ref, hess_ref, stat_scr, bins_scr, turn_scr,
    hist, core_in, core_sum, x_in, x_sum, z_in, last_x, last_z, top_out, top_in,
    load_sem, core_send, core_recv, x_send, x_recv, z_send, z_recv,
    last_x_send, last_x_recv, last_z_send, last_z_recv, top_send, top_recv,
):
    feat = lax.axis_index("feat")
    row = lax.axis_index("row")
    core = lax.rem(row, 2)
    z = lax.rem(row // 2, NZ)
    x = row // (2 * NZ)

    def at(dx, dz, core_):
        return (feat, (lax.rem(x + dx, NX) * NZ + lax.rem(z + dz, NZ)) * 2 + core_)

    other = at(0, 0, 1 - core)
    x_peer = [at(d, 0, core) for d in range(NX)]
    y_peer = [(lax.rem(feat + d, NY), row) for d in range(NY)]

    pairs = [(leaf_hbm, leaf_ref), (arm_hbm, arm_ref), (grad_hbm, grad_ref), (hess_hbm, hess_ref)]
    pairs += [(bins_hbm.at[pl.ds(k * 512, 512)], bins_ref.at[pl.ds(k * 512, 512)]) for k in range(4)]
    loads = [pltpu.make_async_copy(src, dst, load_sem.at[k]) for k, (src, dst) in enumerate(pairs)]
    for load in loads:
        load.start()
    barrier = pltpu.get_barrier_semaphore()
    far = (4, 3, 5, 2, 6, 1, 7)
    greeted = [at(0, d, core) for d in far] + [y_peer[d] for d in far]
    greeted += [at(d, e, core) for d in (2, 1, 3) for e in (1, NZ - 1, 0)] + [other]
    for peer in greeted:
        pl.semaphore_signal(barrier, inc=1, device_id=peer, device_id_type=MESH)

    for load in loads[:4]:
        load.wait()
    load_stats(leaf_ref, arm_ref, grad_ref, hess_ref, stat_scr)
    orders = lane_orders(z)
    pl.run_scoped(
        lambda *accs: spread_bins(accs, orders, loads[4:], bins_ref, bins_scr),
        *[pltpu.ACC(q % 2)((TILE, TILE), F32) for q in range(4)],
    )

    def copy(src, dst, send, recv, peer):
        return pltpu.make_async_remote_copy(
            src_ref=src, dst_ref=dst, send_sem=send, recv_sem=recv, device_id=peer, device_id_type=MESH
        )

    def core_copy(c):
        return copy(hist.at[c, 1 - core], core_in.at[c], core_send.at[c], core_recv.at[c], other)

    def last_core_copy(u):
        k = 3 + u
        return copy(hist.at[3, 1 - core, u], core_in.at[3, u], core_send.at[k], core_recv.at[k], other)

    def x_copy(c, d):
        return copy(
            core_sum.at[c, :, lax.rem(x + d, NX)], x_in.at[c, d - 1], x_send.at[c, d - 1], x_recv.at[c, d - 1], x_peer[d]
        )

    def z_copy(c, u):
        d = 3 - c if u else 4 + c
        return copy(x_sum.at[c, u], z_in.at[d - 1], z_send.at[d - 1], z_recv.at[d - 1], at(0, d, core))

    def last_x_copy(d):
        return copy(
            core_sum.at[3, 1, lax.rem(x + d, NX)], last_x.at[d - 1], last_x_send.at[d - 1], last_x_recv.at[d - 1], x_peer[d]
        )

    def last_z_copy(d):
        return copy(
            core_sum.at[3, 0, lax.rem(x + d, NX)], last_z.at[d], last_z_send.at[d], last_z_recv.at[d], at(d, NZ - 1, core)
        )

    def add_core(c):
        core_copy(c).wait_recv()
        core_sum[c] = hist[c, core] + core_in[c]

    def start_x(c):
        add_core(c)
        for d in (2, 1, 3):
            x_copy(c, d).start()

    def start_z(c):
        for d in (1, 3, 2):
            x_copy(c, d).wait_recv()
        x_sum[c] = core_sum[c, :, x] + x_in[c, 0] + x_in[c, 1] + x_in[c, 2]
        for u in range(2):
            z_copy(c, u).start()

    def all_chunks(*accs):
        def step(c, carry):
            sum_chunk(accs, c, stat_scr, bins_scr, turn_scr)

            @pl.when(c == 1)
            def _():
                pl.semaphore_wait(barrier, len(greeted))
                core_copy(0).start()

            @pl.when(c == 2)
            def _():
                start_x(0)

            @pl.when(c > 1)
            def _():
                start_x(c - 1)

            turn_chunk(c, turn_scr, hist)

            @pl.when((c == 1) | (c == 2))
            def _():
                core_copy(c).start()

            @pl.when(c == 3)
            def _():
                for u in range(2):
                    last_core_copy(u).start()

            return carry

        lax.fori_loop(0, 4, step, 0)

    pl.run_scoped(all_chunks, *[pltpu.ACC(q % 2)((16, TILE), F32) for q in range(PAIRS)])

    start_z(0)
    for u in range(2):
        last_core_copy(u).wait_recv()
        core_sum[3, u] = hist[3, core, u] + core_in[3, u]
        for d in (2, 1, 3, 0):
            if u == 0:
                last_z_copy(d).start()
            elif d:
                last_x_copy(d).start()
    for c in range(1, 3):
        start_z(c)
    block = core_sum[3, 1, x]
    for c in range(2):
        for u in range(2):
            z_copy(c, u).wait_recv()
            block = block + z_in[2 - c if u else 3 + c]
    for d in range(NX):
        last_z_copy(d).wait_recv()
        block = block + last_z[d]
        if d:
            last_x_copy(d).wait_recv()
            block = block + last_x[d - 1]
    for u in range(2):
        z_copy(2, u).wait_recv()
        block = block + z_in[0 if u else 5]

    gain = finish(block)
    top = jnp.max(gain, axis=0, keepdims=True)

    def wait_sends():
        for u in range(2):
            last_core_copy(u).wait_send()
        for c in range(3):
            core_copy(c).wait_send()
            for d in range(1, NX):
                x_copy(c, d).wait_send()
            for u in range(2):
                z_copy(c, u).wait_send()
        for d in range(NX):
            last_z_copy(d).wait_send()
            if d:
                last_x_copy(d).wait_send()

    rounds = (
        [other],
        [x_peer[d] for d in (2, 1, 3)],
        [at(0, d, core) for d in far],
        [y_peer[d] for d in far],
    )
    top_copies = []
    for stage, peers in enumerate(rounds):
        top_out[stage] = top
        sent = []
        for k, peer in enumerate(peers):
            s = copy(top_out.at[stage], top_in.at[stage, k], top_send.at[stage, k], top_recv.at[stage, k], peer)
            s.start()
            sent.append(s)
        if stage == 0:
            store_gain(gain, gain_ref)
        if stage == 2:
            wait_sends()
        if stage:
            for s in top_copies:
                s.wait_send()
            top_copies = []
        for s in reversed(sent):
            s.wait_recv()
        for k in range(len(sent)):
            top = jnp.maximum(top, top_in[stage, k])
        top_copies += sent
    best_ref[...] = top
    for s in top_copies:
        s.wait_send()


def write_kernel(gain_ref, top_ref, gain_hbm, best_ref, sem):
    write = pltpu.make_async_copy(gain_ref, gain_hbm, sem)
    write.start()
    for leaf in range(4):
        best_ref[leaf] = jnp.max(top_ref[:, 32 * leaf : 32 * (leaf + 1)])
    write.wait()


def body(bin_values, leaf_ids, treated, gradient, hessian):
    shape = (ROWS // 128, 128)
    dma = pltpu.SemaphoreType.DMA
    block = (8, 512)
    bin_values, leaf_ids, treated, gradient, hessian = (
        pltpu.with_memory_space_constraint(v, pltpu.HBM)
        for v in (bin_values, leaf_ids.reshape(shape), treated.reshape(shape), gradient.reshape(shape), hessian.reshape(shape))
    )
    gain, top = pl.pallas_call(
        kernel,
        out_shape=(jax.ShapeDtypeStruct((8, 128), F32), jax.ShapeDtypeStruct((1, 128), F32)),
        in_specs=[pl.BlockSpec(memory_space=pltpu.HBM)] * 5,
        out_specs=(pl.BlockSpec(memory_space=pltpu.VMEM),) * 2,
        scratch_shapes=[
            pltpu.VMEM((ROWS, FEATS), jnp.int32),
            pltpu.VMEM(shape, jnp.int32),
            pltpu.VMEM(shape, jnp.int32),
            pltpu.VMEM(shape, BF),
            pltpu.VMEM(shape, BF),
            pltpu.VMEM((16, ROWS), BF),
            pltpu.VMEM((4, ROWS, 128), jnp.int8),
            pltpu.VMEM((512, 128), F32),
            pltpu.VMEM((4, 2, 2, NX) + block, F32),
            pltpu.VMEM((4, 2, NX) + block, F32),
            pltpu.VMEM((4, 2, NX) + block, F32),
            pltpu.VMEM((3, NX - 1, 2) + block, F32),
            pltpu.VMEM((3, 2) + block, F32),
            pltpu.VMEM((6,) + block, F32),
            pltpu.VMEM((NX - 1,) + block, F32),
            pltpu.VMEM((NX,) + block, F32),
            pltpu.VMEM((4, 1, 128), F32),
            pltpu.VMEM((4, 7, 1, 128), F32),
            dma((8,)), dma((5,)), dma((5,)), dma((3, 3)), dma((3, 3)), dma((6,)), dma((6,)),
            dma((3,)), dma((3,)), dma((4,)), dma((4,)), dma((4, 7)), dma((4, 7)),
        ],
        compiler_params=pltpu.CompilerParams(collective_id=0, has_side_effects=True, vmem_limit_bytes=24 << 20),
    )(bin_values, leaf_ids, treated, gradient, hessian)
    vmem = pl.BlockSpec(memory_space=pltpu.VMEM)
    gain, best = pl.pallas_call(
        write_kernel,
        out_shape=(jax.ShapeDtypeStruct((8, 128), F32), jax.ShapeDtypeStruct((4,), F32)),
        in_specs=[vmem, vmem],
        out_specs=(pl.BlockSpec(memory_space=pltpu.HBM), pl.BlockSpec(memory_space=pltpu.SMEM)),
        scratch_shapes=[dma(())],
        compiler_params=pltpu.CompilerParams(vmem_limit_bytes=1 << 20),
    )(gain, top)
    return gain.reshape(4, 2, 128), best


def solution(mesh):
    in_specs = (P("row", "feat"), P("row"), P("row"), P("row"), P("row"))
    out_specs = (P(None, ("feat", "row"), None), P())
    return jax.shard_map(body, mesh=mesh, in_specs=in_specs, out_specs=out_specs, check_vma=False)
```
